32 devices in a mesh: groups: 2 (over y), epoch: 4 (over z), strip: 2 (over x), band: 2 (over core).
Axes of the slice: x: 2, y: 2, z: 4, core: 2. Of those that a mesh axis runs over, the one named last changes fastest.
Arguments:
- template: bfloat16 [16, 48, 512], P(('groups', 'epoch'), 'strip', 'band'), parts along dimension 0, may hold values from -6 to 6
- science: float32 [32, 48, 512], P(('groups', 'epoch'), 'strip', 'band'), parts along dimension 0, may hold values from -6 to 6
- variance: float32 [32, 48, 512], P(('groups', 'epoch'), 'strip', 'band'), parts along dimension 0, may hold values from 2 to 40
- bad_mask: int32 [32, 48, 512], P(('groups', 'epoch'), 'strip', 'band'), parts along dimension 0, may hold values 0 or 1
- intersection: int32 [32], P('groups'), parts along dimension 0, may hold values from 0 to 7, as said below
- offsets: int32 [32, 2], P(('groups', 'epoch')), parts along dimension 0, may hold values from -4 to 4
- basis_index: int32 [32, 16], P(('groups', 'epoch')), parts along dimension 0, may hold values from 0 to 48
- coefficients: float32 [32, 16, 6], P(('groups', 'epoch')), parts along dimension 0, may hold values from -2 to 2
- basis: float32 [49, 19, 19], replicated, may hold values from -0.3125 to 0.3125
Outputs:
- residual_image: float32 [32, 48, 512], P(('groups', 'epoch'), 'strip', 'band'), parts along dimension 0
- coadd: float32 [16, 48, 512], P(('groups', 'epoch'), 'strip', 'band'), parts along dimension 0
The draws below stay inside these ranges and needn't reach their ends.
There are 2 independent parts, one for each index of `groups`. The reference program is written for one: setup_inputs(seed, part) draws one part's arguments, and reference() takes and returns one part's arrays. A program takes and returns all parts, laid end to end along the dimension named above; an argument that names none is the same for every part. Nothing has to cross between parts.
Inputs may be any that keep to these rules, and one draw needn't show every extreme that they name: `intersection`: exposure d * 4 + k (k < 4) covers a tile with index from (k) * 2 to (k) * 2 + 1, chosen at random among these.
All inputs are finite; a program needn't handle non-finite values. No bound on the sum of `bad_mask` on one device may be relied on, other than what follows from the above.
Results may differ from the reference program's by a relative error of at most 0.0018.
Values may be sent and summed in bfloat16 or wider, within the bound.
A program may use at most 64 MiB of HBM per device.

```python
import math
import jax
import jax.numpy as jnp
from jax import lax

KS = 19
HALF = 9
SHIFT = 4
NB = 49
NSEL = 16
NPOLY = 6
CAP = 1
TILE_DEV = 2
EXP_DEV = 4
EXPOSURES = 16
TILES = 8
HT = 48
WT = 512


def draw_intersection(key, part):
    position = jnp.arange(EXPOSURES, dtype=jnp.int32)
    owner = position % EXP_DEV // CAP
    choose = jax.random.randint(jax.random.fold_in(key, 17), (EXPOSURES,), 0, TILE_DEV)
    return (owner * TILE_DEV + choose).astype(jnp.int32)


def set_ends(drawn, rng, least, top_value):
    place = [jax.random.randint(jax.random.fold_in(rng, axis), (), 0, length) for axis, length in enumerate(drawn.shape)]
    widest = drawn.shape.index(max(drawn.shape))
    neighbour = place[:widest] + [(place[widest] + 1) % drawn.shape[widest]] + place[widest + 1:]
    return drawn.at[tuple(place)].set(least).at[tuple(neighbour)].set(top_value)


def block_scale(key, shape, shards, low, high):
    def one(dim, shards_of):
        heights = jax.random.uniform(jax.random.fold_in(jax.random.fold_in(key, 6), dim), (shards_of,), jnp.float32, low / len(shards), high / len(shards))
        return jnp.repeat(jnp.exp(heights), shape[dim] // shards_of).reshape((-1,) + (1,) * (len(shape) - dim - 1))

    loudness = one(*shards[0])
    for cut in shards[1:]:
        loudness = loudness * one(*cut)
    return loudness


def scatter_about(stream_key, shape, spread, reach, split=(), kind=jnp.bfloat16):
    drawn = jax.random.normal(stream_key, shape, jnp.float32) * spread
    if len(split) > 0:
        drawn = block_scale(stream_key, shape, split, -0.22, 0.18) * drawn
    return jnp.clip(drawn, min=-reach, max=reach).astype(kind)


def setup_inputs(seed: int = 0, part: int = 0) -> dict:
    streams_of = jax.random.split(jax.random.key(seed), 10)
    part_splits = jax.random.split(jax.random.fold_in(streams_of[9], part), 10)
    return {
        "template": scatter_about(part_splits[0], (TILES, HT, WT), 1.0, 6.0, ((0, 4), (1, 2), (2, 2))),
        "science": scatter_about(part_splits[1], (EXPOSURES, HT, WT), 1.0, 6.0, ((0, 4), (1, 2), (2, 2)), jnp.float32),
        "variance": jnp.clip(jnp.exp(math.log(40.0) - 2.9957323 * jax.random.uniform(part_splits[2], (EXPOSURES, HT, WT), jnp.float32) ** block_scale(part_splits[2], (EXPOSURES, HT, WT), ((0, 4), (1, 2), (2, 2)), -0.2, 0.2)), 2.0, 40.0),
        "bad_mask": set_ends((jax.random.randint(part_splits[3], (EXPOSURES, HT, WT), 0, 16) < 15).astype(jnp.int32), jax.random.fold_in(part_splits[3], 1), 0, 1),
        "intersection": draw_intersection(jax.random.fold_in(jax.random.fold_in(streams_of[9], part), 71), part),
        "offsets": set_ends(jax.random.randint(part_splits[5], (EXPOSURES, 2), 0 - SHIFT, SHIFT + 1), jax.random.fold_in(part_splits[5], 1), 0 - SHIFT, SHIFT).astype(jnp.int32),
        "basis_index": set_ends(jax.random.randint(part_splits[6], (EXPOSURES, NSEL), 0, NB), jax.random.fold_in(part_splits[6], 1), 0, NB - 1).astype(jnp.int32),
        "coefficients": scatter_about(part_splits[7], (EXPOSURES, NSEL, NPOLY), (0.5 / NSEL ** 0.5), 2.0, ((0, 4),), jnp.float32),
        "basis": scatter_about(streams_of[8], (NB, KS, KS), (KS * KS) ** -0.5, 0.3125, (), jnp.float32),
    }


highest = lax.Precision.HIGHEST


def poly_terms(rows_unit, cols_unit):
    ones = jnp.ones_like(rows_unit * cols_unit)
    return jnp.stack([ones, rows_unit * ones, cols_unit * ones, rows_unit * rows_unit * ones, rows_unit * cols_unit, cols_unit * cols_unit * ones])


def reference(template, science, variance, bad_mask, intersection, offsets, basis_index, coefficients, basis):
    height = template.shape[1]
    width = template.shape[2]
    rim = HALF + SHIFT
    padded = jnp.pad(template.astype(jnp.float32), ((0, 0), (rim, rim), (rim, rim)))
    picked = jnp.take(basis, basis_index, axis=0)
    kernels = jnp.einsum("ejp,ejab->epab", coefficients, picked, precision=highest).astype(jnp.bfloat16)
    kernels = lax.optimization_barrier(kernels).astype(jnp.float32)
    rows_unit = (2.0 * jnp.arange(height, dtype=jnp.float32) + 1.0) / height - 1.0
    cols_unit = (2.0 * jnp.arange(width, dtype=jnp.float32) + 1.0) / width - 1.0
    shapes = poly_terms(rows_unit[:, None], cols_unit[None, :])

    def one_model(item):
        tile, shift, kernel = item
        slab = lax.dynamic_index_in_dim(padded, tile.astype(jnp.int32), 0, keepdims=False)
        window = lax.dynamic_slice(slab, ((SHIFT + shift[0]).astype(jnp.int32), (SHIFT + shift[1]).astype(jnp.int32)), (height + 2 * HALF, width + 2 * HALF))
        conv = lax.conv_general_dilated(window[None, None], kernel[:, None], (1, 1), "VALID", precision=highest)[0]
        return jnp.sum(conv * shapes, axis=0)

    models = lax.map(one_model, (intersection, offsets, kernels))
    residual_image = science - models
    weight = bad_mask.astype(jnp.float32) / variance
    numer = jax.ops.segment_sum(weight * residual_image, intersection, num_segments=TILES)
    denom = jax.ops.segment_sum(weight, intersection, num_segments=TILES)
    return residual_image, numer / (denom + 1.0)
```

```python
import functools

import jax
import jax.numpy as jnp
from jax import lax
from jax.experimental import pallas as pl
from jax.experimental.pallas import tpu as pltpu
from jax.sharding import PartitionSpec as P

HALF = 9
SHIFT = 4
RIM = HALF + SHIFT
EDGE_ROWS = 16
LANES = 128
SLOT = 64
GROUPS = 4

MESH = pl.DeviceIdType.MESH
STEPS = [(ds, db) for ds in (-1, 1, 0) for db in (-1, 1, 0)]


def kernel(
    sizes,
    intersection_hbm,
    offsets_hbm,
    basis_index_hbm,
    coefficients_hbm,
    template_hbm,
    science_hbm,
    variance_hbm,
    bad_mask_hbm,
    basis_hbm,
    residual_out,
    coadd_out,
    intersection,
    offsets,
    basis_index,
    coefficients,
    template,
    science,
    variance,
    bad_mask,
    basis,
    residual,
    coadd,
    full,
    bottom,
    mid,
    top,
    low,
    coefs,
    kernels,
    slab,
    toeplitz,
    weight,
    weight_in,
    value_out,
    value_in,
    own_value,
    local_sem,
    send_sem,
    recv_sem,
    back_send,
    back_recv,
):
    n_epoch, n_strip, n_band = sizes
    tile_dev, height, width = template.shape
    exp_dev = science.shape[0]
    n_poly, _, n_sel = coefficients.shape
    ks, _, n_basis = basis.shape
    group = lax.axis_index("groups")
    me = lax.axis_index("epoch")
    strip = lax.axis_index("strip")
    band = lax.axis_index("band")

    side = 2 * lax.div(2 * me, n_epoch) - 1

    def away(step):
        return lax.rem(me + n_epoch + side * step, n_epoch)

    def target(epoch, ds, db):
        return (group, epoch, strip + ds, band + db)

    def there(ds, db):
        sides = []
        if ds < 0:
            sides.append(strip >= -ds)
        if ds > 0:
            sides.append(strip < n_strip - ds)
        if db < 0:
            sides.append(band >= -db)
        if db > 0:
            sides.append(band < n_band - db)
        return sides

    def guarded(sides, body):
        if not sides:
            body()
        elif len(sides) == 1:
            pl.when(sides[0])(body)
        else:
            pl.when(jnp.logical_and(sides[0], sides[1]))(body)

    loads = [
        pltpu.make_async_copy(held, here, local_sem.at[i])
        for i, (held, here) in enumerate(
            (
                (basis_hbm, basis),
                (variance_hbm, variance),
                (bad_mask_hbm, bad_mask),
                (science_hbm, science),
                (intersection_hbm, intersection),
                (template_hbm, template),
                (basis_index_hbm, basis_index),
                (coefficients_hbm, coefficients),
                (offsets_hbm, offsets),
            )
        )
    ]
    for i in (4, 5, 6, 7, 0, 1, 2, 3, 8):
        loads[i].start()

    barrier = pltpu.get_barrier_semaphore()
    for ds, db in STEPS:

        def greet(ds=ds, db=db):
            for step in range(n_epoch):
                if step == 0 and ds == 0 and db == 0:
                    continue
                epoch = away(step)
                pl.semaphore_signal(
                    barrier, inc=1, device_id=target(epoch, ds, db), device_id_type=MESH
                )

        guarded(there(ds, db), greet)

    loads[4].wait()
    loads[5].wait()
    for step in range(n_epoch):
        epoch = away(step)
        tile = intersection[epoch * exp_dev + me] - me * tile_dev
        chosen = template[jnp.clip(tile, 0, tile_dev - 1)]
        full[epoch] = chosen
        wide = chosen.astype(jnp.float32)
        bottom[epoch] = wide[height - EDGE_ROWS :].astype(jnp.bfloat16)
    mid[me, :, LANES : LANES + width] = full[me]

    zero = jnp.bfloat16(0)
    slab[:, height + 2 * EDGE_ROWS :, :] = jnp.zeros((slab.shape[0], 8, LANES), jnp.float32)

    @pl.when(strip == 0)
    def _():
        top[...] = jnp.full(top.shape, zero)

    @pl.when(strip == n_strip - 1)
    def _():
        low[...] = jnp.full(low.shape, zero)

    for edge, lanes in ((band == 0, slice(0, LANES)), (band == n_band - 1, slice(LANES + width, None))):

        @pl.when(edge)
        def _(lanes=lanes):
            mid[:, :, lanes] = jnp.full(mid[:, :, lanes].shape, zero)

            @pl.when(strip > 0)
            def _():
                top[:, :, lanes] = jnp.full(top[:, :, lanes].shape, zero)

            @pl.when(strip < n_strip - 1)
            def _():
                low[:, :, lanes] = jnp.full(low[:, :, lanes].shape, zero)

    partners = n_epoch
    if n_strip > 1:
        near = jnp.minimum(strip, 1) + jnp.minimum(n_strip - 1 - strip, 1)
        partners = partners * (1 + near)
    if n_band > 1:
        near = jnp.minimum(band, 1) + jnp.minimum(n_band - 1 - band, 1)
        partners = partners * (1 + near)
    pl.semaphore_wait(barrier, partners - 1)

    def piece(step, ds, db, arriving):
        other = away(step)
        held = {0: slice(0, width), 1: slice(width - LANES, width), -1: slice(0, LANES)}[db]
        lands = {
            0: slice(LANES, LANES + width),
            1: slice(0, LANES),
            -1: slice(LANES + width, 2 * LANES + width),
        }[db]
        slot = other if arriving else me
        source = full.at[other, :, held]
        dest = mid
        if ds == 1:
            source, dest = bottom.at[other, :, held], top
        if ds == -1:
            source, dest = full.at[other, 0:EDGE_ROWS, held], low
        return pltpu.make_async_remote_copy(
            src_ref=source,
            dst_ref=dest.at[slot, :, lands],
            send_sem=send_sem.at[other, ds + 1, db + 1],
            recv_sem=recv_sem.at[slot, ds + 1, db + 1],
            device_id=target(other, ds, db),
            device_id_type=MESH,
        )

    for step in list(range(1, n_epoch)) + [0]:
        for ds, db in STEPS:
            if step == 0 and ds == 0 and db == 0:
                continue
            guarded(there(ds, db), lambda step=step, ds=ds, db=db: piece(step, ds, db, False).start())

    def back(which, out, into, step, arriving):
        other = away(step)
        slot = other if arriving else me
        return pltpu.make_async_remote_copy(
            src_ref=out.at[other],
            dst_ref=into.at[slot],
            send_sem=back_send.at[which, other],
            recv_sem=back_recv.at[which, slot],
            device_id=target(other, 0, 0),
            device_id_type=MESH,
        )

    loads[1].wait()
    loads[2].wait()
    for exposure in range(exp_dev):
        weight[exposure] = bad_mask[exposure].astype(jnp.float32) / variance[exposure]

    loads[6].wait()
    loads[7].wait()
    lane = lax.broadcasted_iota(jnp.int32, (8, LANES), 1)
    sub = lax.broadcasted_iota(jnp.int32, (8, LANES), 0)
    half = LANES // 2
    highs, lows = [], []
    for exposure in range(exp_dev):
        for p in range(n_poly):
            coefs[exposure, p : p + 1, 0:n_sel] = coefficients[p, exposure : exposure + 1, :]
    for exposure in range(exp_dev):
        some = coefs[exposure]
        parts = []
        for j in range(n_sel):
            column = jnp.broadcast_to(some[:, j : j + 1], (8, LANES))
            parts.append(jnp.where(lane == basis_index[exposure, j], column, 0.0))
        while len(parts) > 1:
            parts = [
                parts[i] + parts[i + 1] if i + 1 < len(parts) else parts[i]
                for i in range(0, len(parts), 2)
            ]
        mix = jnp.where(sub < n_poly, parts[0], 0.0)
        mix = mix + pltpu.roll(mix, half, 1)
        high = mix.astype(jnp.bfloat16).astype(jnp.float32)
        highs.append(high)
        lows.append(mix - high)
    mixes = jnp.concatenate(highs + lows, axis=0).astype(jnp.bfloat16)

    n_pairs = (ks + 1) // 2
    loads[0].wait()
    blank = jnp.zeros((8, LANES), jnp.float32)

    def taps(b, g):
        if b >= ks or g * 8 >= ks:
            return blank
        here = min(8, ks - g * 8)
        tile = basis[g * 8 : g * 8 + here, b, :]
        if here < 8:
            tile = jnp.concatenate([tile, jnp.zeros((8 - here, tile.shape[1]), jnp.float32)], axis=0)
        tile = jnp.concatenate([tile, jnp.zeros((8, LANES - tile.shape[1]), jnp.float32)], axis=1)
        high = tile.astype(jnp.bfloat16).astype(jnp.float32)
        return jnp.where(lane < half, high, pltpu.roll(tile - high, half, 1))

    table = jnp.concatenate(
        [
            taps(2 * q + h, g)
            for q in range(n_pairs)
            for g in range(GROUPS)
            for h in range(2)
        ],
        axis=0,
    ).astype(jnp.bfloat16)
    both = lax.dot_general(
        mixes, table, (((1,), (1,)), ((), ())), preferred_element_type=jnp.float32
    )
    mixed = both[: 8 * exp_dev] + both[8 * exp_dev :]
    kernels[...] = mixed.astype(jnp.bfloat16).astype(jnp.float32)

    for step in range(1, n_epoch):
        back(0, weight, weight_in, step, False).start()

    loads[8].wait()
    later = jnp.bitwise_and(lane, 7) >= sub
    n_tiles = n_pairs * SLOT // LANES
    for exposure in range(exp_dev):
        for p in range(0, n_poly, 2):
            for t in range(n_tiles):
                halves = []
                for h in range(2):
                    at = exposure * 8 + p + h
                    wide = jnp.broadcast_to(
                        kernels[at : at + 1, t * LANES : (t + 1) * LANES], (8, LANES)
                    )
                    near = pltpu.roll(wide, 0, 1, stride=1, stride_axis=0)
                    far = pltpu.roll(wide, 8, 1, stride=1, stride_axis=0)
                    halves.append(jnp.where(later, near, far))
                toeplitz[
                    exposure, p * 8 : (p + 2) * 8, t * LANES : (t + 1) * LANES
                ] = jnp.concatenate(halves, axis=0).astype(jnp.bfloat16)

    row = lax.broadcasted_iota(jnp.int32, (height, 1), 0) + strip * height
    col = lax.broadcasted_iota(jnp.int32, (1, width), 1) + band * width
    r = (2.0 * row.astype(jnp.float32) + 1.0) / (height * n_strip) - 1.0
    c = (2.0 * col.astype(jnp.float32) + 1.0) / (width * n_band) - 1.0
    r = jnp.broadcast_to(r, (height, width))
    c = jnp.broadcast_to(c, (height, width))

    def arrive(step):
        for ds, db in STEPS:
            if ds == 0 and db == 0 and step == 0:
                continue
            guarded(
                there(-ds, -db),
                lambda ds=ds, db=db: piece(step, ds, db, True).wait_recv(),
            )

    loads[3].wait()
    for step in range(n_epoch):
        k = away(step)
        arrive(step)
        n_lane = width // LANES
        for rows, held in ((0, top), (EDGE_ROWS, mid), (EDGE_ROWS + height, low)):
            size = held.shape[1]
            wide = held[k].astype(jnp.float32)
            for t in range(n_lane):
                slab[t, rows : rows + size, :] = wide[:, (t + 1) * LANES : (t + 2) * LANES]
            edge = lax.broadcasted_iota(jnp.int32, (size, LANES), 1) < half
            slab[n_lane, rows : rows + size, :] = jnp.where(
                edge, wide[:, (n_lane + 1) * LANES :], wide[:, :LANES]
            )
        span = height + 8 * GROUPS - 8
        down = EDGE_ROWS - HALF + offsets[0, k]
        along = HALF - offsets[1, k]
        at_lane = lax.broadcasted_iota(jnp.int32, (span, LANES), 1)
        views = []
        for h in range(2):
            turned = [
                pltpu.roll(slab[t, pl.ds(down, span), :], along - h, 1) for t in range(n_lane + 1)
            ]
            views.append(
                jnp.concatenate(
                    [
                        jnp.where(at_lane < along - h, turned[t - 1], turned[t])
                        for t in range(n_lane + 1)
                    ],
                    axis=1,
                )
            )
        tiles = [
            jnp.concatenate(
                [views[0][g * 8 : g * 8 + 8], views[1][g * 8 : g * 8 + 8]], axis=0
            ).astype(jnp.bfloat16)
            for g in range(span // 8)
        ]
        moved = [[tile[:, 2 * q : 2 * q + width] for tile in tiles] for q in range(n_pairs)]
        factor = toeplitz[k]
        for block in range(height // 8):
            stacked = jnp.concatenate(
                [moved[q][block + g] for q in range(n_pairs) for g in range(GROUPS)], axis=0
            )
            conv = jnp.dot(factor, stacked, preferred_element_type=jnp.float32)
            q = [conv[p * 8 : (p + 1) * 8] for p in range(n_poly)]
            at = slice(block * 8, block * 8 + 8)
            rr, cc = r[at], c[at]
            model = q[0] + rr * (q[1] + rr * q[3] + cc * q[4]) + cc * (q[2] + cc * q[5])
            left = science[k, at] - model
            residual[k, at] = left
            value = weight[k, at] * left
            if step == 0:
                own_value[at] = value
            else:
                value_out[k, at] = value
        pltpu.make_async_copy(residual.at[k], residual_out.at[k], local_sem.at[9 + k]).start()
        if step > 0:
            back(1, value_out, value_in, step, False).start()

    numer = [None] * tile_dev
    denom = [None] * tile_dev
    for step in range(n_epoch):
        k = away(step)
        tile = intersection[k * exp_dev + me] - me * tile_dev
        if step == 0:
            upper, under = own_value[...], weight[me]
        else:
            back(0, weight, weight_in, step, True).wait_recv()
            back(1, value_out, value_in, step, True).wait_recv()
            upper = value_in[k]
            under = weight_in[k]
        for t in range(tile_dev):
            here = (tile == t).astype(jnp.float32)
            numer[t] = upper * here if step == 0 else numer[t] + upper * here
            denom[t] = under * here if step == 0 else denom[t] + under * here
    for t in range(tile_dev):
        coadd[t] = numer[t] / (denom[t] + 1.0)
    last = pltpu.make_async_copy(coadd, coadd_out, local_sem.at[9 + n_epoch])
    last.start()

    for step in range(n_epoch):
        for ds, db in STEPS:
            if step == 0 and ds == 0 and db == 0:
                continue
            guarded(
                there(ds, db),
                lambda step=step, ds=ds, db=db: piece(step, ds, db, False).wait_send(),
            )
        if step > 0:
            back(0, weight, weight_in, step, False).wait_send()
            back(1, value_out, value_in, step, False).wait_send()
        k = away(step)
        pltpu.make_async_copy(residual.at[k], residual_out.at[k], local_sem.at[9 + k]).wait()
    last.wait()


def leave(residual, coadd, residual_out, coadd_out, images, tiles, sem):
    parts = [
        (held.at[i], here.at[i], out.at[i])
        for held, here, out in ((residual, images, residual_out), (coadd, tiles, coadd_out))
        for i in range(here.shape[0])
    ]
    arrive = [
        pltpu.make_async_copy(held, here, sem.at[0, i]) for i, (held, here, _) in enumerate(parts)
    ]
    depart = [
        pltpu.make_async_copy(here, out, sem.at[1, i]) for i, (_, here, out) in enumerate(parts)
    ]
    for copy in arrive:
        copy.start()
    for i in range(len(parts)):
        arrive[i].wait()
        depart[i].start()
    for copy in depart:
        copy.wait()


def local(sizes, template, science, variance, bad_mask, intersection, offsets, basis_index, coefficients, basis):
    n_epoch = sizes[0]
    tile_dev, height, width = template.shape
    exp_dev = science.shape[0]
    assert exp_dev == n_epoch
    n_poly = coefficients.shape[2]
    ks = basis.shape[1]
    lanes_all = width + 2 * LANES
    n_pairs = (ks + 1) // 2
    far = pl.BlockSpec(memory_space=pltpu.HBM)
    free = pl.BlockSpec(memory_space=pl.ANY)
    bf16, f32 = jnp.bfloat16, jnp.float32
    dma = pltpu.SemaphoreType.DMA
    offsets = offsets.T
    coefficients = coefficients.transpose(2, 0, 1)
    basis = basis.transpose(1, 2, 0)
    residual, coadd = pl.pallas_call(
        functools.partial(kernel, sizes),
        out_shape=(
            jax.ShapeDtypeStruct(science.shape, f32),
            jax.ShapeDtypeStruct(template.shape, f32),
        ),
        in_specs=[far] * 9,
        out_specs=(free, free),
        scratch_shapes=[
            pltpu.SMEM(intersection.shape, jnp.int32),
            pltpu.SMEM(offsets.shape, jnp.int32),
            pltpu.SMEM(basis_index.shape, jnp.int32),
            pltpu.VMEM(coefficients.shape, f32),
            pltpu.VMEM(template.shape, bf16),
            pltpu.VMEM(science.shape, f32),
            pltpu.VMEM(science.shape, f32),
            pltpu.VMEM(science.shape, jnp.int32),
            pltpu.VMEM(basis.shape, f32),
            pltpu.VMEM(science.shape, f32),
            pltpu.VMEM(template.shape, f32),
            pltpu.VMEM((n_epoch, height, width), bf16),
            pltpu.VMEM((n_epoch, EDGE_ROWS, width), bf16),
            pltpu.VMEM((exp_dev, height, lanes_all), bf16),
            pltpu.VMEM((exp_dev, EDGE_ROWS, lanes_all), bf16),
            pltpu.VMEM((exp_dev, EDGE_ROWS, lanes_all), bf16),
            pltpu.VMEM((exp_dev, 8, LANES), f32),
            pltpu.VMEM((8 * exp_dev, n_pairs * SLOT), f32),
            pltpu.VMEM((width // LANES + 1, 2 * EDGE_ROWS + height + 8, LANES), f32),
            pltpu.VMEM((exp_dev, n_poly * 8, n_pairs * SLOT), bf16),
            pltpu.VMEM((exp_dev, height, width), f32),
            pltpu.VMEM((exp_dev, height, width), f32),
            pltpu.VMEM((exp_dev, height, width), f32),
            pltpu.VMEM((exp_dev, height, width), f32),
            pltpu.VMEM((height, width), f32),
            dma((10 + n_epoch,)),
            dma((n_epoch, 3, 3)),
            dma((n_epoch, 3, 3)),
            dma((2, n_epoch)),
            dma((2, n_epoch)),
        ],
        compiler_params=pltpu.CompilerParams(
            collective_id=0, has_side_effects=True
        ),
    )(
        intersection, offsets, basis_index, coefficients,
        template, science, variance, bad_mask, basis,
    )
    return pl.pallas_call(
        leave,
        out_shape=(
            jax.ShapeDtypeStruct(science.shape, f32),
            jax.ShapeDtypeStruct(template.shape, f32),
        ),
        in_specs=[free] * 2,
        out_specs=(free, free),
        scratch_shapes=[
            pltpu.VMEM(science.shape, f32),
            pltpu.VMEM(template.shape, f32),
            dma((2, exp_dev + tile_dev)),
        ],
    )(residual, coadd)


def solution(mesh):
    sizes = (mesh.shape["epoch"], mesh.shape["strip"], mesh.shape["band"])
    image = P(("groups", "epoch"), "strip", "band")
    split = ("groups", "epoch")
    in_specs = (
        image, image, image, image, P("groups"),
        P(split, None), P(split, None), P(split, None, None), P(),
    )
    return jax.shard_map(
        functools.partial(local, sizes),
        mesh=mesh,
        in_specs=in_specs,
        out_specs=(image, image),
        check_vma=False,
    )
```

```python
import functools

import jax
import jax.numpy as jnp
from jax import lax
from jax.experimental import pallas as pl
from jax.experimental.pallas import tpu as pltpu
from jax.sharding import PartitionSpec as P

HALF = 9
SHIFT = 4
EDGE_ROWS = 16
LANES = 128
SLOT = 64
GROUPS = 4
SCIENCE_TOP = 6.0
WEIGHT_TOP = 0.5
LEVELS = 65535.0

MESH = pl.DeviceIdType.MESH


def links_of(size, place):
    if size == 1:
        return []
    if size == 2:
        return [(1 - 2 * place, 0, place, None, None)]
    return [
        (-1, 0, 1, place > 0, place < size - 1),
        (1, 1, 0, place < size - 1, place > 0),
    ]


def both(first, second):
    if first is None:
        return second
    if second is None:
        return first
    return jnp.logical_and(first, second)


def guarded(side, body):
    if side is None:
        body()
    else:
        pl.when(side)(body)


def encode(science, weight):
    high = (science + SCIENCE_TOP) * (LEVELS / (2.0 * SCIENCE_TOP)) + 0.5
    low = weight * (LEVELS / WEIGHT_TOP) + 0.5
    high = jnp.clip(high, 0.0, LEVELS).astype(jnp.int32)
    low = jnp.clip(low, 0.0, LEVELS).astype(jnp.int32)
    return jnp.bitwise_or(jnp.left_shift(high, 16), low)


def decode(code):
    high = lax.shift_right_logical(code, jnp.full(code.shape, 16, jnp.int32))
    low = jnp.bitwise_and(code, 65535)
    science = high.astype(jnp.float32) * (2.0 * SCIENCE_TOP / LEVELS) - SCIENCE_TOP
    return science, low.astype(jnp.float32) * (WEIGHT_TOP / LEVELS)


def kernel(
    sizes,
    intersection_hbm,
    offsets_hbm,
    basis_index_hbm,
    coefficients_hbm,
    template_hbm,
    science_hbm,
    variance_hbm,
    bad_mask_hbm,
    basis_hbm,
    residual,
    coadd,
    intersection,
    offsets,
    offsets_in,
    basis_index,
    basis_index_in,
    coefficients,
    coefficients_in,
    template,
    science,
    variance,
    bad_mask,
    basis,
    chosen,
    chosen_edge,
    own_edge,
    centre,
    vertical,
    lateral,
    corner,
    own_vertical,
    own_lateral,
    own_corner,
    coefs,
    table,
    kernels,
    slab,
    toeplitz,
    weight,
    code,
    code_in,
    model_out,
    numer,
    denom,
    local_sem,
    send_sem,
    recv_sem,
    own_send,
    own_recv,
):
    n_epoch, n_strip, n_band = sizes
    tile_dev, height, width = template.shape
    exp_dev = science.shape[0]
    n_poly, _, n_sel = coefficients.shape
    ks, _, n_basis = basis.shape
    n_lane = width // LANES
    half = LANES // 2
    f32, bf16 = jnp.float32, jnp.bfloat16
    group = lax.axis_index("groups")
    me = lax.axis_index("epoch")
    strip = lax.axis_index("strip")
    band = lax.axis_index("band")

    ups = links_of(n_strip, strip)
    sides = links_of(n_band, band)
    none = (0, None, None, None, None)
    near = [(u, s) for u in [none] + ups for s in [none] + sides]

    def device(epoch, u, s):
        return (group, epoch, strip + u[0], band + s[0])

    loads = [
        pltpu.make_async_copy(held, here, local_sem.at[i])
        for i, (held, here) in enumerate(
            (
                (intersection_hbm, intersection),
                (template_hbm, template),
                (variance_hbm, variance),
                (bad_mask_hbm, bad_mask),
                (science_hbm, science),
                (basis_index_hbm, basis_index),
                (coefficients_hbm, coefficients),
                (basis_hbm, basis),
                (offsets_hbm, offsets),
            )
        )
    ]
    for load in loads:
        load.start()

    barrier = pltpu.get_barrier_semaphore()

    def greet(epoch, skip):
        for u, s in near:
            if skip and u is none and s is none:
                continue

            def hello(u=u, s=s):
                pl.semaphore_signal(
                    barrier, inc=1, device_id=device(epoch, u, s), device_id_type=MESH
                )

            guarded(both(u[3], s[3]), hello)

    greet(me, True)
    for step in range(n_epoch - 1, 0, -1):
        pl.when(me + step < n_epoch)(lambda step=step: greet(me + step, False))

    def count(size, place):
        if size < 3:
            return size
        return 1 + jnp.minimum(place, 1) + jnp.minimum(size - 1 - place, 1)

    partners = count(n_strip, strip) * count(n_band, band)
    pl.semaphore_wait(barrier, partners * (me + 1) - 1)

    def slot_of(sender, receiver):
        return sender - (sender > receiver).astype(jnp.int32)

    def lanes_of(s):
        if n_band == 2:
            start = (1 - band) * (width - LANES)
            return pl.ds(pl.multiple_of(start, LANES), LANES)
        return slice(0, LANES) if s[1] == 0 else slice(width - LANES, width)

    def copy(source, dest, sent, received, to):
        return pltpu.make_async_remote_copy(
            src_ref=source,
            dst_ref=dest,
            send_sem=sent,
            recv_sem=received,
            device_id=to,
            device_id_type=MESH,
        )

    n_up, n_side = len(ups), len(sides)
    images = []
    for u, s in near:
        i = 0 if u is none else 1 + ups.index(u)
        j = 0 if s is none else 1 + sides.index(s)
        images.append((u, s, i * (1 + n_side) + j))
    n_image = (1 + n_up) * (1 + n_side)
    CODE, COEF, OFFS, INDX = n_image, n_image + 1, n_image + 2, n_image + 3

    def image(epoch, u, s, kind, sender, at=None):
        source_at = epoch if at is None else at
        if u is none and s is none:
            source, dest = chosen.at[source_at], centre.at[sender]
        elif s is none:
            source, dest = chosen_edge.at[u[1], source_at], vertical.at[u[2], sender]
        elif u is none:
            source, dest = chosen.at[source_at, :, lanes_of(s)], lateral.at[s[2], sender]
        else:
            source = chosen_edge.at[u[1], source_at, :, lanes_of(s)]
            dest = corner.at[u[2], s[2], sender]
        return copy(
            source, dest, send_sem.at[kind], recv_sem.at[slot_of(sender, epoch), kind], device(epoch, u, s)
        )

    def arriving(epoch, u, s, kind):
        if u is none and s is none:
            dest = centre.at[epoch]
        elif s is none:
            dest = vertical.at[u[2], epoch]
        elif u is none:
            dest = lateral.at[s[2], epoch]
        else:
            dest = corner.at[u[2], s[2], epoch]
        return copy(dest, dest, send_sem.at[kind], recv_sem.at[slot_of(epoch, me), kind], device(epoch, u, s))

    def landing(links, place, size):
        if size == 2:
            return [(k[0], k[1], 1 - place, None, None) for k in links]
        return [(k[0], k[1], k[2], k[4], k[3]) for k in links]

    ups_in = landing(ups, strip, n_strip)
    sides_in = landing(sides, band, n_band)
    images_in = []
    for u, s, kind in images:
        a = none if u is none else ups_in[ups.index(u)]
        b = none if s is none else sides_in[sides.index(s)]
        images_in.append((a, b, kind))

    def send_image(epoch):
        for u, s, kind in images:
            guarded(
                both(u[3], s[3]), lambda u=u, s=s, kind=kind: image(epoch, u, s, kind, me).start()
            )

    def wait_image(epoch):
        for u, s, kind in images_in:
            guarded(
                both(u[3], s[3]), lambda u=u, s=s, kind=kind: arriving(epoch, u, s, kind).wait_recv()
            )

    def small(epoch, sender):
        return [
            copy(held, into.at[sender], send_sem.at[kind], recv_sem.at[slot_of(sender, epoch), kind], device(epoch, none, none))
            for held, into, kind in (
                (offsets_hbm, offsets_in, OFFS),
                (basis_index_hbm, basis_index_in, INDX),
                (coefficients_hbm, coefficients_in, COEF),
            )
        ]

    def coded(epoch, sender):
        return copy(
            code.at[epoch], code_in.at[sender], send_sem.at[CODE], recv_sem.at[slot_of(sender, epoch), CODE],
            device(epoch, none, none),
        )

    def own_piece(u, s, kind, incoming):
        if s is none:
            source, dest = own_edge.at[0 if incoming else u[1]], own_vertical.at[u[2]]
        elif u is none:
            source, dest = template.at[:, :, lanes_of(s)], own_lateral.at[s[2]]
        else:
            source = own_edge.at[0 if incoming else u[1], :, :, lanes_of(s)]
            dest = own_corner.at[u[2], s[2]]
        if incoming:
            source = dest
        return copy(source, dest, own_send.at[kind], own_recv.at[kind], device(me, u, s))

    def send_small(epoch):
        for one in small(epoch, me):
            one.start()

    for epoch in range(n_epoch - 1):
        pl.when(epoch < me)(lambda epoch=epoch: send_small(epoch))

    loads[0].wait()
    loads[1].wait()

    def rim(wide, which):
        low, high = wide[:EDGE_ROWS], wide[height - EDGE_ROWS :]
        if n_strip == 2:
            return jnp.where(strip == 0, high, low)
        return low if which == 0 else high

    for epoch in range(n_epoch):
        tile = intersection[epoch * exp_dev + me] - me * tile_dev
        picked = template[jnp.clip(tile, 0, tile_dev - 1)]
        chosen[epoch] = picked
        wide = picked.astype(f32)
        for which in range(n_up):
            chosen_edge[which, epoch] = rim(wide, which).astype(bf16)
    for epoch in range(n_epoch - 1):
        pl.when(epoch < me)(lambda epoch=epoch: send_image(epoch))
    for t in range(tile_dev):
        wide = template[t].astype(f32)
        for which in range(n_up):
            own_edge[which, t] = rim(wide, which).astype(bf16)
    for u, s, kind in images[1:]:
        guarded(both(u[3], s[3]), lambda u=u, s=s, kind=kind: own_piece(u, s, kind, False).start())

    def clear(ref):
        ref[...] = jnp.zeros(ref.shape, ref.dtype)

    def clear_up(slot):
        clear(vertical.at[slot])
        clear(own_vertical.at[slot])

    def clear_side(slot):
        clear(lateral.at[slot])
        clear(own_lateral.at[slot])

    def clear_corner(slot, at):
        clear(corner.at[slot, at])
        clear(own_corner.at[slot, at])

    loads[2].wait()
    loads[3].wait()
    loads[4].wait()
    for epoch in range(n_epoch):
        share = bad_mask[epoch].astype(f32) / variance[epoch]
        weight[epoch] = share
        code[epoch] = encode(science[epoch], share)
    for epoch in range(n_epoch - 1):
        pl.when(epoch < me)(lambda epoch=epoch: coded(epoch, me).start())

    if n_strip == 1:
        clear(vertical)
        clear(own_vertical)
        clear(corner)
        clear(own_corner)
    elif n_strip == 2:
        clear_up(strip)
        for at in range(2):
            clear_corner(strip, at)
    else:
        for slot, edge in ((0, strip == 0), (1, strip == n_strip - 1)):

            @pl.when(edge)
            def _(slot=slot):
                clear_up(slot)
                for at in range(2):
                    clear_corner(slot, at)

    if n_band == 1:
        clear(lateral)
        clear(own_lateral)
        if n_strip > 1:
            clear(corner)
            clear(own_corner)
    elif n_band == 2:
        clear_side(band)
        if n_strip == 2:
            clear_corner(1 - strip, band)
        elif n_strip > 2:
            for slot, held in ((0, strip > 0), (1, strip < n_strip - 1)):
                pl.when(held)(lambda slot=slot: clear_corner(slot, band))
    else:
        for slot, edge in ((0, band == 0), (1, band == n_band - 1)):

            @pl.when(edge)
            def _(slot=slot):
                clear_side(slot)
                for at in range(2):
                    clear_corner(at, slot)

    slab[:, :, height + 2 * EDGE_ROWS :, :] = jnp.zeros(
        (slab.shape[0], slab.shape[1], 8, LANES), f32
    )

    lane = lax.broadcasted_iota(jnp.int32, (8, LANES), 1)
    sub = lax.broadcasted_iota(jnp.int32, (8, LANES), 0)
    n_pairs = (ks + 1) // 2
    n_tiles = n_pairs * SLOT // LANES
    later = jnp.bitwise_and(lane, 7) >= sub

    def mix_of(row, coefficient, indices):
        for p in range(n_poly):
            coefs[row, p : p + 1, 0:n_sel] = coefficient(p)
        some = coefs[row]
        parts = []
        for j in range(n_sel):
            column = jnp.broadcast_to(some[:, j : j + 1], (8, LANES))
            parts.append(jnp.where(lane == indices(j), column, 0.0))
        while len(parts) > 1:
            parts = [
                parts[i] + parts[i + 1] if i + 1 < len(parts) else parts[i]
                for i in range(0, len(parts), 2)
            ]
        mix = jnp.where(sub < n_poly, parts[0], 0.0)
        mix = mix + pltpu.roll(mix, half, 1)
        high = mix.astype(bf16).astype(f32)
        return high, mix - high

    def mixed(pairs):
        rows = jnp.concatenate([p[0] for p in pairs] + [p[1] for p in pairs], axis=0)
        out = lax.dot_general(
            rows.astype(bf16), table[...], (((1,), (1,)), ((), ())), preferred_element_type=f32
        )
        size = 8 * len(pairs)
        return (out[:size] + out[size:]).astype(bf16).astype(f32)

    def spread(row, into):
        for p in range(0, n_poly, 2):
            for t in range(n_tiles):
                halves = []
                for h in range(2):
                    at = row * 8 + p + h
                    wide = jnp.broadcast_to(
                        kernels[at : at + 1, t * LANES : (t + 1) * LANES], (8, LANES)
                    )
                    close = pltpu.roll(wide, 0, 1, stride=1, stride_axis=0)
                    far = pltpu.roll(wide, 8, 1, stride=1, stride_axis=0)
                    halves.append(jnp.where(later, close, far))
                toeplitz[into, p * 8 : (p + 2) * 8, t * LANES : (t + 1) * LANES] = (
                    jnp.concatenate(halves, axis=0).astype(bf16)
                )

    loads[5].wait()
    loads[6].wait()
    pairs = [
        mix_of(
            exposure,
            lambda p, exposure=exposure: coefficients[p, exposure : exposure + 1, :],
            lambda j, exposure=exposure: basis_index[exposure, j],
        )
        for exposure in range(exp_dev)
    ]

    loads[7].wait()
    blank = jnp.zeros((8, LANES), f32)

    def taps(b, g):
        if b >= ks or g * 8 >= ks:
            return blank
        here = min(8, ks - g * 8)
        tile = basis[g * 8 : g * 8 + here, b, :]
        if here < 8:
            tile = jnp.concatenate([tile, jnp.zeros((8 - here, n_basis), f32)], axis=0)
        tile = jnp.concatenate([tile, jnp.zeros((8, LANES - n_basis), f32)], axis=1)
        high = tile.astype(bf16).astype(f32)
        return jnp.where(lane < half, high, pltpu.roll(tile - high, half, 1))

    table[...] = jnp.concatenate(
        [
            taps(2 * q + h, g)
            for q in range(n_pairs)
            for g in range(GROUPS)
            for h in range(2)
        ],
        axis=0,
    ).astype(bf16)
    kernels[0 : 8 * exp_dev] = mixed(pairs)
    loads[8].wait()
    for exposure in range(exp_dev):
        spread(exposure, exposure)

    row = lax.broadcasted_iota(jnp.int32, (height, 1), 0) + strip * height
    col = lax.broadcasted_iota(jnp.int32, (1, width), 1) + band * width
    r = (2.0 * row.astype(f32) + 1.0) / (height * n_strip) - 1.0
    c = (2.0 * col.astype(f32) + 1.0) / (width * n_band) - 1.0
    r = jnp.broadcast_to(r, (height, width))
    c = jnp.broadcast_to(c, (height, width))

    span = height + 8 * GROUPS - 8
    at_lane = lax.broadcasted_iota(jnp.int32, (span, LANES), 1)

    def lay(board, middle, up, side, edge, at):
        for rows, body, rims in (
            (0, up(0), (edge(0, 1), edge(0, 0))),
            (EDGE_ROWS, middle, (side(1), side(0))),
            (EDGE_ROWS + height, up(1), (edge(1, 1), edge(1, 0))),
        ):
            wide = body.astype(f32)
            size = wide.shape[0]
            for t in range(n_lane):
                slab[board, t, rows : rows + size, :] = wide[:, t * LANES : (t + 1) * LANES]
            first = lax.broadcasted_iota(jnp.int32, (size, LANES), 1) < half
            slab[board, n_lane, rows : rows + size, :] = jnp.where(
                first, rims[0].astype(f32), rims[1].astype(f32)
            )

    def lay_own(board, tile):
        lay(
            board,
            template[tile],
            lambda v: own_vertical[v, tile],
            lambda s: own_lateral[s, tile],
            lambda v, s: own_corner[v, s, tile],
            tile,
        )

    def lay_other(board, epoch):
        lay(
            board,
            centre[epoch],
            lambda v: vertical[v, epoch],
            lambda s: lateral[s, epoch],
            lambda v, s: corner[v, s, epoch],
            epoch,
        )

    def models(board, factor, down, along):
        views = []
        for h in range(2):
            turned = [
                pltpu.roll(slab[board, t, pl.ds(down, span), :], along - h, 1)
                for t in range(n_lane + 1)
            ]
            views.append(
                jnp.concatenate(
                    [
                        jnp.where(at_lane < along - h, turned[t - 1], turned[t])
                        for t in range(n_lane + 1)
                    ],
                    axis=1,
                )
            )
        tiles = [
            jnp.concatenate(
                [views[0][g * 8 : g * 8 + 8], views[1][g * 8 : g * 8 + 8]], axis=0
            ).astype(bf16)
            for g in range(span // 8)
        ]
        moved = [[tile[:, 2 * q : 2 * q + width] for tile in tiles] for q in range(n_pairs)]
        for block in range(height // 8):
            stacked = jnp.concatenate(
                [moved[q][block + g] for q in range(n_pairs) for g in range(GROUPS)], axis=0
            )
            conv = jnp.dot(factor, stacked, preferred_element_type=f32)
            q = [conv[p * 8 : (p + 1) * 8] for p in range(n_poly)]
            at = slice(block * 8, block * 8 + 8)
            rr, cc = r[at], c[at]
            yield at, q[0] + rr * (q[1] + rr * q[3] + cc * q[4]) + cc * (q[2] + cc * q[5])

    def tile_of(epoch):
        return intersection[epoch * exp_dev + me] - me * tile_dev

    def down_of(shift):
        return EDGE_ROWS - HALF + shift

    def along_of(shift):
        return HALF - shift

    for u, s, kind in images_in[1:]:
        guarded(both(u[3], s[3]), lambda u=u, s=s, kind=kind: own_piece(u, s, kind, True).wait_recv())

    tile = tile_of(me)
    lay_own(0, jnp.clip(tile, 0, tile_dev - 1))
    for at, model in models(0, toeplitz[me], down_of(offsets[0, me]), along_of(offsets[1, me])):
        left = science[me, at] - model
        residual[me, at] = left
        share = weight[me, at]
        for t in range(tile_dev):
            here = (tile == t).astype(f32)
            numer[t, at] = share * left * here
            denom[t, at] = share * here

    def process(step):
        ahead = me + step < n_epoch
        epoch = jnp.where(ahead, me + step, n_epoch - 1 - step)
        for one in small(me, epoch):
            one.wait_recv()
        last = exp_dev
        kernels[8 * last : 8 * last + 8] = mixed(
            [
                mix_of(
                    last,
                    lambda p: coefficients_in[epoch, p, pl.ds(me, 1), :],
                    lambda j: basis_index_in[epoch, me, j],
                )
            ]
        )
        spread(last, last)
        tile = tile_of(epoch)
        lay_own(0, jnp.clip(tile, 0, tile_dev - 1))
        for at, model in models(
            0, toeplitz[last], down_of(offsets_in[epoch, 0, me]), along_of(offsets_in[epoch, 1, me])
        ):
            model_out[at] = model

        wait_image(epoch)

        @pl.when(ahead)
        def _():
            send_image(epoch)
            send_small(epoch)
            coded(epoch, me).start()

        lay_other(1, epoch)
        for at, model in models(
            1, toeplitz[epoch], down_of(offsets[0, epoch]), along_of(offsets[1, epoch])
        ):
            residual[epoch, at] = science[epoch, at] - model

        coded(me, epoch).wait_recv()
        seen, share = decode(code_in[epoch])
        value = share * (seen - model_out[...])
        for t in range(tile_dev):
            here = (tile == t).astype(f32)
            numer[t] = numer[t] + value * here
            denom[t] = denom[t] + share * here

    if n_epoch <= 4:
        for step in range(1, n_epoch):
            process(step)
    else:
        lax.fori_loop(1, n_epoch, lambda step, carry: (process(step), carry)[1], 0)

    for t in range(tile_dev):
        coadd[t] = numer[t] / (denom[t] + 1.0)

    for u, s, kind in images[1:]:
        guarded(both(u[3], s[3]), lambda u=u, s=s, kind=kind: own_piece(u, s, kind, False).wait_send())
    if n_epoch > 1:
        rest = pl.ds(0, n_epoch - 1)
        for u, s, kind in images:

            def gone(u=u, s=s, kind=kind):
                if u is none and s is none:
                    source = chosen.at[rest]
                elif s is none:
                    source = chosen_edge.at[u[1], rest]
                elif u is none:
                    source = chosen.at[rest, :, lanes_of(s)]
                else:
                    source = chosen_edge.at[u[1], rest, :, lanes_of(s)]
                copy(source, source, send_sem.at[kind], recv_sem.at[0, kind], device(me, u, s)).wait_send()

            guarded(both(u[3], s[3]), gone)
        for held, kind in (
            (offsets_in, OFFS),
            (basis_index_in, INDX),
            (coefficients_in, COEF),
            (code, CODE),
        ):
            source = held.at[rest]
            copy(
                source, source, send_sem.at[kind], recv_sem.at[0, kind], device(me, none, none)
            ).wait_send()


def leave(residual, coadd, residual_out, coadd_out, sem):
    parts = [
        (held.at[i], out.at[i])
        for held, out in ((residual, residual_out), (coadd, coadd_out))
        for i in range(held.shape[0])
    ]
    copies = [pltpu.make_async_copy(held, out, sem.at[i]) for i, (held, out) in enumerate(parts)]
    for one in copies:
        one.start()
    for one in copies:
        one.wait()


def local(sizes, template, science, variance, bad_mask, intersection, offsets, basis_index, coefficients, basis):
    n_epoch, n_strip, n_band = sizes
    tile_dev, height, width = template.shape
    exp_dev = science.shape[0]
    assert exp_dev == n_epoch
    n_poly = coefficients.shape[2]
    n_sel = basis_index.shape[1]
    ks = basis.shape[1]
    n_pairs = (ks + 1) // 2
    far = pl.BlockSpec(memory_space=pltpu.HBM)
    near = pl.BlockSpec(memory_space=pltpu.VMEM)
    free = pl.BlockSpec(memory_space=pl.ANY)
    bf16, f32 = jnp.bfloat16, jnp.float32
    dma = pltpu.SemaphoreType.DMA
    offsets = offsets.T
    coefficients = coefficients.transpose(2, 0, 1)
    basis = basis.transpose(1, 2, 0)
    n_up, n_side = min(n_strip - 1, 2), min(n_band - 1, 2)
    n_image = (1 + n_up) * (1 + n_side)
    edges = max(n_up, 1)
    rim = EDGE_ROWS
    residual, coadd = pl.pallas_call(
        functools.partial(kernel, sizes),
        out_shape=(
            pltpu.VMEM(science.shape, f32),
            pltpu.VMEM(template.shape, f32),
        ),
        in_specs=[far] * 9,
        out_specs=(near, near),
        scratch_shapes=[
            pltpu.SMEM(intersection.shape, jnp.int32),
            pltpu.SMEM(offsets.shape, jnp.int32),
            pltpu.SMEM((n_epoch,) + offsets.shape, jnp.int32),
            pltpu.SMEM(basis_index.shape, jnp.int32),
            pltpu.SMEM((n_epoch,) + basis_index.shape, jnp.int32),
            pltpu.VMEM(coefficients.shape, f32),
            pltpu.VMEM((n_epoch,) + coefficients.shape, f32),
            pltpu.VMEM(template.shape, bf16),
            pltpu.VMEM(science.shape, f32),
            pltpu.VMEM(science.shape, f32),
            pltpu.VMEM(science.shape, jnp.int32),
            pltpu.VMEM(basis.shape, f32),
            pltpu.VMEM((n_epoch, height, width), bf16),
            pltpu.VMEM((edges, n_epoch, rim, width), bf16),
            pltpu.VMEM((edges, tile_dev, rim, width), bf16),
            pltpu.VMEM((n_epoch, height, width), bf16),
            pltpu.VMEM((2, n_epoch, rim, width), bf16),
            pltpu.VMEM((2, n_epoch, height, LANES), bf16),
            pltpu.VMEM((2, 2, n_epoch, rim, LANES), bf16),
            pltpu.VMEM((2, tile_dev, rim, width), bf16),
            pltpu.VMEM((2, tile_dev, height, LANES), bf16),
            pltpu.VMEM((2, 2, tile_dev, rim, LANES), bf16),
            pltpu.VMEM((exp_dev + 1, 8, LANES), f32),
            pltpu.VMEM((n_pairs * SLOT, LANES), bf16),
            pltpu.VMEM((8 * exp_dev + 8, n_pairs * SLOT), f32),
            pltpu.VMEM((2, width // LANES + 1, 2 * rim + height + 8, LANES), f32),
            pltpu.VMEM((exp_dev + 1, n_poly * 8, n_pairs * SLOT), bf16),
            pltpu.VMEM((exp_dev, height, width), f32),
            pltpu.VMEM((n_epoch, height, width), jnp.int32),
            pltpu.VMEM((n_epoch, height, width), jnp.int32),
            pltpu.VMEM((height, width), f32),
            pltpu.VMEM(template.shape, f32),
            pltpu.VMEM(template.shape, f32),
            dma((9,)),
            dma((n_image + 4,)),
            dma((max(n_epoch - 1, 1), n_image + 4)),
            dma((n_image,)),
            dma((n_image,)),
        ],
        compiler_params=pltpu.CompilerParams(
            collective_id=0, has_side_effects=True
        ),
    )(
        intersection, offsets, basis_index, coefficients,
        template, science, variance, bad_mask, basis,
    )
    return pl.pallas_call(
        leave,
        out_shape=(
            jax.ShapeDtypeStruct(science.shape, f32),
            jax.ShapeDtypeStruct(template.shape, f32),
        ),
        in_specs=[near] * 2,
        out_specs=(free, free),
        scratch_shapes=[dma((exp_dev + tile_dev,))],
    )(*(pltpu.with_memory_space_constraint(x, pltpu.VMEM) for x in (residual, coadd)))


def solution(mesh):
    sizes = (mesh.shape["epoch"], mesh.shape["strip"], mesh.shape["band"])
    image = P(("groups", "epoch"), "strip", "band")
    split = ("groups", "epoch")
    in_specs = (
        image, image, image, image, P("groups"),
        P(split, None), P(split, None), P(split, None, None), P(),
    )
    return jax.shard_map(
        functools.partial(local, sizes),
        mesh=mesh,
        in_specs=in_specs,
        out_specs=(image, image),
        check_vma=False,
    )
```

```python
import functools

import jax
import jax.numpy as jnp
from jax import lax
from jax.experimental import pallas as pl
from jax.experimental.pallas import tpu as pltpu
from jax.sharding import PartitionSpec as P

HALF = 9
SHIFT = 4
EDGE_ROWS = 16
LANES = 128
SLOT = 64
GROUPS = 4
SCIENCE_TOP = 6.0
WEIGHT_TOP = 0.5
LEVELS = 65535.0

MESH = pl.DeviceIdType.MESH


def links_of(size, place):
    if size == 1:
        return []
    if size == 2:
        return [(1 - 2 * place, 0, place, None, None)]
    return [
        (-1, 0, 1, place > 0, place < size - 1),
        (1, 1, 0, place < size - 1, place > 0),
    ]


def both(first, second):
    if first is None:
        return second
    if second is None:
        return first
    return jnp.logical_and(first, second)


def guarded(side, body):
    if side is None:
        body()
    else:
        pl.when(side)(body)


def encode(science, weight):
    high = (science + SCIENCE_TOP) * (LEVELS / (2.0 * SCIENCE_TOP)) + 0.5
    low = weight * (LEVELS / WEIGHT_TOP) + 0.5
    high = jnp.clip(high, 0.0, LEVELS).astype(jnp.int32)
    low = jnp.clip(low, 0.0, LEVELS).astype(jnp.int32)
    return jnp.bitwise_or(jnp.left_shift(high, 16), low)


def decode(code):
    high = lax.shift_right_logical(code, jnp.full(code.shape, 16, jnp.int32))
    low = jnp.bitwise_and(code, 65535)
    science = high.astype(jnp.float32) * (2.0 * SCIENCE_TOP / LEVELS) - SCIENCE_TOP
    return science, low.astype(jnp.float32) * (WEIGHT_TOP / LEVELS)


def kernel(
    sizes,
    intersection_hbm,
    offsets_hbm,
    basis_index_hbm,
    coefficients_hbm,
    template_hbm,
    science_hbm,
    variance_hbm,
    bad_mask_hbm,
    basis_hbm,
    residual,
    coadd,
    intersection,
    offsets,
    offsets_in,
    basis_index,
    basis_index_in,
    coefficients,
    coefs_in,
    template,
    science,
    variance,
    bad_mask,
    basis,
    chosen,
    chosen_edge,
    own_edge,
    centre,
    vertical,
    lateral,
    corner,
    own_vertical,
    own_lateral,
    own_corner,
    coefs,
    table,
    kernels,
    slab,
    toeplitz,
    weight,
    code,
    code_in,
    model_out,
    numer,
    denom,
    local_sem,
    send_sem,
    recv_sem,
    own_send,
    own_recv,
    token,
):
    n_epoch, n_strip, n_band = sizes
    tile_dev, height, width = template.shape
    exp_dev = science.shape[0]
    n_poly, _, n_sel = coefficients.shape
    ks, _, n_basis = basis.shape
    n_lane = width // LANES
    half = LANES // 2
    f32, bf16 = jnp.float32, jnp.bfloat16
    group = lax.axis_index("groups")
    me = lax.axis_index("epoch")
    strip = lax.axis_index("strip")
    band = lax.axis_index("band")

    ups = links_of(n_strip, strip)
    sides = links_of(n_band, band)
    none = (0, None, None, None, None)
    near = [(u, s) for u in [none] + ups for s in [none] + sides]

    def device(epoch, u, s):
        return (group, epoch, strip + u[0], band + s[0])

    loads = [
        pltpu.make_async_copy(held, here, local_sem.at[i])
        for i, (held, here) in enumerate(
            (
                (intersection_hbm, intersection),
                (template_hbm, template),
                (variance_hbm, variance),
                (bad_mask_hbm, bad_mask),
                (science_hbm, science),
                (coefficients_hbm, coefficients),
                (basis_index_hbm, basis_index),
                (basis_hbm, basis),
                (offsets_hbm, offsets),
            )
        )
    ]
    for load in loads:
        load.start()

    def count(size, place):
        if size < 3:
            return size
        return 1 + jnp.minimum(place, 1) + jnp.minimum(size - 1 - place, 1)

    def before(size, place):
        return place if size < 3 else jnp.minimum(place, 1)

    across = count(n_band, band)
    partners = count(n_strip, strip) * across
    ahead_of_me = before(n_strip, strip) * across + before(n_band, band)

    def lower(u, s):
        if u is not none:
            return strip + u[0] < strip
        return band + s[0] < band

    barrier = pltpu.get_barrier_semaphore()

    def signal(sem, epoch, u, s):
        pl.semaphore_signal(sem, inc=1, device_id=device(epoch, u, s), device_id_type=MESH)

    def to_epoch(sem, epoch):
        for u, s in near:
            guarded(both(u[3], s[3]), lambda u=u, s=s: signal(sem, epoch, u, s))

    for u, s in near[1:]:
        guarded(
            both(both(u[3], s[3]), jnp.logical_not(lower(u, s))),
            lambda u=u, s=s: signal(barrier, me, u, s),
        )
    for step in range(1, n_epoch):
        pl.when(me + step < n_epoch)(lambda step=step: to_epoch(barrier, me + step))
    met = partners * me + ahead_of_me

    @pl.when(met > 0)
    def _():
        pl.semaphore_wait(barrier, met)

    for u, s in near[1:]:
        guarded(
            both(both(u[3], s[3]), lower(u, s)),
            lambda u=u, s=s: signal(token.at[me], me, u, s),
        )
    for epoch in range(n_epoch - 1):
        pl.when(epoch < me)(lambda epoch=epoch: to_epoch(token.at[me], epoch))

    def slot_of(sender, receiver):
        return sender - (sender > receiver).astype(jnp.int32)

    def lanes_of(s):
        if n_band == 2:
            start = (1 - band) * (width - LANES)
            return pl.ds(pl.multiple_of(start, LANES), LANES)
        return slice(0, LANES) if s[1] == 0 else slice(width - LANES, width)

    def copy(source, dest, sent, received, to):
        return pltpu.make_async_remote_copy(
            src_ref=source,
            dst_ref=dest,
            send_sem=sent,
            recv_sem=received,
            device_id=to,
            device_id_type=MESH,
        )

    n_up, n_side = len(ups), len(sides)
    images = []
    for u, s in near:
        i = 0 if u is none else 1 + ups.index(u)
        j = 0 if s is none else 1 + sides.index(s)
        images.append((u, s, i * (1 + n_side) + j))
    n_image = (1 + n_up) * (1 + n_side)
    CODE, COEF, OFFS, INDX = n_image, n_image + 1, n_image + 2, n_image + 3

    def image(epoch, u, s, kind, sender, at=None):
        source_at = epoch if at is None else at
        if u is none and s is none:
            source, dest = chosen.at[source_at], centre.at[sender]
        elif s is none:
            source, dest = chosen_edge.at[u[1], source_at], vertical.at[u[2], sender]
        elif u is none:
            source, dest = chosen.at[source_at, :, lanes_of(s)], lateral.at[s[2], sender]
        else:
            source = chosen_edge.at[u[1], source_at, :, lanes_of(s)]
            dest = corner.at[u[2], s[2], sender]
        return copy(
            source, dest, send_sem.at[kind], recv_sem.at[slot_of(sender, epoch), kind], device(epoch, u, s)
        )

    def arriving(epoch, u, s, kind):
        if u is none and s is none:
            dest = centre.at[epoch]
        elif s is none:
            dest = vertical.at[u[2], epoch]
        elif u is none:
            dest = lateral.at[s[2], epoch]
        else:
            dest = corner.at[u[2], s[2], epoch]
        return copy(dest, dest, send_sem.at[kind], recv_sem.at[slot_of(epoch, me), kind], device(epoch, u, s))

    def landing(links, place, size):
        if size == 2:
            return [(k[0], k[1], 1 - place, None, None) for k in links]
        return [(k[0], k[1], k[2], k[4], k[3]) for k in links]

    ups_in = landing(ups, strip, n_strip)
    sides_in = landing(sides, band, n_band)
    images_in = []
    for u, s, kind in images:
        a = none if u is none else ups_in[ups.index(u)]
        b = none if s is none else sides_in[sides.index(s)]
        images_in.append((a, b, kind))

    def send_image(epoch):
        for u, s, kind in images:
            guarded(
                both(u[3], s[3]), lambda u=u, s=s, kind=kind: image(epoch, u, s, kind, me).start()
            )

    def wait_image(epoch):
        for u, s, kind in images_in:
            guarded(
                both(u[3], s[3]), lambda u=u, s=s, kind=kind: arriving(epoch, u, s, kind).wait_recv()
            )

    def small(epoch, sender):
        return [
            copy(held, into.at[sender], send_sem.at[kind], recv_sem.at[slot_of(sender, epoch), kind], device(epoch, none, none))
            for held, into, kind in (
                (offsets_hbm, offsets_in, OFFS),
                (basis_index_hbm, basis_index_in, INDX),
            )
        ]

    def coefficient_tile(epoch, sender):
        return copy(
            coefs.at[epoch], coefs_in.at[sender], send_sem.at[COEF], recv_sem.at[slot_of(sender, epoch), COEF],
            device(epoch, none, none),
        )

    def coded(epoch, sender):
        return copy(
            code.at[epoch], code_in.at[sender], send_sem.at[CODE], recv_sem.at[slot_of(sender, epoch), CODE],
            device(epoch, none, none),
        )

    def own_piece(u, s, kind, incoming):
        if s is none:
            source, dest = own_edge.at[0 if incoming else u[1]], own_vertical.at[u[2]]
        elif u is none:
            source, dest = template.at[:, :, lanes_of(s)], own_lateral.at[s[2]]
        else:
            source = own_edge.at[0 if incoming else u[1], :, :, lanes_of(s)]
            dest = own_corner.at[u[2], s[2]]
        if incoming:
            source = dest
        return copy(source, dest, own_send.at[kind], own_recv.at[kind], device(me, u, s))

    def send_small(epoch):
        for one in small(epoch, me):
            one.start()

    for epoch in range(n_epoch - 1):
        pl.when(epoch < me)(lambda epoch=epoch: send_small(epoch))

    loads[0].wait()
    loads[1].wait()

    def rim(wide, which):
        low, high = wide[:EDGE_ROWS], wide[height - EDGE_ROWS :]
        if n_strip == 2:
            return jnp.where(strip == 0, high, low)
        return low if which == 0 else high

    for epoch in range(n_epoch):
        tile = intersection[epoch * exp_dev + me] - me * tile_dev
        picked = template[jnp.clip(tile, 0, tile_dev - 1)]
        chosen[epoch] = picked
        wide = picked.astype(f32)
        for which in range(n_up):
            chosen_edge[which, epoch] = rim(wide, which).astype(bf16)
    loads[5].wait()
    for exposure in range(exp_dev):
        coefs[exposure] = jnp.zeros((8, LANES), f32)
        for p in range(n_poly):
            coefs[exposure, p : p + 1, 0:n_sel] = coefficients[p, exposure : exposure + 1, :]

    def send_early(epoch):
        coefficient_tile(epoch, me).start()
        send_image(epoch)

    for epoch in range(n_epoch - 1):
        pl.when(epoch < me)(lambda epoch=epoch: send_early(epoch))
    loads[2].wait()
    loads[3].wait()
    loads[4].wait()
    for epoch in range(n_epoch):
        share = bad_mask[epoch].astype(f32) / variance[epoch]
        weight[epoch] = share
        code[epoch] = encode(science[epoch], share)
    for epoch in range(n_epoch - 1):
        pl.when(epoch < me)(lambda epoch=epoch: coded(epoch, me).start())

    for t in range(tile_dev):
        wide = template[t].astype(f32)
        for which in range(n_up):
            own_edge[which, t] = rim(wide, which).astype(bf16)
    for u, s, kind in images[1:]:
        guarded(
            both(both(u[3], s[3]), lower(u, s)),
            lambda u=u, s=s, kind=kind: own_piece(u, s, kind, False).start(),
        )

    def clear(ref):
        ref[...] = jnp.zeros(ref.shape, ref.dtype)

    def clear_up(slot):
        clear(vertical.at[slot])
        clear(own_vertical.at[slot])

    def clear_side(slot):
        clear(lateral.at[slot])
        clear(own_lateral.at[slot])

    def clear_corner(slot, at):
        clear(corner.at[slot, at])
        clear(own_corner.at[slot, at])

    if n_strip == 1:
        clear(vertical)
        clear(own_vertical)
        clear(corner)
        clear(own_corner)
    elif n_strip == 2:
        clear_up(strip)
        for at in range(2):
            clear_corner(strip, at)
    else:
        for slot, edge in ((0, strip == 0), (1, strip == n_strip - 1)):

            @pl.when(edge)
            def _(slot=slot):
                clear_up(slot)
                for at in range(2):
                    clear_corner(slot, at)

    if n_band == 1:
        clear(lateral)
        clear(own_lateral)
        if n_strip > 1:
            clear(corner)
            clear(own_corner)
    elif n_band == 2:
        clear_side(band)
        if n_strip == 2:
            clear_corner(1 - strip, band)
        elif n_strip > 2:
            for slot, held in ((0, strip > 0), (1, strip < n_strip - 1)):
                pl.when(held)(lambda slot=slot: clear_corner(slot, band))
    else:
        for slot, edge in ((0, band == 0), (1, band == n_band - 1)):

            @pl.when(edge)
            def _(slot=slot):
                clear_side(slot)
                for at in range(2):
                    clear_corner(at, slot)

    slab[:, :, height + 2 * EDGE_ROWS :, :] = jnp.zeros(
        (slab.shape[0], slab.shape[1], 8, LANES), f32
    )

    lane = lax.broadcasted_iota(jnp.int32, (8, LANES), 1)
    sub = lax.broadcasted_iota(jnp.int32, (8, LANES), 0)
    n_pairs = (ks + 1) // 2
    n_tiles = n_pairs * SLOT // LANES
    later = jnp.bitwise_and(lane, 7) >= sub

    def mix_of(some, indices):
        parts = []
        for j in range(n_sel):
            column = jnp.broadcast_to(some[:, j : j + 1], (8, LANES))
            parts.append(jnp.where(lane == indices(j), column, 0.0))
        while len(parts) > 1:
            parts = [
                parts[i] + parts[i + 1] if i + 1 < len(parts) else parts[i]
                for i in range(0, len(parts), 2)
            ]
        mix = jnp.where(sub < n_poly, parts[0], 0.0)
        mix = mix + pltpu.roll(mix, half, 1)
        high = mix.astype(bf16).astype(f32)
        return high, mix - high

    def mixed(pairs):
        rows = jnp.concatenate([p[0] for p in pairs] + [p[1] for p in pairs], axis=0)
        out = lax.dot_general(
            rows.astype(bf16), table[...], (((1,), (1,)), ((), ())), preferred_element_type=f32
        )
        size = 8 * len(pairs)
        return (out[:size] + out[size:]).astype(bf16).astype(f32)

    def spread(row, into):
        for p in range(0, n_poly, 2):
            for t in range(n_tiles):
                halves = []
                for h in range(2):
                    at = row * 8 + p + h
                    wide = jnp.broadcast_to(
                        kernels[at : at + 1, t * LANES : (t + 1) * LANES], (8, LANES)
                    )
                    close = pltpu.roll(wide, 0, 1, stride=1, stride_axis=0)
                    far = pltpu.roll(wide, 8, 1, stride=1, stride_axis=0)
                    halves.append(jnp.where(later, close, far))
                toeplitz[into, p * 8 : (p + 2) * 8, t * LANES : (t + 1) * LANES] = (
                    jnp.concatenate(halves, axis=0).astype(bf16)
                )

    loads[6].wait()
    pairs = [
        mix_of(
            coefs[exposure],
            lambda j, exposure=exposure: basis_index[exposure, j],
        )
        for exposure in range(exp_dev)
    ]

    loads[7].wait()
    blank = jnp.zeros((8, LANES), f32)

    def taps(b, g):
        if b >= ks or g * 8 >= ks:
            return blank
        here = min(8, ks - g * 8)
        tile = basis[g * 8 : g * 8 + here, b, :]
        if here < 8:
            tile = jnp.concatenate([tile, jnp.zeros((8 - here, n_basis), f32)], axis=0)
        tile = jnp.concatenate([tile, jnp.zeros((8, LANES - n_basis), f32)], axis=1)
        high = tile.astype(bf16).astype(f32)
        return jnp.where(lane < half, high, pltpu.roll(tile - high, half, 1))

    table[...] = jnp.concatenate(
        [
            taps(2 * q + h, g)
            for q in range(n_pairs)
            for g in range(GROUPS)
            for h in range(2)
        ],
        axis=0,
    ).astype(bf16)
    kernels[0 : 8 * exp_dev] = mixed(pairs)
    loads[8].wait()
    for exposure in range(exp_dev):
        spread(exposure, exposure)

    row = lax.broadcasted_iota(jnp.int32, (height, 1), 0) + strip * height
    col = lax.broadcasted_iota(jnp.int32, (1, width), 1) + band * width
    r = (2.0 * row.astype(f32) + 1.0) / (height * n_strip) - 1.0
    c = (2.0 * col.astype(f32) + 1.0) / (width * n_band) - 1.0
    r = jnp.broadcast_to(r, (height, width))
    c = jnp.broadcast_to(c, (height, width))

    span = height + 8 * GROUPS - 8
    at_lane = lax.broadcasted_iota(jnp.int32, (span, LANES), 1)

    def lay(board, middle, up, side, edge, at):
        for rows, body, rims in (
            (0, up(0), (edge(0, 1), edge(0, 0))),
            (EDGE_ROWS, middle, (side(1), side(0))),
            (EDGE_ROWS + height, up(1), (edge(1, 1), edge(1, 0))),
        ):
            wide = body.astype(f32)
            size = wide.shape[0]
            for t in range(n_lane):
                slab[board, t, rows : rows + size, :] = wide[:, t * LANES : (t + 1) * LANES]
            first = lax.broadcasted_iota(jnp.int32, (size, LANES), 1) < half
            slab[board, n_lane, rows : rows + size, :] = jnp.where(
                first, rims[0].astype(f32), rims[1].astype(f32)
            )

    def lay_own(board, tile):
        lay(
            board,
            template[tile],
            lambda v: own_vertical[v, tile],
            lambda s: own_lateral[s, tile],
            lambda v, s: own_corner[v, s, tile],
            tile,
        )

    def lay_other(board, epoch):
        lay(
            board,
            centre[epoch],
            lambda v: vertical[v, epoch],
            lambda s: lateral[s, epoch],
            lambda v, s: corner[v, s, epoch],
            epoch,
        )

    def models(board, factor, down, along):
        views = []
        for h in range(2):
            turned = [
                pltpu.roll(slab[board, t, pl.ds(down, span), :], along - h, 1)
                for t in range(n_lane + 1)
            ]
            views.append(
                jnp.concatenate(
                    [
                        jnp.where(at_lane < along - h, turned[t - 1], turned[t])
                        for t in range(n_lane + 1)
                    ],
                    axis=1,
                )
            )
        tiles = [
            jnp.concatenate(
                [views[0][g * 8 : g * 8 + 8], views[1][g * 8 : g * 8 + 8]], axis=0
            ).astype(bf16)
            for g in range(span // 8)
        ]
        moved = [[tile[:, 2 * q : 2 * q + width] for tile in tiles] for q in range(n_pairs)]
        for block in range(height // 8):
            stacked = jnp.concatenate(
                [moved[q][block + g] for q in range(n_pairs) for g in range(GROUPS)], axis=0
            )
            conv = jnp.dot(factor, stacked, preferred_element_type=f32)
            q = [conv[p * 8 : (p + 1) * 8] for p in range(n_poly)]
            at = slice(block * 8, block * 8 + 8)
            rr, cc = r[at], c[at]
            yield at, q[0] + rr * (q[1] + rr * q[3] + cc * q[4]) + cc * (q[2] + cc * q[5])

    def tile_of(epoch):
        return intersection[epoch * exp_dev + me] - me * tile_dev

    def down_of(shift):
        return EDGE_ROWS - HALF + shift

    def along_of(shift):
        return HALF - shift

    behind = partners - 1 - ahead_of_me

    @pl.when(behind > 0)
    def _():
        pl.semaphore_wait(token.at[me], behind)

    for u, s, kind in images[1:]:
        guarded(
            both(both(u[3], s[3]), jnp.logical_not(lower(u, s))),
            lambda u=u, s=s, kind=kind: own_piece(u, s, kind, False).start(),
        )
    for step in range(1, n_epoch):

        @pl.when(me + step < n_epoch)
        def _(epoch=me + step):
            pl.semaphore_wait(token.at[epoch], partners)
            send_small(epoch)
            send_early(epoch)
            coded(epoch, me).start()

    for u, s, kind in images_in[1:]:
        guarded(both(u[3], s[3]), lambda u=u, s=s, kind=kind: own_piece(u, s, kind, True).wait_recv())

    tile = tile_of(me)
    lay_own(0, jnp.clip(tile, 0, tile_dev - 1))
    for at, model in models(0, toeplitz[me], down_of(offsets[0, me]), along_of(offsets[1, me])):
        left = science[me, at] - model
        residual[me, at] = left
        share = weight[me, at]
        for t in range(tile_dev):
            here = (tile == t).astype(f32)
            numer[t, at] = share * left * here
            denom[t, at] = share * here

    def partner(step):
        return jnp.where(me + step < n_epoch, me + step, n_epoch - 1 - step)

    def process(step):
        epoch = partner(step)
        for one in small(me, epoch) + [coefficient_tile(me, epoch)]:
            one.wait_recv()
        last = exp_dev
        kernels[8 * last : 8 * last + 8] = mixed(
            [
                mix_of(coefs_in[epoch], lambda j: basis_index_in[epoch, me, j])
            ]
        )
        spread(last, last)
        tile = tile_of(epoch)
        lay_own(0, jnp.clip(tile, 0, tile_dev - 1))
        for at, model in models(
            0, toeplitz[last], down_of(offsets_in[epoch, 0, me]), along_of(offsets_in[epoch, 1, me])
        ):
            model_out[epoch, at] = model

        wait_image(epoch)

        lay_other(1, epoch)
        for at, model in models(
            1, toeplitz[epoch], down_of(offsets[0, epoch]), along_of(offsets[1, epoch])
        ):
            residual[epoch, at] = science[epoch, at] - model

    def gather(step):
        epoch = partner(step)
        tile = tile_of(epoch)
        coded(me, epoch).wait_recv()
        seen, share = decode(code_in[epoch])
        value = share * (seen - model_out[epoch])
        for t in range(tile_dev):
            here = (tile == t).astype(f32)
            numer[t] = numer[t] + value * here
            denom[t] = denom[t] + share * here

    if n_epoch <= 4:
        for step in range(1, n_epoch):
            process(step)
        for step in range(1, n_epoch):
            gather(step)
    else:
        lax.fori_loop(1, n_epoch, lambda step, carry: (process(step), carry)[1], 0)
        lax.fori_loop(1, n_epoch, lambda step, carry: (gather(step), carry)[1], 0)

    for t in range(tile_dev):
        coadd[t] = numer[t] / (denom[t] + 1.0)

    for u, s, kind in images[1:]:
        guarded(both(u[3], s[3]), lambda u=u, s=s, kind=kind: own_piece(u, s, kind, False).wait_send())
    if n_epoch > 1:
        rest = pl.ds(0, n_epoch - 1)
        for u, s, kind in images:

            def gone(u=u, s=s, kind=kind):
                if u is none and s is none:
                    source = chosen.at[rest]
                elif s is none:
                    source = chosen_edge.at[u[1], rest]
                elif u is none:
                    source = chosen.at[rest, :, lanes_of(s)]
                else:
                    source = chosen_edge.at[u[1], rest, :, lanes_of(s)]
                copy(source, source, send_sem.at[kind], recv_sem.at[0, kind], device(me, u, s)).wait_send()

            guarded(both(u[3], s[3]), gone)
        for held, kind in (
            (offsets_in, OFFS),
            (basis_index_in, INDX),
            (coefs, COEF),
            (code, CODE),
        ):
            source = held.at[rest]
            copy(
                source, source, send_sem.at[kind], recv_sem.at[0, kind], device(me, none, none)
            ).wait_send()


def leave(residual, coadd, residual_out, coadd_out, sem):
    parts = [
        (held.at[i], out.at[i])
        for held, out in ((residual, residual_out), (coadd, coadd_out))
        for i in range(held.shape[0])
    ]
    copies = [pltpu.make_async_copy(held, out, sem.at[i]) for i, (held, out) in enumerate(parts)]
    for one in copies:
        one.start()
    for one in copies:
        one.wait()


def local(sizes, template, science, variance, bad_mask, intersection, offsets, basis_index, coefficients, basis):
    n_epoch, n_strip, n_band = sizes
    tile_dev, height, width = template.shape
    exp_dev = science.shape[0]
    assert exp_dev == n_epoch
    n_poly = coefficients.shape[2]
    n_sel = basis_index.shape[1]
    ks = basis.shape[1]
    n_pairs = (ks + 1) // 2
    far = pl.BlockSpec(memory_space=pltpu.HBM)
    near = pl.BlockSpec(memory_space=pltpu.VMEM)
    free = pl.BlockSpec(memory_space=pl.ANY)
    bf16, f32 = jnp.bfloat16, jnp.float32
    dma = pltpu.SemaphoreType.DMA
    offsets = offsets.T
    coefficients = coefficients.transpose(2, 0, 1)
    basis = basis.transpose(1, 2, 0)
    n_up, n_side = min(n_strip - 1, 2), min(n_band - 1, 2)
    n_image = (1 + n_up) * (1 + n_side)
    edges = max(n_up, 1)
    rim = EDGE_ROWS
    residual, coadd = pl.pallas_call(
        functools.partial(kernel, sizes),
        out_shape=(
            pltpu.VMEM(science.shape, f32),
            pltpu.VMEM(template.shape, f32),
        ),
        in_specs=[far] * 9,
        out_specs=(near, near),
        scratch_shapes=[
            pltpu.SMEM(intersection.shape, jnp.int32),
            pltpu.SMEM(offsets.shape, jnp.int32),
            pltpu.SMEM((n_epoch,) + offsets.shape, jnp.int32),
            pltpu.SMEM(basis_index.shape, jnp.int32),
            pltpu.SMEM((n_epoch,) + basis_index.shape, jnp.int32),
            pltpu.VMEM(coefficients.shape, f32),
            pltpu.VMEM((n_epoch, 8, LANES), f32),
            pltpu.VMEM(template.shape, bf16),
            pltpu.VMEM(science.shape, f32),
            pltpu.VMEM(science.shape, f32),
            pltpu.VMEM(science.shape, jnp.int32),
            pltpu.VMEM(basis.shape, f32),
            pltpu.VMEM((n_epoch, height, width), bf16),
            pltpu.VMEM((edges, n_epoch, rim, width), bf16),
            pltpu.VMEM((edges, tile_dev, rim, width), bf16),
            pltpu.VMEM((n_epoch, height, width), bf16),
            pltpu.VMEM((2, n_epoch, rim, width), bf16),
            pltpu.VMEM((2, n_epoch, height, LANES), bf16),
            pltpu.VMEM((2, 2, n_epoch, rim, LANES), bf16),
            pltpu.VMEM((2, tile_dev, rim, width), bf16),
            pltpu.VMEM((2, tile_dev, height, LANES), bf16),
            pltpu.VMEM((2, 2, tile_dev, rim, LANES), bf16),
            pltpu.VMEM((exp_dev, 8, LANES), f32),
            pltpu.VMEM((n_pairs * SLOT, LANES), bf16),
            pltpu.VMEM((8 * exp_dev + 8, n_pairs * SLOT), f32),
            pltpu.VMEM((2, width // LANES + 1, 2 * rim + height + 8, LANES), f32),
            pltpu.VMEM((exp_dev + 1, n_poly * 8, n_pairs * SLOT), bf16),
            pltpu.VMEM((exp_dev, height, width), f32),
            pltpu.VMEM((n_epoch, height, width), jnp.int32),
            pltpu.VMEM((n_epoch, height, width), jnp.int32),
            pltpu.VMEM((n_epoch, height, width), f32),
            pltpu.VMEM(template.shape, f32),
            pltpu.VMEM(template.shape, f32),
            dma((9,)),
            dma((n_image + 4,)),
            dma((max(n_epoch - 1, 1), n_image + 4)),
            dma((n_image,)),
            dma((n_image,)),
            pltpu.SemaphoreType.REGULAR((n_epoch,)),
        ],
        compiler_params=pltpu.CompilerParams(
            collective_id=0, has_side_effects=True
        ),
    )(
        intersection, offsets, basis_index, coefficients,
        template, science, variance, bad_mask, basis,
    )
    return pl.pallas_call(
        leave,
        out_shape=(
            jax.ShapeDtypeStruct(science.shape, f32),
            jax.ShapeDtypeStruct(template.shape, f32),
        ),
        in_specs=[near] * 2,
        out_specs=(free, free),
        scratch_shapes=[dma((exp_dev + tile_dev,))],
    )(*(pltpu.with_memory_space_constraint(x, pltpu.VMEM) for x in (residual, coadd)))


def solution(mesh):
    sizes = (mesh.shape["epoch"], mesh.shape["strip"], mesh.shape["band"])
    image = P(("groups", "epoch"), "strip", "band")
    split = ("groups", "epoch")
    in_specs = (
        image, image, image, image, P("groups"),
        P(split, None), P(split, None), P(split, None, None), P(),
    )
    return jax.shard_map(
        functools.partial(local, sizes),
        mesh=mesh,
        in_specs=in_specs,
        out_specs=(image, image),
        check_vma=False,
    )
```

```python
import functools

import jax
import jax.numpy as jnp
from jax import lax
from jax.experimental import pallas as pl
from jax.experimental.pallas import tpu as pltpu
from jax.sharding import PartitionSpec as P

HALF = 9
SHIFT = 4
EDGE_ROWS = 16
LANES = 128
SLOT = 64
GROUPS = 4
SCIENCE_TOP = 6.0
WEIGHT_TOP = 0.5
LEVELS = 65535.0

MESH = pl.DeviceIdType.MESH


def links_of(size, place):
    if size == 1:
        return []
    if size == 2:
        return [(1 - 2 * place, 0, place, None, None)]
    return [
        (-1, 0, 1, place > 0, place < size - 1),
        (1, 1, 0, place < size - 1, place > 0),
    ]


def both(first, second):
    if first is None:
        return second
    if second is None:
        return first
    return jnp.logical_and(first, second)


def guarded(side, body):
    if side is None:
        body()
    else:
        pl.when(side)(body)


def encode(science, weight):
    high = (science + SCIENCE_TOP) * (LEVELS / (2.0 * SCIENCE_TOP)) + 0.5
    low = weight * (LEVELS / WEIGHT_TOP) + 0.5
    high = jnp.clip(high, 0.0, LEVELS).astype(jnp.int32)
    low = jnp.clip(low, 0.0, LEVELS).astype(jnp.int32)
    return jnp.bitwise_or(jnp.left_shift(high, 16), low)


def decode(code):
    high = lax.shift_right_logical(code, jnp.full(code.shape, 16, jnp.int32))
    low = jnp.bitwise_and(code, 65535)
    science = high.astype(jnp.float32) * (2.0 * SCIENCE_TOP / LEVELS) - SCIENCE_TOP
    return science, low.astype(jnp.float32) * (WEIGHT_TOP / LEVELS)


def kernel(
    sizes,
    intersection_hbm,
    offsets_hbm,
    basis_index_hbm,
    coefficients_hbm,
    template_hbm,
    science_hbm,
    variance_hbm,
    bad_mask_hbm,
    basis_hbm,
    residual,
    coadd,
    intersection,
    offsets,
    offsets_in,
    basis_index,
    basis_index_in,
    coefficients,
    coefs_in,
    template,
    science,
    variance,
    bad_mask,
    basis,
    chosen,
    chosen_edge,
    own_edge,
    centre,
    vertical,
    lateral,
    corner,
    own_vertical,
    own_lateral,
    own_corner,
    coefs,
    table,
    kernels,
    slab,
    toeplitz,
    weight,
    code,
    code_in,
    model_out,
    numer,
    denom,
    local_sem,
    send_sem,
    recv_sem,
    own_send,
    own_recv,
    token,
):
    n_epoch, n_strip, n_band = sizes
    tile_dev, height, width = template.shape
    exp_dev = science.shape[0]
    n_poly, _, n_sel = coefficients.shape
    ks, _, n_basis = basis.shape
    n_lane = width // LANES
    half = LANES // 2
    f32, bf16 = jnp.float32, jnp.bfloat16
    group = lax.axis_index("groups")
    me = lax.axis_index("epoch")
    strip = lax.axis_index("strip")
    band = lax.axis_index("band")

    ups = links_of(n_strip, strip)
    sides = links_of(n_band, band)
    none = (0, None, None, None, None)
    near = [(u, s) for u in [none] + ups for s in [none] + sides]
    column = [(u, none) for u in [none] + ups]

    def device(epoch, u, s):
        return (group, epoch, strip + u[0], band + s[0])

    loads = [
        pltpu.make_async_copy(held, here, local_sem.at[i])
        for i, (held, here) in enumerate(
            (
                (intersection_hbm, intersection),
                (template_hbm, template),
                (variance_hbm, variance),
                (bad_mask_hbm, bad_mask),
                (science_hbm, science),
                (coefficients_hbm, coefficients),
                (basis_index_hbm, basis_index),
                (basis_hbm, basis),
                (offsets_hbm, offsets),
            )
        )
    ]
    for load in loads:
        load.start()

    def count(size, place):
        if size < 3:
            return size
        return 1 + jnp.minimum(place, 1) + jnp.minimum(size - 1 - place, 1)

    def before(size, place):
        return place if size < 3 else jnp.minimum(place, 1)

    across = count(n_band, band)
    partners = count(n_strip, strip)
    ahead_of_me = before(n_strip, strip) * across + before(n_band, band)

    def lower(u, s):
        if u is not none:
            return strip + u[0] < strip
        return band + s[0] < band

    barrier = pltpu.get_barrier_semaphore()

    def signal(sem, epoch, u, s):
        pl.semaphore_signal(sem, inc=1, device_id=device(epoch, u, s), device_id_type=MESH)

    def to_epoch(sem, epoch):
        for u, s in column:
            guarded(u[3], lambda u=u, s=s: signal(sem, epoch, u, s))

    for u, s in near[1:]:
        guarded(
            both(both(u[3], s[3]), jnp.logical_not(lower(u, s))),
            lambda u=u, s=s: signal(barrier, me, u, s),
        )
    for step in range(1, n_epoch):
        pl.when(me + step < n_epoch)(lambda step=step: to_epoch(barrier, me + step))
    met = partners * me + ahead_of_me

    @pl.when(met > 0)
    def _():
        pl.semaphore_wait(barrier, met)

    for u, s in near[1:]:
        guarded(
            both(both(u[3], s[3]), lower(u, s)),
            lambda u=u, s=s: signal(token.at[me], me, u, s),
        )
    for epoch in range(n_epoch - 1):
        pl.when(epoch < me)(lambda epoch=epoch: to_epoch(token.at[me], epoch))

    def slot_of(sender, receiver):
        return sender - (sender > receiver).astype(jnp.int32)

    def lanes_of(s):
        if n_band == 2:
            start = (1 - band) * (width - LANES)
            return pl.ds(pl.multiple_of(start, LANES), LANES)
        return slice(0, LANES) if s[1] == 0 else slice(width - LANES, width)

    def copy(source, dest, sent, received, to):
        return pltpu.make_async_remote_copy(
            src_ref=source,
            dst_ref=dest,
            send_sem=sent,
            recv_sem=received,
            device_id=to,
            device_id_type=MESH,
        )

    n_up, n_side = len(ups), len(sides)
    images = []
    for u, s in near:
        i = 0 if u is none else 1 + ups.index(u)
        j = 0 if s is none else 1 + sides.index(s)
        images.append((u, s, i * (1 + n_side) + j))
    n_image = (1 + n_up) * (1 + n_side)
    CODE, COEF, OFFS, INDX = n_image, n_image + 1, n_image + 2, n_image + 3

    def landing(links, place, size):
        if size == 2:
            return [(k[0], k[1], 1 - place, None, None) for k in links]
        return [(k[0], k[1], k[2], k[4], k[3]) for k in links]

    ups_in = landing(ups, strip, n_strip)
    sides_in = landing(sides, band, n_band)
    images_in = []
    for u, s, kind in images:
        a = none if u is none else ups_in[ups.index(u)]
        b = none if s is none else sides_in[sides.index(s)]
        images_in.append((a, b, kind))

    def landed(epoch, u, s):
        if u is none and s is none:
            return centre.at[epoch]
        if s is none:
            return vertical.at[u[2], epoch]
        if u is none:
            return lateral.at[s[2], epoch]
        return corner.at[u[2], s[2], epoch]

    def send_image(epoch):
        for u, s, kind in images:
            if s is not none:
                continue
            source = chosen.at[epoch] if u is none else chosen_edge.at[u[1], epoch]
            one = copy(
                source, landed(me, u, s), send_sem.at[kind], recv_sem.at[slot_of(me, epoch), kind],
                device(epoch, u, s),
            )
            guarded(u[3], one.start)

    def wait_pieces(epoch, side):
        for u, s, kind in images_in:
            if (s is not none) != side:
                continue
            here = landed(epoch, u, s)
            one = copy(
                here, here, send_sem.at[kind], recv_sem.at[slot_of(epoch, me), kind], device(epoch, none, none)
            )
            guarded(both(u[3], s[3]), one.wait_recv)

    def forward(epoch):
        for (a, _, kind), (_, s, _) in zip(images_in, images):
            if s is none:
                continue
            source = centre.at[epoch, :, lanes_of(s)]
            if a is not none:
                source = vertical.at[a[2], epoch, :, lanes_of(s)]
            one = copy(
                source, landed(epoch, a, s), send_sem.at[kind], recv_sem.at[slot_of(epoch, me), kind],
                device(me, none, s),
            )
            guarded(both(a[3], s[3]), one.start)

    def small(epoch, sender):
        return [
            copy(held, into.at[sender], send_sem.at[kind], recv_sem.at[slot_of(sender, epoch), kind], device(epoch, none, none))
            for held, into, kind in (
                (offsets_hbm, offsets_in, OFFS),
                (basis_index_hbm, basis_index_in, INDX),
            )
        ]

    def coefficient_tile(epoch, sender):
        return copy(
            coefs.at[epoch], coefs_in.at[sender], send_sem.at[COEF], recv_sem.at[slot_of(sender, epoch), COEF],
            device(epoch, none, none),
        )

    def coded(epoch, sender):
        return copy(
            code.at[epoch], code_in.at[sender], send_sem.at[CODE], recv_sem.at[slot_of(sender, epoch), CODE],
            device(epoch, none, none),
        )

    def own_piece(u, s, kind, incoming):
        if s is none:
            source, dest = own_edge.at[0 if incoming else u[1]], own_vertical.at[u[2]]
        elif u is none:
            source, dest = template.at[:, :, lanes_of(s)], own_lateral.at[s[2]]
        else:
            source = own_edge.at[0 if incoming else u[1], :, :, lanes_of(s)]
            dest = own_corner.at[u[2], s[2]]
        if incoming:
            source = dest
        return copy(source, dest, own_send.at[kind], own_recv.at[kind], device(me, u, s))

    def send_small(epoch):
        for one in small(epoch, me):
            one.start()

    for epoch in range(n_epoch - 1):
        pl.when(epoch < me)(lambda epoch=epoch: send_small(epoch))

    loads[0].wait()
    loads[1].wait()

    def rim(wide, which):
        low, high = wide[:EDGE_ROWS], wide[height - EDGE_ROWS :]
        if n_strip == 2:
            return jnp.where(strip == 0, high, low)
        return low if which == 0 else high

    for epoch in range(n_epoch):
        tile = intersection[epoch * exp_dev + me] - me * tile_dev
        picked = template[jnp.clip(tile, 0, tile_dev - 1)]
        chosen[epoch] = picked
        wide = picked.astype(f32)
        for which in range(n_up):
            chosen_edge[which, epoch] = rim(wide, which).astype(bf16)
    loads[5].wait()
    for exposure in range(exp_dev):
        coefs[exposure] = jnp.zeros((8, LANES), f32)
        for p in range(n_poly):
            coefs[exposure, p : p + 1, 0:n_sel] = coefficients[p, exposure : exposure + 1, :]

    def send_early(epoch):
        coefficient_tile(epoch, me).start()
        send_image(epoch)

    for epoch in range(n_epoch - 1):
        pl.when(epoch < me)(lambda epoch=epoch: send_early(epoch))
    loads[2].wait()
    loads[3].wait()
    loads[4].wait()
    for epoch in range(n_epoch):
        share = bad_mask[epoch].astype(f32) / variance[epoch]
        weight[epoch] = share
        code[epoch] = encode(science[epoch], share)
    for epoch in range(n_epoch - 1):
        pl.when(epoch < me)(lambda epoch=epoch: coded(epoch, me).start())

    for t in range(tile_dev):
        wide = template[t].astype(f32)
        for which in range(n_up):
            own_edge[which, t] = rim(wide, which).astype(bf16)
    for u, s, kind in images[1:]:
        guarded(
            both(both(u[3], s[3]), lower(u, s)),
            lambda u=u, s=s, kind=kind: own_piece(u, s, kind, False).start(),
        )

    def clear(ref):
        ref[...] = jnp.zeros(ref.shape, ref.dtype)

    def clear_up(slot):
        clear(vertical.at[slot])
        clear(own_vertical.at[slot])

    def clear_side(slot):
        clear(lateral.at[slot])
        clear(own_lateral.at[slot])

    def clear_corner(slot, at):
        clear(corner.at[slot, at])
        clear(own_corner.at[slot, at])

    if n_strip == 1:
        clear(vertical)
        clear(own_vertical)
        clear(corner)
        clear(own_corner)
    elif n_strip == 2:
        clear_up(strip)
        for at in range(2):
            clear_corner(strip, at)
    else:
        for slot, edge in ((0, strip == 0), (1, strip == n_strip - 1)):

            @pl.when(edge)
            def _(slot=slot):
                clear_up(slot)
                for at in range(2):
                    clear_corner(slot, at)

    if n_band == 1:
        clear(lateral)
        clear(own_lateral)
        if n_strip > 1:
            clear(corner)
            clear(own_corner)
    elif n_band == 2:
        clear_side(band)
        if n_strip == 2:
            clear_corner(1 - strip, band)
        elif n_strip > 2:
            for slot, held in ((0, strip > 0), (1, strip < n_strip - 1)):
                pl.when(held)(lambda slot=slot: clear_corner(slot, band))
    else:
        for slot, edge in ((0, band == 0), (1, band == n_band - 1)):

            @pl.when(edge)
            def _(slot=slot):
                clear_side(slot)
                for at in range(2):
                    clear_corner(at, slot)

    slab[:, :, height + 2 * EDGE_ROWS :, :] = jnp.zeros(
        (slab.shape[0], slab.shape[1], 8, LANES), f32
    )

    lane = lax.broadcasted_iota(jnp.int32, (8, LANES), 1)
    sub = lax.broadcasted_iota(jnp.int32, (8, LANES), 0)
    n_pairs = (ks + 1) // 2
    n_tiles = n_pairs * SLOT // LANES
    later = jnp.bitwise_and(lane, 7) >= sub

    def mix_of(some, indices):
        parts = []
        for j in range(n_sel):
            column = jnp.broadcast_to(some[:, j : j + 1], (8, LANES))
            parts.append(jnp.where(lane == indices(j), column, 0.0))
        while len(parts) > 1:
            parts = [
                parts[i] + parts[i + 1] if i + 1 < len(parts) else parts[i]
                for i in range(0, len(parts), 2)
            ]
        mix = jnp.where(sub < n_poly, parts[0], 0.0)
        mix = mix + pltpu.roll(mix, half, 1)
        high = mix.astype(bf16).astype(f32)
        return high, mix - high

    def mixed(pairs):
        rows = jnp.concatenate([p[0] for p in pairs] + [p[1] for p in pairs], axis=0)
        out = lax.dot_general(
            rows.astype(bf16), table[...], (((1,), (1,)), ((), ())), preferred_element_type=f32
        )
        size = 8 * len(pairs)
        return (out[:size] + out[size:]).astype(bf16).astype(f32)

    def spread(row, into):
        for p in range(0, n_poly, 2):
            for t in range(n_tiles):
                halves = []
                for h in range(2):
                    at = row * 8 + p + h
                    wide = jnp.broadcast_to(
                        kernels[at : at + 1, t * LANES : (t + 1) * LANES], (8, LANES)
                    )
                    close = pltpu.roll(wide, 0, 1, stride=1, stride_axis=0)
                    far = pltpu.roll(wide, 8, 1, stride=1, stride_axis=0)
                    halves.append(jnp.where(later, close, far))
                toeplitz[into, p * 8 : (p + 2) * 8, t * LANES : (t + 1) * LANES] = (
                    jnp.concatenate(halves, axis=0).astype(bf16)
                )

    loads[6].wait()
    pairs = [
        mix_of(
            coefs[exposure],
            lambda j, exposure=exposure: basis_index[exposure, j],
        )
        for exposure in range(exp_dev)
    ]

    loads[7].wait()
    blank = jnp.zeros((8, LANES), f32)

    def taps(b, g):
        if b >= ks or g * 8 >= ks:
            return blank
        here = min(8, ks - g * 8)
        tile = basis[g * 8 : g * 8 + here, b, :]
        if here < 8:
            tile = jnp.concatenate([tile, jnp.zeros((8 - here, n_basis), f32)], axis=0)
        tile = jnp.concatenate([tile, jnp.zeros((8, LANES - n_basis), f32)], axis=1)
        high = tile.astype(bf16).astype(f32)
        return jnp.where(lane < half, high, pltpu.roll(tile - high, half, 1))

    table[...] = jnp.concatenate(
        [
            taps(2 * q + h, g)
            for q in range(n_pairs)
            for g in range(GROUPS)
            for h in range(2)
        ],
        axis=0,
    ).astype(bf16)
    kernels[0 : 8 * exp_dev] = mixed(pairs)
    loads[8].wait()
    for exposure in range(exp_dev):
        spread(exposure, exposure)

    row = lax.broadcasted_iota(jnp.int32, (height, 1), 0) + strip * height
    col = lax.broadcasted_iota(jnp.int32, (1, width), 1) + band * width
    r = (2.0 * row.astype(f32) + 1.0) / (height * n_strip) - 1.0
    c = (2.0 * col.astype(f32) + 1.0) / (width * n_band) - 1.0
    r = jnp.broadcast_to(r, (height, width))
    c = jnp.broadcast_to(c, (height, width))

    span = height + 8 * GROUPS - 8
    at_lane = lax.broadcasted_iota(jnp.int32, (span, LANES), 1)

    def lay(board, middle, up, side, edge, at):
        for rows, body, rims in (
            (0, up(0), (edge(0, 1), edge(0, 0))),
            (EDGE_ROWS, middle, (side(1), side(0))),
            (EDGE_ROWS + height, up(1), (edge(1, 1), edge(1, 0))),
        ):
            wide = body.astype(f32)
            size = wide.shape[0]
            for t in range(n_lane):
                slab[board, t, rows : rows + size, :] = wide[:, t * LANES : (t + 1) * LANES]
            first = lax.broadcasted_iota(jnp.int32, (size, LANES), 1) < half
            slab[board, n_lane, rows : rows + size, :] = jnp.where(
                first, rims[0].astype(f32), rims[1].astype(f32)
            )

    def lay_own(board, tile):
        lay(
            board,
            template[tile],
            lambda v: own_vertical[v, tile],
            lambda s: own_lateral[s, tile],
            lambda v, s: own_corner[v, s, tile],
            tile,
        )

    def lay_other(board, epoch):
        lay(
            board,
            centre[epoch],
            lambda v: vertical[v, epoch],
            lambda s: lateral[s, epoch],
            lambda v, s: corner[v, s, epoch],
            epoch,
        )

    def models(board, factor, down, along):
        views = []
        for h in range(2):
            turned = [
                pltpu.roll(slab[board, t, pl.ds(down, span), :], along - h, 1)
                for t in range(n_lane + 1)
            ]
            views.append(
                jnp.concatenate(
                    [
                        jnp.where(at_lane < along - h, turned[t - 1], turned[t])
                        for t in range(n_lane + 1)
                    ],
                    axis=1,
                )
            )
        tiles = [
            jnp.concatenate(
                [views[0][g * 8 : g * 8 + 8], views[1][g * 8 : g * 8 + 8]], axis=0
            ).astype(bf16)
            for g in range(span // 8)
        ]
        moved = [[tile[:, 2 * q : 2 * q + width] for tile in tiles] for q in range(n_pairs)]
        for block in range(height // 8):
            stacked = jnp.concatenate(
                [moved[q][block + g] for q in range(n_pairs) for g in range(GROUPS)], axis=0
            )
            conv = jnp.dot(factor, stacked, preferred_element_type=f32)
            q = [conv[p * 8 : (p + 1) * 8] for p in range(n_poly)]
            at = slice(block * 8, block * 8 + 8)
            rr, cc = r[at], c[at]
            yield at, q[0] + rr * (q[1] + rr * q[3] + cc * q[4]) + cc * (q[2] + cc * q[5])

    def tile_of(epoch):
        return intersection[epoch * exp_dev + me] - me * tile_dev

    def down_of(shift):
        return EDGE_ROWS - HALF + shift

    def along_of(shift):
        return HALF - shift

    behind = partners * across - 1 - ahead_of_me

    @pl.when(behind > 0)
    def _():
        pl.semaphore_wait(token.at[me], behind)

    for u, s, kind in images[1:]:
        guarded(
            both(both(u[3], s[3]), jnp.logical_not(lower(u, s))),
            lambda u=u, s=s, kind=kind: own_piece(u, s, kind, False).start(),
        )
    for step in range(1, n_epoch):

        @pl.when(me + step < n_epoch)
        def _(epoch=me + step):
            pl.semaphore_wait(token.at[epoch], partners)
            send_small(epoch)
            send_early(epoch)
            coded(epoch, me).start()

    def own_board(tile):
        return jnp.clip(tile, 0, tile_dev - 1)

    def partner(step):
        return jnp.where(me + step < n_epoch, me + step, n_epoch - 1 - step)

    def wait_small(step):
        epoch = partner(step)
        for one in small(me, epoch) + [coefficient_tile(me, epoch)]:
            one.wait_recv()

    def wait_image(step):
        wait_pieces(partner(step), False)
        forward(partner(step))

    def wait_side(step):
        wait_pieces(partner(step), True)

    def theirs(step):
        epoch = partner(step)
        last = exp_dev
        kernels[8 * last : 8 * last + 8] = mixed(
            [mix_of(coefs_in[epoch], lambda j: basis_index_in[epoch, me, j])]
        )
        spread(last, last)
        for at, model in models(
            own_board(tile_of(epoch)),
            toeplitz[last],
            down_of(offsets_in[epoch, 0, me]),
            along_of(offsets_in[epoch, 1, me]),
        ):
            model_out[epoch, at] = model

    def ours(step):
        epoch = partner(step)
        lay_other(tile_dev, epoch)
        for at, model in models(
            tile_dev, toeplitz[epoch], down_of(offsets[0, epoch]), along_of(offsets[1, epoch])
        ):
            residual[epoch, at] = science[epoch, at] - model

    def gather(step):
        epoch = partner(step)
        tile = tile_of(epoch)
        coded(me, epoch).wait_recv()
        seen, share = decode(code_in[epoch])
        value = share * (seen - model_out[epoch])
        for t in range(tile_dev):
            here = (tile == t).astype(f32)
            numer[t] = numer[t] + value * here
            denom[t] = denom[t] + share * here

    def first():
        tile = tile_of(me)
        for at, model in models(own_board(tile), toeplitz[me], down_of(offsets[0, me]), along_of(offsets[1, me])):
            left = science[me, at] - model
            residual[me, at] = left
            share = weight[me, at]
            for t in range(tile_dev):
                here = (tile == t).astype(f32)
                numer[t, at] = share * left * here
                denom[t, at] = share * here

    for u, s, kind in images_in[1:]:
        guarded(both(u[3], s[3]), lambda u=u, s=s, kind=kind: own_piece(u, s, kind, True).wait_recv())

    if n_epoch <= 4:
        if n_epoch > 1:
            wait_small(1)
        for t in range(tile_dev):
            lay_own(t, t)
        if n_epoch > 1:
            theirs(1)
        first()
        for step in range(1, n_epoch):
            wait_image(step)
            if step + 1 < n_epoch:
                wait_small(step + 1)
            wait_side(step)
            ours(step)
            if step + 1 < n_epoch:
                theirs(step + 1)
        for step in range(1, n_epoch):
            gather(step)
    else:
        for t in range(tile_dev):
            lay_own(t, t)
        first()

        def body(step, carry):
            wait_small(step)
            theirs(step)
            wait_image(step)
            wait_side(step)
            ours(step)
            return carry

        lax.fori_loop(1, n_epoch, body, 0)
        lax.fori_loop(1, n_epoch, lambda step, carry: (gather(step), carry)[1], 0)

    for t in range(tile_dev):
        coadd[t] = numer[t] / (denom[t] + 1.0)

    for u, s, kind in images[1:]:
        guarded(both(u[3], s[3]), lambda u=u, s=s, kind=kind: own_piece(u, s, kind, False).wait_send())
    if n_epoch > 1:
        rest = pl.ds(0, n_epoch - 1)
        for u, s, kind in images:

            def gone(u=u, s=s, kind=kind):
                if u is none and s is none:
                    source = centre.at[rest]
                elif s is none:
                    source = vertical.at[0, rest]
                elif u is none:
                    source = lateral.at[0, rest]
                else:
                    source = corner.at[0, 0, rest]
                copy(source, source, send_sem.at[kind], recv_sem.at[0, kind], device(me, u, s)).wait_send()

            guarded(both(u[3], s[3]), gone)
        for held, kind in (
            (offsets_in, OFFS),
            (basis_index_in, INDX),
            (coefs, COEF),
            (code, CODE),
        ):
            source = held.at[rest]
            copy(
                source, source, send_sem.at[kind], recv_sem.at[0, kind], device(me, none, none)
            ).wait_send()


def leave(residual, coadd, residual_out, coadd_out, sem):
    parts = [
        (held.at[i], out.at[i])
        for held, out in ((residual, residual_out), (coadd, coadd_out))
        for i in range(held.shape[0])
    ]
    copies = [pltpu.make_async_copy(held, out, sem.at[i]) for i, (held, out) in enumerate(parts)]
    for one in copies:
        one.start()
    for one in copies:
        one.wait()


def local(sizes, template, science, variance, bad_mask, intersection, offsets, basis_index, coefficients, basis):
    n_epoch, n_strip, n_band = sizes
    tile_dev, height, width = template.shape
    exp_dev = science.shape[0]
    assert exp_dev == n_epoch
    n_poly = coefficients.shape[2]
    n_sel = basis_index.shape[1]
    ks = basis.shape[1]
    n_pairs = (ks + 1) // 2
    far = pl.BlockSpec(memory_space=pltpu.HBM)
    near = pl.BlockSpec(memory_space=pltpu.VMEM)
    free = pl.BlockSpec(memory_space=pl.ANY)
    bf16, f32 = jnp.bfloat16, jnp.float32
    dma = pltpu.SemaphoreType.DMA
    offsets = offsets.T
    coefficients = coefficients.transpose(2, 0, 1)
    basis = basis.transpose(1, 2, 0)
    n_up, n_side = min(n_strip - 1, 2), min(n_band - 1, 2)
    n_image = (1 + n_up) * (1 + n_side)
    edges = max(n_up, 1)
    rim = EDGE_ROWS
    residual, coadd = pl.pallas_call(
        functools.partial(kernel, sizes),
        out_shape=(
            pltpu.VMEM(science.shape, f32),
            pltpu.VMEM(template.shape, f32),
        ),
        in_specs=[far] * 9,
        out_specs=(near, near),
        scratch_shapes=[
            pltpu.SMEM(intersection.shape, jnp.int32),
            pltpu.SMEM(offsets.shape, jnp.int32),
            pltpu.SMEM((n_epoch,) + offsets.shape, jnp.int32),
            pltpu.SMEM(basis_index.shape, jnp.int32),
            pltpu.SMEM((n_epoch,) + basis_index.shape, jnp.int32),
            pltpu.VMEM(coefficients.shape, f32),
            pltpu.VMEM((n_epoch, 8, LANES), f32),
            pltpu.VMEM(template.shape, bf16),
            pltpu.VMEM(science.shape, f32),
            pltpu.VMEM(science.shape, f32),
            pltpu.VMEM(science.shape, jnp.int32),
            pltpu.VMEM(basis.shape, f32),
            pltpu.VMEM((n_epoch, height, width), bf16),
            pltpu.VMEM((edges, n_epoch, rim, width), bf16),
            pltpu.VMEM((edges, tile_dev, rim, width), bf16),
            pltpu.VMEM((n_epoch, height, width), bf16),
            pltpu.VMEM((2, n_epoch, rim, width), bf16),
            pltpu.VMEM((2, n_epoch, height, LANES), bf16),
            pltpu.VMEM((2, 2, n_epoch, rim, LANES), bf16),
            pltpu.VMEM((2, tile_dev, rim, width), bf16),
            pltpu.VMEM((2, tile_dev, height, LANES), bf16),
            pltpu.VMEM((2, 2, tile_dev, rim, LANES), bf16),
            pltpu.VMEM((exp_dev, 8, LANES), f32),
            pltpu.VMEM((n_pairs * SLOT, LANES), bf16),
            pltpu.VMEM((8 * exp_dev + 8, n_pairs * SLOT), f32),
            pltpu.VMEM((tile_dev + 1, width // LANES + 1, 2 * rim + height + 8, LANES), f32),
            pltpu.VMEM((exp_dev + 1, n_poly * 8, n_pairs * SLOT), bf16),
            pltpu.VMEM((exp_dev, height, width), f32),
            pltpu.VMEM((n_epoch, height, width), jnp.int32),
            pltpu.VMEM((n_epoch, height, width), jnp.int32),
            pltpu.VMEM((n_epoch, height, width), f32),
            pltpu.VMEM(template.shape, f32),
            pltpu.VMEM(template.shape, f32),
            dma((9,)),
            dma((n_image + 4,)),
            dma((max(n_epoch - 1, 1), n_image + 4)),
            dma((n_image,)),
            dma((n_image,)),
            pltpu.SemaphoreType.REGULAR((n_epoch,)),
        ],
        compiler_params=pltpu.CompilerParams(
            collective_id=0, has_side_effects=True
        ),
    )(
        intersection, offsets, basis_index, coefficients,
        template, science, variance, bad_mask, basis,
    )
    return pl.pallas_call(
        leave,
        out_shape=(
            jax.ShapeDtypeStruct(science.shape, f32),
            jax.ShapeDtypeStruct(template.shape, f32),
        ),
        in_specs=[near] * 2,
        out_specs=(free, free),
        scratch_shapes=[dma((exp_dev + tile_dev,))],
    )(*(pltpu.with_memory_space_constraint(x, pltpu.VMEM) for x in (residual, coadd)))


def solution(mesh):
    sizes = (mesh.shape["epoch"], mesh.shape["strip"], mesh.shape["band"])
    image = P(("groups", "epoch"), "strip", "band")
    split = ("groups", "epoch")
    in_specs = (
        image, image, image, image, P("groups"),
        P(split, None), P(split, None), P(split, None, None), P(),
    )
    return jax.shard_map(
        functools.partial(local, sizes),
        mesh=mesh,
        in_specs=in_specs,
        out_specs=(image, image),
        check_vma=False,
    )
```

```python
import functools

import jax
import jax.numpy as jnp
from jax import lax
from jax.experimental import pallas as pl
from jax.experimental.pallas import tpu as pltpu
from jax.sharding import PartitionSpec as P

HALF = 9
SHIFT = 4
EDGE_ROWS = 16
LANES = 128
SLOT = 64
GROUPS = 4
SCIENCE_TOP = 6.0
WEIGHT_TOP = 0.5
LEVELS = 65535.0

MESH = pl.DeviceIdType.MESH


def links_of(size, place):
    if size == 1:
        return []
    if size == 2:
        return [(1 - 2 * place, 0, place, None, None)]
    return [
        (-1, 0, 1, place > 0, place < size - 1),
        (1, 1, 0, place < size - 1, place > 0),
    ]


def both(first, second):
    if first is None:
        return second
    if second is None:
        return first
    return jnp.logical_and(first, second)


def guarded(side, body):
    if side is None:
        body()
    else:
        pl.when(side)(body)


def encode(science, weight):
    high = (science + SCIENCE_TOP) * (LEVELS / (2.0 * SCIENCE_TOP)) + 0.5
    low = weight * (LEVELS / WEIGHT_TOP) + 0.5
    high = jnp.clip(high, 0.0, LEVELS).astype(jnp.int32)
    low = jnp.clip(low, 0.0, LEVELS).astype(jnp.int32)
    return jnp.bitwise_or(jnp.left_shift(high, 16), low)


def decode(code):
    high = lax.shift_right_logical(code, jnp.full(code.shape, 16, jnp.int32))
    low = jnp.bitwise_and(code, 65535)
    science = high.astype(jnp.float32) * (2.0 * SCIENCE_TOP / LEVELS) - SCIENCE_TOP
    return science, low.astype(jnp.float32) * (WEIGHT_TOP / LEVELS)


def kernel(
    sizes,
    intersection_hbm,
    offsets_hbm,
    basis_index_hbm,
    coefficients_hbm,
    template_hbm,
    science_hbm,
    variance_hbm,
    bad_mask_hbm,
    basis_hbm,
    residual,
    coadd,
    intersection,
    offsets,
    offsets_in,
    basis_index,
    basis_index_in,
    coefficients,
    coefs_in,
    template,
    science,
    variance,
    bad_mask,
    basis,
    chosen,
    chosen_edge,
    own_edge,
    centre,
    vertical,
    lateral,
    corner,
    own_vertical,
    own_lateral,
    own_corner,
    coefs,
    table,
    kernels,
    slab,
    toeplitz,
    weight,
    code,
    code_in,
    model_out,
    model_in,
    numer,
    denom,
    local_sem,
    send_sem,
    recv_sem,
    own_send,
    own_recv,
    token,
):
    n_epoch, n_strip, n_band = sizes
    tile_dev, height, width = template.shape
    exp_dev = science.shape[0]
    n_poly, _, n_sel = coefficients.shape
    ks, _, n_basis = basis.shape
    n_lane = width // LANES
    half = LANES // 2
    f32, bf16 = jnp.float32, jnp.bfloat16
    group = lax.axis_index("groups")
    me = lax.axis_index("epoch")
    strip = lax.axis_index("strip")
    band = lax.axis_index("band")

    ups = links_of(n_strip, strip)
    sides = links_of(n_band, band)
    none = (0, None, None, None, None)
    near = [(u, s) for u in [none] + ups for s in [none] + sides]

    def device(epoch, u, s):
        return (group, epoch, strip + u[0], band + s[0])

    loads = [
        pltpu.make_async_copy(held, here, local_sem.at[i])
        for i, (held, here) in enumerate(
            (
                (intersection_hbm, intersection),
                (template_hbm, template),
                (variance_hbm, variance),
                (bad_mask_hbm, bad_mask),
                (science_hbm, science),
                (coefficients_hbm, coefficients),
                (basis_index_hbm, basis_index),
                (basis_hbm, basis),
                (offsets_hbm, offsets),
            )
        )
    ]
    for load in loads:
        load.start()

    def count(size, place):
        if size < 3:
            return size
        return 1 + jnp.minimum(place, 1) + jnp.minimum(size - 1 - place, 1)

    def before(size, place):
        return place if size < 3 else jnp.minimum(place, 1)

    across = count(n_band, band)
    partners = count(n_strip, strip) * across
    ahead_of_me = before(n_strip, strip) * across + before(n_band, band)

    def lower(u, s):
        if u is not none:
            return strip + u[0] < strip
        return band + s[0] < band

    barrier = pltpu.get_barrier_semaphore()

    def signal(sem, epoch, u, s):
        pl.semaphore_signal(sem, inc=1, device_id=device(epoch, u, s), device_id_type=MESH)

    def to_epoch(sem, epoch):
        for u, s in near:
            guarded(both(u[3], s[3]), lambda u=u, s=s: signal(sem, epoch, u, s))

    for u, s in near[1:]:
        guarded(
            both(both(u[3], s[3]), jnp.logical_not(lower(u, s))),
            lambda u=u, s=s: signal(barrier, me, u, s),
        )
    for step in range(1, n_epoch):
        pl.when(me + step < n_epoch)(lambda step=step: to_epoch(barrier, me + step))
    met = partners * me + ahead_of_me

    @pl.when(met > 0)
    def _():
        pl.semaphore_wait(barrier, met)

    for u, s in near[1:]:
        guarded(
            both(both(u[3], s[3]), lower(u, s)),
            lambda u=u, s=s: signal(token.at[me], me, u, s),
        )
    for epoch in range(n_epoch - 1):
        pl.when(epoch < me)(lambda epoch=epoch: signal(token.at[me], epoch, none, none))

    def slot_of(sender, receiver):
        return sender - (sender > receiver).astype(jnp.int32)

    def lanes_of(s):
        if n_band == 2:
            start = (1 - band) * (width - LANES)
            return pl.ds(pl.multiple_of(start, LANES), LANES)
        return slice(0, LANES) if s[1] == 0 else slice(width - LANES, width)

    def copy(source, dest, sent, received, to):
        return pltpu.make_async_remote_copy(
            src_ref=source,
            dst_ref=dest,
            send_sem=sent,
            recv_sem=received,
            device_id=to,
            device_id_type=MESH,
        )

    n_up, n_side = len(ups), len(sides)
    images = []
    for u, s in near:
        i = 0 if u is none else 1 + ups.index(u)
        j = 0 if s is none else 1 + sides.index(s)
        images.append((u, s, i * (1 + n_side) + j))
    n_image = (1 + n_up) * (1 + n_side)
    CODE, COEF, OFFS, INDX, MODEL = (n_image + i for i in range(5))

    def image(epoch, u, s, kind, sender, at=None):
        source_at = epoch if at is None else at
        if u is none and s is none:
            source, dest = chosen.at[source_at], centre.at[sender]
        elif s is none:
            source, dest = chosen_edge.at[u[1], source_at], vertical.at[u[2], sender]
        elif u is none:
            source, dest = chosen.at[source_at, :, lanes_of(s)], lateral.at[s[2], sender]
        else:
            source = chosen_edge.at[u[1], source_at, :, lanes_of(s)]
            dest = corner.at[u[2], s[2], sender]
        return copy(
            source, dest, send_sem.at[kind], recv_sem.at[slot_of(sender, epoch), kind], device(epoch, u, s)
        )

    def arriving(epoch, u, s, kind):
        if u is none and s is none:
            dest = centre.at[epoch]
        elif s is none:
            dest = vertical.at[u[2], epoch]
        elif u is none:
            dest = lateral.at[s[2], epoch]
        else:
            dest = corner.at[u[2], s[2], epoch]
        return copy(dest, dest, send_sem.at[kind], recv_sem.at[slot_of(epoch, me), kind], device(epoch, u, s))

    def landing(links, place, size):
        if size == 2:
            return [(k[0], k[1], 1 - place, None, None) for k in links]
        return [(k[0], k[1], k[2], k[4], k[3]) for k in links]

    ups_in = landing(ups, strip, n_strip)
    sides_in = landing(sides, band, n_band)
    images_in = []
    for u, s, kind in images:
        a = none if u is none else ups_in[ups.index(u)]
        b = none if s is none else sides_in[sides.index(s)]
        images_in.append((a, b, kind))

    def send_image(epoch):
        for u, s, kind in images:
            guarded(
                both(u[3], s[3]), lambda u=u, s=s, kind=kind: image(epoch, u, s, kind, me).start()
            )

    def wait_image(epoch):
        for u, s, kind in images_in:
            guarded(
                both(u[3], s[3]), lambda u=u, s=s, kind=kind: arriving(epoch, u, s, kind).wait_recv()
            )

    def small(epoch, sender):
        return [
            copy(held, into.at[sender], send_sem.at[kind], recv_sem.at[slot_of(sender, epoch), kind], device(epoch, none, none))
            for held, into, kind in (
                (offsets_hbm, offsets_in, OFFS),
                (basis_index_hbm, basis_index_in, INDX),
            )
        ]

    def coefficient_tile(epoch, sender):
        return copy(
            coefs.at[epoch], coefs_in.at[sender], send_sem.at[COEF], recv_sem.at[slot_of(sender, epoch), COEF],
            device(epoch, none, none),
        )

    def coded(epoch, sender):
        return copy(
            code.at[epoch], code_in.at[sender], send_sem.at[CODE], recv_sem.at[slot_of(sender, epoch), CODE],
            device(epoch, none, none),
        )

    def returned(epoch, sender):
        return copy(
            model_out.at[epoch], model_in.at[sender], send_sem.at[MODEL], recv_sem.at[slot_of(sender, epoch), MODEL],
            device(epoch, none, none),
        )

    def own_piece(u, s, kind, incoming):
        if s is none:
            source, dest = own_edge.at[0 if incoming else u[1]], own_vertical.at[u[2]]
        elif u is none:
            source, dest = template.at[:, :, lanes_of(s)], own_lateral.at[s[2]]
        else:
            source = own_edge.at[0 if incoming else u[1], :, :, lanes_of(s)]
            dest = own_corner.at[u[2], s[2]]
        if incoming:
            source = dest
        return copy(source, dest, own_send.at[kind], own_recv.at[kind], device(me, u, s))

    def send_small(epoch):
        for one in small(epoch, me):
            one.start()

    for epoch in range(n_epoch - 1):
        pl.when(epoch < me)(lambda epoch=epoch: send_small(epoch))

    loads[0].wait()
    loads[1].wait()

    def rim(wide, which):
        low, high = wide[:EDGE_ROWS], wide[height - EDGE_ROWS :]
        if n_strip == 2:
            return jnp.where(strip == 0, high, low)
        return low if which == 0 else high

    for epoch in range(n_epoch):
        tile = intersection[epoch * exp_dev + me] - me * tile_dev
        picked = template[jnp.clip(tile, 0, tile_dev - 1)]
        chosen[epoch] = picked
        wide = picked.astype(f32)
        for which in range(n_up):
            chosen_edge[which, epoch] = rim(wide, which).astype(bf16)
    loads[5].wait()
    for exposure in range(exp_dev):
        coefs[exposure] = jnp.zeros((8, LANES), f32)
        for p in range(n_poly):
            coefs[exposure, p : p + 1, 0:n_sel] = coefficients[p, exposure : exposure + 1, :]

    for epoch in range(n_epoch - 1):
        pl.when(epoch < me)(lambda epoch=epoch: coefficient_tile(epoch, me).start())
    pl.when(me > 0)(lambda: send_image(0))
    loads[2].wait()
    loads[3].wait()
    loads[4].wait()
    for epoch in range(n_epoch):
        share = bad_mask[epoch].astype(f32) / variance[epoch]
        weight[epoch] = share
        code[epoch] = encode(science[epoch], share)
    for epoch in range(n_epoch - 1):

        @pl.when(epoch < me)
        def _(epoch=epoch):
            if epoch > 0:
                send_image(epoch)
            coded(epoch, me).start()

    for t in range(tile_dev):
        wide = template[t].astype(f32)
        for which in range(n_up):
            own_edge[which, t] = rim(wide, which).astype(bf16)
    for u, s, kind in images[1:]:
        guarded(
            both(both(u[3], s[3]), lower(u, s)),
            lambda u=u, s=s, kind=kind: own_piece(u, s, kind, False).start(),
        )

    def clear(ref):
        ref[...] = jnp.zeros(ref.shape, ref.dtype)

    def clear_up(slot):
        clear(vertical.at[slot])
        clear(own_vertical.at[slot])

    def clear_side(slot):
        clear(lateral.at[slot])
        clear(own_lateral.at[slot])

    def clear_corner(slot, at):
        clear(corner.at[slot, at])
        clear(own_corner.at[slot, at])

    if n_strip == 1:
        clear(vertical)
        clear(own_vertical)
        clear(corner)
        clear(own_corner)
    elif n_strip == 2:
        clear_up(strip)
        for at in range(2):
            clear_corner(strip, at)
    else:
        for slot, edge in ((0, strip == 0), (1, strip == n_strip - 1)):

            @pl.when(edge)
            def _(slot=slot):
                clear_up(slot)
                for at in range(2):
                    clear_corner(slot, at)

    if n_band == 1:
        clear(lateral)
        clear(own_lateral)
        if n_strip > 1:
            clear(corner)
            clear(own_corner)
    elif n_band == 2:
        clear_side(band)
        if n_strip == 2:
            clear_corner(1 - strip, band)
        elif n_strip > 2:
            for slot, held in ((0, strip > 0), (1, strip < n_strip - 1)):
                pl.when(held)(lambda slot=slot: clear_corner(slot, band))
    else:
        for slot, edge in ((0, band == 0), (1, band == n_band - 1)):

            @pl.when(edge)
            def _(slot=slot):
                clear_side(slot)
                for at in range(2):
                    clear_corner(at, slot)

    slab[:, :, height + 2 * EDGE_ROWS :, :] = jnp.zeros(
        (slab.shape[0], slab.shape[1], 8, LANES), f32
    )

    lane = lax.broadcasted_iota(jnp.int32, (8, LANES), 1)
    sub = lax.broadcasted_iota(jnp.int32, (8, LANES), 0)
    n_pairs = (ks + 1) // 2
    n_tiles = n_pairs * SLOT // LANES
    later = jnp.bitwise_and(lane, 7) >= sub

    def mix_of(some, indices):
        parts = []
        for j in range(n_sel):
            column = jnp.broadcast_to(some[:, j : j + 1], (8, LANES))
            parts.append(jnp.where(lane == indices(j), column, 0.0))
        while len(parts) > 1:
            parts = [
                parts[i] + parts[i + 1] if i + 1 < len(parts) else parts[i]
                for i in range(0, len(parts), 2)
            ]
        mix = jnp.where(sub < n_poly, parts[0], 0.0)
        mix = mix + pltpu.roll(mix, half, 1)
        high = mix.astype(bf16).astype(f32)
        return high, mix - high

    def mixed(pairs):
        rows = jnp.concatenate([p[0] for p in pairs] + [p[1] for p in pairs], axis=0)
        out = lax.dot_general(
            rows.astype(bf16), table[...], (((1,), (1,)), ((), ())), preferred_element_type=f32
        )
        size = 8 * len(pairs)
        return (out[:size] + out[size:]).astype(bf16).astype(f32)

    def spread(row, into):
        for p in range(0, n_poly, 2):
            for t in range(n_tiles):
                halves = []
                for h in range(2):
                    at = row * 8 + p + h
                    wide = jnp.broadcast_to(
                        kernels[at : at + 1, t * LANES : (t + 1) * LANES], (8, LANES)
                    )
                    close = pltpu.roll(wide, 0, 1, stride=1, stride_axis=0)
                    far = pltpu.roll(wide, 8, 1, stride=1, stride_axis=0)
                    halves.append(jnp.where(later, close, far))
                toeplitz[into, p * 8 : (p + 2) * 8, t * LANES : (t + 1) * LANES] = (
                    jnp.concatenate(halves, axis=0).astype(bf16)
                )

    loads[6].wait()
    pairs = [
        mix_of(
            coefs[exposure],
            lambda j, exposure=exposure: basis_index[exposure, j],
        )
        for exposure in range(exp_dev)
    ]

    loads[7].wait()
    blank = jnp.zeros((8, LANES), f32)

    def taps(b, g):
        if b >= ks or g * 8 >= ks:
            return blank
        here = min(8, ks - g * 8)
        tile = basis[g * 8 : g * 8 + here, b, :]
        if here < 8:
            tile = jnp.concatenate([tile, jnp.zeros((8 - here, n_basis), f32)], axis=0)
        tile = jnp.concatenate([tile, jnp.zeros((8, LANES - n_basis), f32)], axis=1)
        high = tile.astype(bf16).astype(f32)
        return jnp.where(lane < half, high, pltpu.roll(tile - high, half, 1))

    table[...] = jnp.concatenate(
        [
            taps(2 * q + h, g)
            for q in range(n_pairs)
            for g in range(GROUPS)
            for h in range(2)
        ],
        axis=0,
    ).astype(bf16)
    kernels[0 : 8 * exp_dev] = mixed(pairs)
    loads[8].wait()
    for exposure in range(exp_dev):
        spread(exposure, exposure)

    row = lax.broadcasted_iota(jnp.int32, (height, 1), 0) + strip * height
    col = lax.broadcasted_iota(jnp.int32, (1, width), 1) + band * width
    r = (2.0 * row.astype(f32) + 1.0) / (height * n_strip) - 1.0
    c = (2.0 * col.astype(f32) + 1.0) / (width * n_band) - 1.0
    r = jnp.broadcast_to(r, (height, width))
    c = jnp.broadcast_to(c, (height, width))

    span = height + 8 * GROUPS - 8
    at_lane = lax.broadcasted_iota(jnp.int32, (span, LANES), 1)

    def lay(board, middle, up, side, edge, at):
        for rows, body, rims in (
            (0, up(0), (edge(0, 1), edge(0, 0))),
            (EDGE_ROWS, middle, (side(1), side(0))),
            (EDGE_ROWS + height, up(1), (edge(1, 1), edge(1, 0))),
        ):
            wide = body.astype(f32)
            size = wide.shape[0]
            for t in range(n_lane):
                slab[board, t, rows : rows + size, :] = wide[:, t * LANES : (t + 1) * LANES]
            first = lax.broadcasted_iota(jnp.int32, (size, LANES), 1) < half
            slab[board, n_lane, rows : rows + size, :] = jnp.where(
                first, rims[0].astype(f32), rims[1].astype(f32)
            )

    def lay_own(board, tile):
        lay(
            board,
            template[tile],
            lambda v: own_vertical[v, tile],
            lambda s: own_lateral[s, tile],
            lambda v, s: own_corner[v, s, tile],
            tile,
        )

    def lay_other(board, epoch):
        lay(
            board,
            centre[epoch],
            lambda v: vertical[v, epoch],
            lambda s: lateral[s, epoch],
            lambda v, s: corner[v, s, epoch],
            epoch,
        )

    def models(board, factor, down, along):
        views = []
        for h in range(2):
            turned = [
                pltpu.roll(slab[board, t, pl.ds(down, span), :], along - h, 1)
                for t in range(n_lane + 1)
            ]
            views.append(
                jnp.concatenate(
                    [
                        jnp.where(at_lane < along - h, turned[t - 1], turned[t])
                        for t in range(n_lane + 1)
                    ],
                    axis=1,
                )
            )
        tiles = [
            jnp.concatenate(
                [views[0][g * 8 : g * 8 + 8], views[1][g * 8 : g * 8 + 8]], axis=0
            ).astype(bf16)
            for g in range(span // 8)
        ]
        moved = [[tile[:, 2 * q : 2 * q + width] for tile in tiles] for q in range(n_pairs)]
        for block in range(height // 8):
            stacked = jnp.concatenate(
                [moved[q][block + g] for q in range(n_pairs) for g in range(GROUPS)], axis=0
            )
            conv = jnp.dot(factor, stacked, preferred_element_type=f32)
            q = [conv[p * 8 : (p + 1) * 8] for p in range(n_poly)]
            at = slice(block * 8, block * 8 + 8)
            rr, cc = r[at], c[at]
            yield at, q[0] + rr * (q[1] + rr * q[3] + cc * q[4]) + cc * (q[2] + cc * q[5])

    def tile_of(epoch):
        return intersection[epoch * exp_dev + me] - me * tile_dev

    def down_of(shift):
        return EDGE_ROWS - HALF + shift

    def along_of(shift):
        return HALF - shift

    behind = partners - 1 - ahead_of_me

    @pl.when(behind > 0)
    def _():
        pl.semaphore_wait(token.at[me], behind)

    for u, s, kind in images[1:]:
        guarded(
            both(both(u[3], s[3]), jnp.logical_not(lower(u, s))),
            lambda u=u, s=s, kind=kind: own_piece(u, s, kind, False).start(),
        )
    for step in range(1, n_epoch):

        @pl.when(me + step < n_epoch)
        def _(epoch=me + step):
            pl.semaphore_wait(token.at[epoch], 1)
            send_small(epoch)
            coefficient_tile(epoch, me).start()
            coded(epoch, me).start()

    for u, s, kind in images_in[1:]:
        guarded(both(u[3], s[3]), lambda u=u, s=s, kind=kind: own_piece(u, s, kind, True).wait_recv())

    for t in range(tile_dev):
        lay_own(t, t)

    def own_board(tile):
        return jnp.clip(tile, 0, tile_dev - 1)

    tile = tile_of(me)
    for at, model in models(own_board(tile), toeplitz[me], down_of(offsets[0, me]), along_of(offsets[1, me])):
        left = science[me, at] - model
        residual[me, at] = left
        share = weight[me, at]
        for t in range(tile_dev):
            here = (tile == t).astype(f32)
            numer[t, at] = share * left * here
            denom[t, at] = share * here

    def partner(step):
        return jnp.where(me + step < n_epoch, me + step, n_epoch - 1 - step)

    def theirs(step):
        epoch = partner(step)
        for one in small(me, epoch) + [coefficient_tile(me, epoch)]:
            one.wait_recv()
        last = exp_dev
        kernels[8 * last : 8 * last + 8] = mixed(
            [mix_of(coefs_in[epoch], lambda j: basis_index_in[epoch, me, j])]
        )
        spread(last, last)
        for at, model in models(
            own_board(tile_of(epoch)),
            toeplitz[last],
            down_of(offsets_in[epoch, 0, me]),
            along_of(offsets_in[epoch, 1, me]),
        ):
            model_out[epoch, at] = model
        pl.when(epoch > me)(lambda: returned(epoch, me).start())

    def ours(step):
        epoch = partner(step)
        wait_image(epoch)
        lay_other(tile_dev, epoch)
        for at, model in models(
            tile_dev, toeplitz[epoch], down_of(offsets[0, epoch]), along_of(offsets[1, epoch])
        ):
            residual[epoch, at] = science[epoch, at] - model

    def settle(step):
        epoch = partner(step)
        returned(me, epoch).wait_recv()
        residual[epoch] = science[epoch] - model_in[epoch]

    def mine(step):
        pl.when(partner(step) > me)(lambda: ours(step))

    def finish(step):
        gather(step)
        pl.when(partner(step) < me)(lambda: settle(step))

    def gather(step):
        epoch = partner(step)
        tile = tile_of(epoch)
        coded(me, epoch).wait_recv()
        seen, share = decode(code_in[epoch])
        value = share * (seen - model_out[epoch])
        for t in range(tile_dev):
            here = (tile == t).astype(f32)
            numer[t] = numer[t] + value * here
            denom[t] = denom[t] + share * here

    if n_epoch <= 4:
        for step in range(1, n_epoch):
            theirs(step)
        for step in range(1, n_epoch):
            mine(step)
        for step in range(1, n_epoch):
            finish(step)
    else:
        lax.fori_loop(1, n_epoch, lambda step, carry: (theirs(step), carry)[1], 0)
        lax.fori_loop(1, n_epoch, lambda step, carry: (mine(step), carry)[1], 0)
        lax.fori_loop(1, n_epoch, lambda step, carry: (finish(step), carry)[1], 0)

    for t in range(tile_dev):
        coadd[t] = numer[t] / (denom[t] + 1.0)

    for u, s, kind in images[1:]:
        guarded(both(u[3], s[3]), lambda u=u, s=s, kind=kind: own_piece(u, s, kind, False).wait_send())
    if n_epoch > 1:
        rest = pl.ds(0, n_epoch - 1)

        def drain(source, kind, u, s):
            copy(source, source, send_sem.at[kind], recv_sem.at[0, kind], device(me, u, s)).wait_send()

        for number in range(1, n_epoch):

            @pl.when(me == number)
            def _(number=number):
                lead = pl.ds(0, number)
                for u, s, kind in images:
                    if u is none and s is none:
                        source = chosen.at[lead]
                    elif s is none:
                        source = chosen_edge.at[u[1], lead]
                    elif u is none:
                        source = chosen.at[lead, :, lanes_of(s)]
                    else:
                        source = chosen_edge.at[u[1], lead, :, lanes_of(s)]
                    guarded(
                        both(u[3], s[3]),
                        lambda u=u, s=s, kind=kind, source=source: drain(source, kind, u, s),
                    )

            @pl.when(me == n_epoch - 1 - number)
            def _(number=number):
                drain(model_out.at[pl.ds(0, number)], MODEL, none, none)

        for held, kind in (
            (offsets_in, OFFS),
            (basis_index_in, INDX),
            (coefs, COEF),
            (code, CODE),
        ):
            drain(held.at[rest], kind, none, none)


def leave(residual, coadd, residual_out, coadd_out, sem):
    parts = [
        (held.at[i], out.at[i])
        for held, out in ((residual, residual_out), (coadd, coadd_out))
        for i in range(held.shape[0])
    ]
    copies = [pltpu.make_async_copy(held, out, sem.at[i]) for i, (held, out) in enumerate(parts)]
    for one in copies:
        one.start()
    for one in copies:
        one.wait()


def local(sizes, template, science, variance, bad_mask, intersection, offsets, basis_index, coefficients, basis):
    n_epoch, n_strip, n_band = sizes
    tile_dev, height, width = template.shape
    exp_dev = science.shape[0]
    assert exp_dev == n_epoch
    n_poly = coefficients.shape[2]
    n_sel = basis_index.shape[1]
    ks = basis.shape[1]
    n_pairs = (ks + 1) // 2
    far = pl.BlockSpec(memory_space=pltpu.HBM)
    near = pl.BlockSpec(memory_space=pltpu.VMEM)
    free = pl.BlockSpec(memory_space=pl.ANY)
    bf16, f32 = jnp.bfloat16, jnp.float32
    dma = pltpu.SemaphoreType.DMA
    offsets = offsets.T
    coefficients = coefficients.transpose(2, 0, 1)
    basis = basis.transpose(1, 2, 0)
    n_up, n_side = min(n_strip - 1, 2), min(n_band - 1, 2)
    n_image = (1 + n_up) * (1 + n_side)
    edges = max(n_up, 1)
    rim = EDGE_ROWS
    residual, coadd = pl.pallas_call(
        functools.partial(kernel, sizes),
        out_shape=(
            pltpu.VMEM(science.shape, f32),
            pltpu.VMEM(template.shape, f32),
        ),
        in_specs=[far] * 9,
        out_specs=(near, near),
        scratch_shapes=[
            pltpu.SMEM(intersection.shape, jnp.int32),
            pltpu.SMEM(offsets.shape, jnp.int32),
            pltpu.SMEM((n_epoch,) + offsets.shape, jnp.int32),
            pltpu.SMEM(basis_index.shape, jnp.int32),
            pltpu.SMEM((n_epoch,) + basis_index.shape, jnp.int32),
            pltpu.VMEM(coefficients.shape, f32),
            pltpu.VMEM((n_epoch, 8, LANES), f32),
            pltpu.VMEM(template.shape, bf16),
            pltpu.VMEM(science.shape, f32),
            pltpu.VMEM(science.shape, f32),
            pltpu.VMEM(science.shape, jnp.int32),
            pltpu.VMEM(basis.shape, f32),
            pltpu.VMEM((n_epoch, height, width), bf16),
            pltpu.VMEM((edges, n_epoch, rim, width), bf16),
            pltpu.VMEM((edges, tile_dev, rim, width), bf16),
            pltpu.VMEM((n_epoch, height, width), bf16),
            pltpu.VMEM((2, n_epoch, rim, width), bf16),
            pltpu.VMEM((2, n_epoch, height, LANES), bf16),
            pltpu.VMEM((2, 2, n_epoch, rim, LANES), bf16),
            pltpu.VMEM((2, tile_dev, rim, width), bf16),
            pltpu.VMEM((2, tile_dev, height, LANES), bf16),
            pltpu.VMEM((2, 2, tile_dev, rim, LANES), bf16),
            pltpu.VMEM((exp_dev, 8, LANES), f32),
            pltpu.VMEM((n_pairs * SLOT, LANES), bf16),
            pltpu.VMEM((8 * exp_dev + 8, n_pairs * SLOT), f32),
            pltpu.VMEM((tile_dev + 1, width // LANES + 1, 2 * rim + height + 8, LANES), f32),
            pltpu.VMEM((exp_dev + 1, n_poly * 8, n_pairs * SLOT), bf16),
            pltpu.VMEM((exp_dev, height, width), f32),
            pltpu.VMEM((n_epoch, height, width), jnp.int32),
            pltpu.VMEM((n_epoch, height, width), jnp.int32),
            pltpu.VMEM((n_epoch, height, width), f32),
            pltpu.VMEM((n_epoch, height, width), f32),
            pltpu.VMEM(template.shape, f32),
            pltpu.VMEM(template.shape, f32),
            dma((9,)),
            dma((n_image + 5,)),
            dma((max(n_epoch - 1, 1), n_image + 5)),
            dma((n_image,)),
            dma((n_image,)),
            pltpu.SemaphoreType.REGULAR((n_epoch,)),
        ],
        compiler_params=pltpu.CompilerParams(
            collective_id=0, has_side_effects=True
        ),
    )(
        intersection, offsets, basis_index, coefficients,
        template, science, variance, bad_mask, basis,
    )
    return pl.pallas_call(
        leave,
        out_shape=(
            jax.ShapeDtypeStruct(science.shape, f32),
            jax.ShapeDtypeStruct(template.shape, f32),
        ),
        in_specs=[near] * 2,
        out_specs=(free, free),
        scratch_shapes=[dma((exp_dev + tile_dev,))],
    )(*(pltpu.with_memory_space_constraint(x, pltpu.VMEM) for x in (residual, coadd)))


def solution(mesh):
    sizes = (mesh.shape["epoch"], mesh.shape["strip"], mesh.shape["band"])
    image = P(("groups", "epoch"), "strip", "band")
    split = ("groups", "epoch")
    in_specs = (
        image, image, image, image, P("groups"),
        P(split, None), P(split, None), P(split, None, None), P(),
    )
    return jax.shard_map(
        functools.partial(local, sizes),
        mesh=mesh,
        in_specs=in_specs,
        out_specs=(image, image),
        check_vma=False,
    )
```

```python
import functools

import jax
import jax.numpy as jnp
from jax import lax
from jax.experimental import pallas as pl
from jax.experimental.pallas import tpu as pltpu
from jax.sharding import PartitionSpec as P

HALF = 9
SHIFT = 4
EDGE_ROWS = 16
LANES = 128
SLOT = 64
GROUPS = 4
SIDE = 16
SCIENCE_TOP = 6.0
WEIGHT_TOP = 0.5
LEVELS = 65535.0

MESH = pl.DeviceIdType.MESH


def links_of(size, place):
    if size == 1:
        return []
    if size == 2:
        return [(1 - 2 * place, 0, place, None, None)]
    return [
        (-1, 0, 1, place > 0, place < size - 1),
        (1, 1, 0, place < size - 1, place > 0),
    ]


def both(first, second):
    if first is None:
        return second
    if second is None:
        return first
    return jnp.logical_and(first, second)


def guarded(side, body):
    if side is None:
        body()
    else:
        pl.when(side)(body)


def encode(science, weight):
    high = (science + SCIENCE_TOP) * (LEVELS / (2.0 * SCIENCE_TOP)) + 0.5
    low = weight * (LEVELS / WEIGHT_TOP) + 0.5
    high = jnp.clip(high, 0.0, LEVELS).astype(jnp.int32)
    low = jnp.clip(low, 0.0, LEVELS).astype(jnp.int32)
    return jnp.bitwise_or(jnp.left_shift(high, 16), low)


def decode(code):
    high = lax.shift_right_logical(code, jnp.full(code.shape, 16, jnp.int32))
    low = jnp.bitwise_and(code, 65535)
    science = high.astype(jnp.float32) * (2.0 * SCIENCE_TOP / LEVELS) - SCIENCE_TOP
    return science, low.astype(jnp.float32) * (WEIGHT_TOP / LEVELS)


def kernel(
    sizes,
    intersection_hbm,
    offsets_hbm,
    basis_index_hbm,
    coefficients_hbm,
    template_hbm,
    science_hbm,
    variance_hbm,
    bad_mask_hbm,
    basis_hbm,
    residual,
    coadd,
    intersection,
    offsets,
    offsets_in,
    basis_index,
    basis_index_in,
    coefficients,
    coefs_in,
    template,
    science,
    variance,
    bad_mask,
    basis,
    chosen,
    chosen_edge,
    chosen_side,
    chosen_corner,
    own_edge,
    own_side,
    own_diagonal,
    centre,
    vertical,
    lateral,
    corner,
    own_vertical,
    own_lateral,
    own_corner,
    coefs,
    coef_row,
    table,
    kernels,
    slab,
    toeplitz,
    weight,
    code,
    code_in,
    model_out,
    model_in,
    numer,
    denom,
    local_sem,
    send_sem,
    recv_sem,
    own_send,
    own_recv,
    token,
):
    n_epoch, n_strip, n_band = sizes
    tile_dev, height, width = template.shape
    exp_dev = science.shape[0]
    n_poly, _, n_sel = coefficients.shape
    ks, _, n_basis = basis.shape
    n_lane = width // LANES
    half = LANES // 2
    f32, bf16 = jnp.float32, jnp.bfloat16
    group = lax.axis_index("groups")
    me = lax.axis_index("epoch")
    strip = lax.axis_index("strip")
    band = lax.axis_index("band")

    ups = links_of(n_strip, strip)
    sides = links_of(n_band, band)
    none = (0, None, None, None, None)
    near = [(u, s) for u in [none] + ups for s in [none] + sides]

    def device(epoch, u, s):
        return (group, epoch, strip + u[0], band + s[0])

    loads = [
        pltpu.make_async_copy(held, here, local_sem.at[i])
        for i, (held, here) in enumerate(
            (
                (intersection_hbm, intersection),
                (template_hbm, template),
                (variance_hbm, variance),
                (bad_mask_hbm, bad_mask),
                (science_hbm, science),
                (coefficients_hbm, coefficients),
                (basis_index_hbm, basis_index),
                (basis_hbm, basis),
                (offsets_hbm, offsets),
            )
        )
    ]
    for load in loads:
        load.start()

    def count(size, place):
        if size < 3:
            return size
        return 1 + jnp.minimum(place, 1) + jnp.minimum(size - 1 - place, 1)

    def before(size, place):
        return place if size < 3 else jnp.minimum(place, 1)

    across = count(n_band, band)
    partners = count(n_strip, strip) * across
    ahead_of_me = before(n_strip, strip) * across + before(n_band, band)

    def lower(u, s):
        if u is not none:
            return strip + u[0] < strip
        return band + s[0] < band

    barrier = pltpu.get_barrier_semaphore()

    def signal(sem, epoch, u, s):
        pl.semaphore_signal(sem, inc=1, device_id=device(epoch, u, s), device_id_type=MESH)

    def to_epoch(sem, epoch):
        for u, s in near:
            guarded(both(u[3], s[3]), lambda u=u, s=s: signal(sem, epoch, u, s))

    for u, s in near[1:]:
        guarded(
            both(both(u[3], s[3]), jnp.logical_not(lower(u, s))),
            lambda u=u, s=s: signal(barrier, me, u, s),
        )
    for step in range(1, n_epoch):
        pl.when(me + step < n_epoch)(lambda step=step: to_epoch(barrier, me + step))
    met = partners * me + ahead_of_me

    @pl.when(met > 0)
    def _():
        pl.semaphore_wait(barrier, met)

    for u, s in near[1:]:
        guarded(
            both(both(u[3], s[3]), lower(u, s)),
            lambda u=u, s=s: signal(token.at[me], me, u, s),
        )
    for epoch in range(n_epoch - 1):
        pl.when(epoch < me)(lambda epoch=epoch: signal(token.at[me], epoch, none, none))

    def slot_of(sender, receiver):
        return sender - (sender > receiver).astype(jnp.int32)

    lane = lax.broadcasted_iota(jnp.int32, (8, LANES), 1)
    sub = lax.broadcasted_iota(jnp.int32, (8, LANES), 0)

    def within(base):
        return jnp.bitwise_and(lane - base, LANES - 1) < SIDE

    def side_tile(wide, which):
        first, last = wide[:, :LANES], wide[:, width - LANES :]
        if n_band == 2:
            return jnp.where(band == 0, last, first), (1 - band) * (LANES - SIDE)
        return (first, 0) if which == 0 else (last, LANES - SIDE)

    def packed(wide, which):
        tile, base = side_tile(wide, which)
        out = jnp.zeros((8, LANES), f32)
        for i in range(wide.shape[0] // 8):
            part = tile[8 * i : 8 * i + 8]
            if i > 0:
                part = pltpu.roll(part, SIDE * i, 1)
            out = jnp.where(within(base + SIDE * i), part, out)
        return out.astype(bf16)

    def copy(source, dest, sent, received, to):
        return pltpu.make_async_remote_copy(
            src_ref=source,
            dst_ref=dest,
            send_sem=sent,
            recv_sem=received,
            device_id=to,
            device_id_type=MESH,
        )

    n_up, n_side = len(ups), len(sides)
    images = []
    for u, s in near:
        i = 0 if u is none else 1 + ups.index(u)
        j = 0 if s is none else 1 + sides.index(s)
        images.append((u, s, i * (1 + n_side) + j))
    n_image = (1 + n_up) * (1 + n_side)
    CODE, COEF, OFFS, INDX, MODEL = (n_image + i for i in range(5))

    def image(epoch, u, s, kind, sender, at=None):
        source_at = epoch if at is None else at
        if u is none and s is none:
            source, dest = chosen.at[source_at], centre.at[sender]
        elif s is none:
            source, dest = chosen_edge.at[u[1], source_at], vertical.at[u[2], sender]
        elif u is none:
            source, dest = chosen_side.at[s[1], source_at], lateral.at[s[2], sender]
        else:
            source = chosen_corner.at[u[1], s[1], source_at]
            dest = corner.at[u[2], s[2], sender]
        return copy(
            source, dest, send_sem.at[kind], recv_sem.at[slot_of(sender, epoch), kind], device(epoch, u, s)
        )

    def arriving(epoch, u, s, kind):
        if u is none and s is none:
            dest = centre.at[epoch]
        elif s is none:
            dest = vertical.at[u[2], epoch]
        elif u is none:
            dest = lateral.at[s[2], epoch]
        else:
            dest = corner.at[u[2], s[2], epoch]
        return copy(dest, dest, send_sem.at[kind], recv_sem.at[slot_of(epoch, me), kind], device(epoch, u, s))

    def landing(links, place, size):
        if size == 2:
            return [(k[0], k[1], 1 - place, None, None) for k in links]
        return [(k[0], k[1], k[2], k[4], k[3]) for k in links]

    ups_in = landing(ups, strip, n_strip)
    sides_in = landing(sides, band, n_band)
    images_in = []
    for u, s, kind in images:
        a = none if u is none else ups_in[ups.index(u)]
        b = none if s is none else sides_in[sides.index(s)]
        images_in.append((a, b, kind))

    def send_image(epoch):
        for u, s, kind in images:
            guarded(
                both(u[3], s[3]), lambda u=u, s=s, kind=kind: image(epoch, u, s, kind, me).start()
            )

    def wait_image(epoch):
        for u, s, kind in images_in:
            guarded(
                both(u[3], s[3]), lambda u=u, s=s, kind=kind: arriving(epoch, u, s, kind).wait_recv()
            )

    def small(epoch, sender):
        return [
            copy(held, into.at[sender], send_sem.at[kind], recv_sem.at[slot_of(sender, epoch), kind], device(epoch, none, none))
            for held, into, kind in (
                (offsets_hbm, offsets_in, OFFS),
                (basis_index_hbm, basis_index_in, INDX),
            )
        ]

    def coefficient_tile(epoch, sender):
        return copy(
            coef_row.at[epoch], coefs_in.at[sender], send_sem.at[COEF], recv_sem.at[slot_of(sender, epoch), COEF],
            device(epoch, none, none),
        )

    def coded(epoch, sender):
        return copy(
            code.at[epoch], code_in.at[sender], send_sem.at[CODE], recv_sem.at[slot_of(sender, epoch), CODE],
            device(epoch, none, none),
        )

    def returned(epoch, sender):
        return copy(
            model_out.at[epoch], model_in.at[sender], send_sem.at[MODEL], recv_sem.at[slot_of(sender, epoch), MODEL],
            device(epoch, none, none),
        )

    def own_piece(u, s, kind, incoming):
        if s is none:
            source, dest = own_edge.at[0 if incoming else u[1]], own_vertical.at[u[2]]
        elif u is none:
            source, dest = own_side.at[0 if incoming else s[1]], own_lateral.at[s[2]]
        else:
            source = own_diagonal.at[0 if incoming else u[1], 0 if incoming else s[1]]
            dest = own_corner.at[u[2], s[2]]
        if incoming:
            source = dest
        return copy(source, dest, own_send.at[kind], own_recv.at[kind], device(me, u, s))

    def send_small(epoch):
        for one in small(epoch, me):
            one.start()

    for epoch in range(n_epoch - 1):
        pl.when(epoch < me)(lambda epoch=epoch: send_small(epoch))

    loads[0].wait()
    loads[1].wait()

    def rim(wide, which):
        low, high = wide[:EDGE_ROWS], wide[height - EDGE_ROWS :]
        if n_strip == 2:
            return jnp.where(strip == 0, high, low)
        return low if which == 0 else high

    for epoch in range(n_epoch):
        tile = intersection[epoch * exp_dev + me] - me * tile_dev
        picked = template[jnp.clip(tile, 0, tile_dev - 1)]
        chosen[epoch] = picked
        wide = picked.astype(f32)
        for side in range(n_side):
            chosen_side[side, epoch] = packed(wide, side)
        for which in range(n_up):
            edge = rim(wide, which)
            chosen_edge[which, epoch] = edge.astype(bf16)
            for side in range(n_side):
                chosen_corner[which, side, epoch] = packed(edge, side)
    loads[5].wait()
    for exposure in range(exp_dev):
        coefs[exposure] = jnp.zeros((8, LANES), f32)
        for p in range(n_poly):
            coefs[exposure, p : p + 1, 0:n_sel] = coefficients[p, exposure : exposure + 1, :]
        coef_row[exposure] = jnp.sum(
            pltpu.roll(coefs[exposure], 0, 1, stride=n_sel, stride_axis=0), axis=0, keepdims=True
        )

    for epoch in range(n_epoch - 1):
        pl.when(epoch < me)(lambda epoch=epoch: coefficient_tile(epoch, me).start())
    pl.when(me > 0)(lambda: send_image(0))
    loads[2].wait()
    loads[3].wait()
    loads[4].wait()
    for epoch in range(n_epoch):
        share = bad_mask[epoch].astype(f32) / variance[epoch]
        weight[epoch] = share
        code[epoch] = encode(science[epoch], share)
    for epoch in range(n_epoch - 1):

        @pl.when(epoch < me)
        def _(epoch=epoch):
            if epoch > 0:
                send_image(epoch)
            coded(epoch, me).start()

    for t in range(tile_dev):
        wide = template[t].astype(f32)
        for side in range(n_side):
            own_side[side, t] = packed(wide, side)
        for which in range(n_up):
            edge = rim(wide, which)
            own_edge[which, t] = edge.astype(bf16)
            for side in range(n_side):
                own_diagonal[which, side, t] = packed(edge, side)
    for u, s, kind in images[1:]:
        guarded(
            both(both(u[3], s[3]), lower(u, s)),
            lambda u=u, s=s, kind=kind: own_piece(u, s, kind, False).start(),
        )

    def clear(ref):
        ref[...] = jnp.zeros(ref.shape, ref.dtype)

    def clear_up(slot):
        clear(vertical.at[slot])
        clear(own_vertical.at[slot])

    def clear_side(slot):
        clear(lateral.at[slot])
        clear(own_lateral.at[slot])

    def clear_corner(slot, at):
        clear(corner.at[slot, at])
        clear(own_corner.at[slot, at])

    if n_strip == 1:
        clear(vertical)
        clear(own_vertical)
        clear(corner)
        clear(own_corner)
    elif n_strip == 2:
        clear_up(strip)
        for at in range(2):
            clear_corner(strip, at)
    else:
        for slot, edge in ((0, strip == 0), (1, strip == n_strip - 1)):

            @pl.when(edge)
            def _(slot=slot):
                clear_up(slot)
                for at in range(2):
                    clear_corner(slot, at)

    if n_band == 1:
        clear(lateral)
        clear(own_lateral)
        if n_strip > 1:
            clear(corner)
            clear(own_corner)
    elif n_band == 2:
        clear_side(band)
        if n_strip == 2:
            clear_corner(1 - strip, band)
        elif n_strip > 2:
            for slot, held in ((0, strip > 0), (1, strip < n_strip - 1)):
                pl.when(held)(lambda slot=slot: clear_corner(slot, band))
    else:
        for slot, edge in ((0, band == 0), (1, band == n_band - 1)):

            @pl.when(edge)
            def _(slot=slot):
                clear_side(slot)
                for at in range(2):
                    clear_corner(at, slot)

    slab[:, :, height + 2 * EDGE_ROWS :, :] = jnp.zeros(
        (slab.shape[0], slab.shape[1], 8, LANES), f32
    )

    n_pairs = (ks + 1) // 2
    n_tiles = n_pairs * SLOT // LANES
    later = jnp.bitwise_and(lane, 7) >= sub

    def mix_of(some, indices):
        parts = []
        for j in range(n_sel):
            column = jnp.broadcast_to(some[:, j : j + 1], (8, LANES))
            parts.append(jnp.where(lane == indices(j), column, 0.0))
        while len(parts) > 1:
            parts = [
                parts[i] + parts[i + 1] if i + 1 < len(parts) else parts[i]
                for i in range(0, len(parts), 2)
            ]
        mix = jnp.where(sub < n_poly, parts[0], 0.0)
        mix = mix + pltpu.roll(mix, half, 1)
        high = mix.astype(bf16).astype(f32)
        return high, mix - high

    def unpacked(line):
        wide = jnp.broadcast_to(line, (8, LANES))
        out = wide
        for p in range(1, n_poly):
            out = jnp.where(sub == p, pltpu.roll(wide, LANES - n_sel * p, 1), out)
        return out

    def mixed(pairs):
        rows = jnp.concatenate([p[0] for p in pairs] + [p[1] for p in pairs], axis=0)
        out = lax.dot_general(
            rows.astype(bf16), table[...], (((1,), (1,)), ((), ())), preferred_element_type=f32
        )
        size = 8 * len(pairs)
        return (out[:size] + out[size:]).astype(bf16).astype(f32)

    def spread(row, into):
        for p in range(0, n_poly, 2):
            for t in range(n_tiles):
                halves = []
                for h in range(2):
                    at = row * 8 + p + h
                    wide = jnp.broadcast_to(
                        kernels[at : at + 1, t * LANES : (t + 1) * LANES], (8, LANES)
                    )
                    close = pltpu.roll(wide, 0, 1, stride=1, stride_axis=0)
                    far = pltpu.roll(wide, 8, 1, stride=1, stride_axis=0)
                    halves.append(jnp.where(later, close, far))
                toeplitz[into, p * 8 : (p + 2) * 8, t * LANES : (t + 1) * LANES] = (
                    jnp.concatenate(halves, axis=0).astype(bf16)
                )

    loads[6].wait()
    pairs = [
        mix_of(
            coefs[exposure],
            lambda j, exposure=exposure: basis_index[exposure, j],
        )
        for exposure in range(exp_dev)
    ]

    loads[7].wait()
    blank = jnp.zeros((8, LANES), f32)

    def taps(b, g):
        if b >= ks or g * 8 >= ks:
            return blank
        here = min(8, ks - g * 8)
        tile = basis[g * 8 : g * 8 + here, b, :]
        if here < 8:
            tile = jnp.concatenate([tile, jnp.zeros((8 - here, n_basis), f32)], axis=0)
        tile = jnp.concatenate([tile, jnp.zeros((8, LANES - n_basis), f32)], axis=1)
        high = tile.astype(bf16).astype(f32)
        return jnp.where(lane < half, high, pltpu.roll(tile - high, half, 1))

    table[...] = jnp.concatenate(
        [
            taps(2 * q + h, g)
            for q in range(n_pairs)
            for g in range(GROUPS)
            for h in range(2)
        ],
        axis=0,
    ).astype(bf16)
    kernels[0 : 8 * exp_dev] = mixed(pairs)
    loads[8].wait()
    for exposure in range(exp_dev):
        spread(exposure, exposure)

    row = lax.broadcasted_iota(jnp.int32, (height, 1), 0) + strip * height
    col = lax.broadcasted_iota(jnp.int32, (1, width), 1) + band * width
    r = (2.0 * row.astype(f32) + 1.0) / (height * n_strip) - 1.0
    c = (2.0 * col.astype(f32) + 1.0) / (width * n_band) - 1.0
    r = jnp.broadcast_to(r, (height, width))
    c = jnp.broadcast_to(c, (height, width))

    span = height + 8 * GROUPS - 8
    at_lane = lax.broadcasted_iota(jnp.int32, (span, LANES), 1)

    beside = [(0, LANES - SIDE), (1, 0)]
    if n_band == 2:
        beside = [(1 - band, band * (LANES - SIDE))]

    def lay(board, middle, up, side, edge, at):
        for rows, body, rims in (
            (0, up(0), [(edge(0, k).astype(f32), base) for k, base in beside]),
            (EDGE_ROWS, middle, [(side(k).astype(f32), base) for k, base in beside]),
            (EDGE_ROWS + height, up(1), [(edge(1, k).astype(f32), base) for k, base in beside]),
        ):
            wide = body.astype(f32)
            size = wide.shape[0]
            for t in range(n_lane):
                slab[board, t, rows : rows + size, :] = wide[:, t * LANES : (t + 1) * LANES]
            for i in range(size // 8):
                part = jnp.zeros((8, LANES), f32)
                for held, base in rims:
                    turned = held if i == 0 else pltpu.roll(held, LANES - SIDE * i, 1)
                    part = jnp.where(within(base), turned, part)
                slab[board, n_lane, rows + 8 * i : rows + 8 * i + 8, :] = part

    def lay_own(board, tile):
        lay(
            board,
            template[tile],
            lambda v: own_vertical[v, tile],
            lambda s: own_lateral[s, tile],
            lambda v, s: own_corner[v, s, tile],
            tile,
        )

    def lay_other(board, epoch):
        lay(
            board,
            centre[epoch],
            lambda v: vertical[v, epoch],
            lambda s: lateral[s, epoch],
            lambda v, s: corner[v, s, epoch],
            epoch,
        )

    def models(board, factor, down, along):
        views = []
        for h in range(2):
            turned = [
                pltpu.roll(slab[board, t, pl.ds(down, span), :], along - h, 1)
                for t in range(n_lane + 1)
            ]
            views.append(
                jnp.concatenate(
                    [
                        jnp.where(at_lane < along - h, turned[t - 1], turned[t])
                        for t in range(n_lane + 1)
                    ],
                    axis=1,
                )
            )
        tiles = [
            jnp.concatenate(
                [views[0][g * 8 : g * 8 + 8], views[1][g * 8 : g * 8 + 8]], axis=0
            ).astype(bf16)
            for g in range(span // 8)
        ]
        moved = [[tile[:, 2 * q : 2 * q + width] for tile in tiles] for q in range(n_pairs)]
        for block in range(height // 8):
            stacked = jnp.concatenate(
                [moved[q][block + g] for q in range(n_pairs) for g in range(GROUPS)], axis=0
            )
            conv = jnp.dot(factor, stacked, preferred_element_type=f32)
            q = [conv[p * 8 : (p + 1) * 8] for p in range(n_poly)]
            at = slice(block * 8, block * 8 + 8)
            rr, cc = r[at], c[at]
            yield at, q[0] + rr * (q[1] + rr * q[3] + cc * q[4]) + cc * (q[2] + cc * q[5])

    def tile_of(epoch):
        return intersection[epoch * exp_dev + me] - me * tile_dev

    def down_of(shift):
        return EDGE_ROWS - HALF + shift

    def along_of(shift):
        return HALF - shift

    behind = partners - 1 - ahead_of_me

    @pl.when(behind > 0)
    def _():
        pl.semaphore_wait(token.at[me], behind)

    for u, s, kind in images[1:]:
        guarded(
            both(both(u[3], s[3]), jnp.logical_not(lower(u, s))),
            lambda u=u, s=s, kind=kind: own_piece(u, s, kind, False).start(),
        )
    for step in range(1, n_epoch):

        @pl.when(me + step < n_epoch)
        def _(epoch=me + step):
            pl.semaphore_wait(token.at[epoch], 1)
            send_small(epoch)
            coefficient_tile(epoch, me).start()
            coded(epoch, me).start()

    for u, s, kind in images_in[1:]:
        guarded(both(u[3], s[3]), lambda u=u, s=s, kind=kind: own_piece(u, s, kind, True).wait_recv())

    for t in range(tile_dev):
        lay_own(t, t)

    def own_board(tile):
        return jnp.clip(tile, 0, tile_dev - 1)

    tile = tile_of(me)
    for at, model in models(own_board(tile), toeplitz[me], down_of(offsets[0, me]), along_of(offsets[1, me])):
        left = science[me, at] - model
        residual[me, at] = left
        share = weight[me, at]
        for t in range(tile_dev):
            here = (tile == t).astype(f32)
            numer[t, at] = share * left * here
            denom[t, at] = share * here

    def partner(step):
        return jnp.where(me + step < n_epoch, me + step, n_epoch - 1 - step)

    def theirs(step):
        epoch = partner(step)
        for one in small(me, epoch) + [coefficient_tile(me, epoch)]:
            one.wait_recv()
        last = exp_dev
        kernels[8 * last : 8 * last + 8] = mixed(
            [mix_of(unpacked(coefs_in[epoch]), lambda j: basis_index_in[epoch, me, j])]
        )
        spread(last, last)
        for at, model in models(
            own_board(tile_of(epoch)),
            toeplitz[last],
            down_of(offsets_in[epoch, 0, me]),
            along_of(offsets_in[epoch, 1, me]),
        ):
            model_out[epoch, at] = model
        pl.when(epoch > me)(lambda: returned(epoch, me).start())

    def ours(step):
        epoch = partner(step)
        wait_image(epoch)
        lay_other(tile_dev, epoch)
        for at, model in models(
            tile_dev, toeplitz[epoch], down_of(offsets[0, epoch]), along_of(offsets[1, epoch])
        ):
            residual[epoch, at] = science[epoch, at] - model

    def settle(step):
        epoch = partner(step)
        returned(me, epoch).wait_recv()
        residual[epoch] = science[epoch] - model_in[epoch]

    def mine(step):
        pl.when(partner(step) > me)(lambda: ours(step))

    def finish(step):
        gather(step)
        pl.when(partner(step) < me)(lambda: settle(step))

    def gather(step):
        epoch = partner(step)
        tile = tile_of(epoch)
        coded(me, epoch).wait_recv()
        seen, share = decode(code_in[epoch])
        value = share * (seen - model_out[epoch])
        for t in range(tile_dev):
            here = (tile == t).astype(f32)
            numer[t] = numer[t] + value * here
            denom[t] = denom[t] + share * here

    if n_epoch <= 4:
        for step in range(1, n_epoch):
            theirs(step)
        if n_epoch > 1:
            pl.when(me == 0)(lambda: mine(1))
        for step in range(n_epoch - 1, 1, -1):
            mine(step)
        if n_epoch > 1:
            pl.when(me > 0)(lambda: mine(1))
        for step in range(1, n_epoch):
            finish(step)
    else:
        lax.fori_loop(1, n_epoch, lambda step, carry: (theirs(step), carry)[1], 0)
        lax.fori_loop(1, n_epoch, lambda step, carry: (mine(step), carry)[1], 0)
        lax.fori_loop(1, n_epoch, lambda step, carry: (finish(step), carry)[1], 0)

    for t in range(tile_dev):
        coadd[t] = numer[t] / (denom[t] + 1.0)

    for u, s, kind in images[1:]:
        guarded(both(u[3], s[3]), lambda u=u, s=s, kind=kind: own_piece(u, s, kind, False).wait_send())
    if n_epoch > 1:
        rest = pl.ds(0, n_epoch - 1)

        def drain(source, kind, u, s):
            copy(source, source, send_sem.at[kind], recv_sem.at[0, kind], device(me, u, s)).wait_send()

        for number in range(1, n_epoch):

            @pl.when(me == number)
            def _(number=number):
                lead = pl.ds(0, number)
                for u, s, kind in images:
                    if u is none and s is none:
                        source = chosen.at[lead]
                    elif s is none:
                        source = chosen_edge.at[u[1], lead]
                    elif u is none:
                        source = chosen_side.at[s[1], lead]
                    else:
                        source = chosen_corner.at[u[1], s[1], lead]
                    guarded(
                        both(u[3], s[3]),
                        lambda u=u, s=s, kind=kind, source=source: drain(source, kind, u, s),
                    )

            @pl.when(me == n_epoch - 1 - number)
            def _(number=number):
                drain(model_out.at[pl.ds(0, number)], MODEL, none, none)

        for held, kind in (
            (offsets_in, OFFS),
            (basis_index_in, INDX),
            (coef_row, COEF),
            (code, CODE),
        ):
            drain(held.at[rest], kind, none, none)


def leave(residual, coadd, residual_out, coadd_out, sem):
    parts = [
        (held.at[i], out.at[i])
        for held, out in ((residual, residual_out), (coadd, coadd_out))
        for i in range(held.shape[0])
    ]
    copies = [pltpu.make_async_copy(held, out, sem.at[i]) for i, (held, out) in enumerate(parts)]
    for one in copies:
        one.start()
    for one in copies:
        one.wait()


def local(sizes, template, science, variance, bad_mask, intersection, offsets, basis_index, coefficients, basis):
    n_epoch, n_strip, n_band = sizes
    tile_dev, height, width = template.shape
    exp_dev = science.shape[0]
    assert exp_dev == n_epoch
    n_poly = coefficients.shape[2]
    n_sel = basis_index.shape[1]
    ks = basis.shape[1]
    n_pairs = (ks + 1) // 2
    far = pl.BlockSpec(memory_space=pltpu.HBM)
    near = pl.BlockSpec(memory_space=pltpu.VMEM)
    free = pl.BlockSpec(memory_space=pl.ANY)
    bf16, f32 = jnp.bfloat16, jnp.float32
    dma = pltpu.SemaphoreType.DMA
    offsets = offsets.T
    coefficients = coefficients.transpose(2, 0, 1)
    basis = basis.transpose(1, 2, 0)
    n_up, n_side = min(n_strip - 1, 2), min(n_band - 1, 2)
    n_image = (1 + n_up) * (1 + n_side)
    edges, sides = max(n_up, 1), max(n_side, 1)
    rim = EDGE_ROWS
    residual, coadd = pl.pallas_call(
        functools.partial(kernel, sizes),
        out_shape=(
            pltpu.VMEM(science.shape, f32),
            pltpu.VMEM(template.shape, f32),
        ),
        in_specs=[far] * 9,
        out_specs=(near, near),
        scratch_shapes=[
            pltpu.SMEM(intersection.shape, jnp.int32),
            pltpu.SMEM(offsets.shape, jnp.int32),
            pltpu.SMEM((n_epoch,) + offsets.shape, jnp.int32),
            pltpu.SMEM(basis_index.shape, jnp.int32),
            pltpu.SMEM((n_epoch,) + basis_index.shape, jnp.int32),
            pltpu.VMEM(coefficients.shape, f32),
            pltpu.VMEM((n_epoch, 1, LANES), f32),
            pltpu.VMEM(template.shape, bf16),
            pltpu.VMEM(science.shape, f32),
            pltpu.VMEM(science.shape, f32),
            pltpu.VMEM(science.shape, jnp.int32),
            pltpu.VMEM(basis.shape, f32),
            pltpu.VMEM((n_epoch, height, width), bf16),
            pltpu.VMEM((edges, n_epoch, rim, width), bf16),
            pltpu.VMEM((sides, n_epoch, 8, LANES), bf16),
            pltpu.VMEM((edges, sides, n_epoch, 8, LANES), bf16),
            pltpu.VMEM((edges, tile_dev, rim, width), bf16),
            pltpu.VMEM((sides, tile_dev, 8, LANES), bf16),
            pltpu.VMEM((edges, sides, tile_dev, 8, LANES), bf16),
            pltpu.VMEM((n_epoch, height, width), bf16),
            pltpu.VMEM((2, n_epoch, rim, width), bf16),
            pltpu.VMEM((2, n_epoch, 8, LANES), bf16),
            pltpu.VMEM((2, 2, n_epoch, 8, LANES), bf16),
            pltpu.VMEM((2, tile_dev, rim, width), bf16),
            pltpu.VMEM((2, tile_dev, 8, LANES), bf16),
            pltpu.VMEM((2, 2, tile_dev, 8, LANES), bf16),
            pltpu.VMEM((exp_dev, 8, LANES), f32),
            pltpu.VMEM((exp_dev, 1, LANES), f32),
            pltpu.VMEM((n_pairs * SLOT, LANES), bf16),
            pltpu.VMEM((8 * exp_dev + 8, n_pairs * SLOT), f32),
            pltpu.VMEM((tile_dev + 1, width // LANES + 1, 2 * rim + height + 8, LANES), f32),
            pltpu.VMEM((exp_dev + 1, n_poly * 8, n_pairs * SLOT), bf16),
            pltpu.VMEM((exp_dev, height, width), f32),
            pltpu.VMEM((n_epoch, height, width), jnp.int32),
            pltpu.VMEM((n_epoch, height, width), jnp.int32),
            pltpu.VMEM((n_epoch, height, width), f32),
            pltpu.VMEM((n_epoch, height, width), f32),
            pltpu.VMEM(template.shape, f32),
            pltpu.VMEM(template.shape, f32),
            dma((9,)),
            dma((n_image + 5,)),
            dma((max(n_epoch - 1, 1), n_image + 5)),
            dma((n_image,)),
            dma((n_image,)),
            pltpu.SemaphoreType.REGULAR((n_epoch,)),
        ],
        compiler_params=pltpu.CompilerParams(
            collective_id=0, has_side_effects=True
        ),
    )(
        intersection, offsets, basis_index, coefficients,
        template, science, variance, bad_mask, basis,
    )
    return pl.pallas_call(
        leave,
        out_shape=(
            jax.ShapeDtypeStruct(science.shape, f32),
            jax.ShapeDtypeStruct(template.shape, f32),
        ),
        in_specs=[near] * 2,
        out_specs=(free, free),
        scratch_shapes=[dma((exp_dev + tile_dev,))],
    )(*(pltpu.with_memory_space_constraint(x, pltpu.VMEM) for x in (residual, coadd)))


def solution(mesh):
    sizes = (mesh.shape["epoch"], mesh.shape["strip"], mesh.shape["band"])
    image = P(("groups", "epoch"), "strip", "band")
    split = ("groups", "epoch")
    in_specs = (
        image, image, image, image, P("groups"),
        P(split, None), P(split, None), P(split, None, None), P(),
    )
    return jax.shard_map(
        functools.partial(local, sizes),
        mesh=mesh,
        in_specs=in_specs,
        out_specs=(image, image),
        check_vma=False,
    )
```

```python
import functools

import jax
import jax.numpy as jnp
from jax import lax
from jax.experimental import pallas as pl
from jax.experimental.pallas import tpu as pltpu
from jax.sharding import PartitionSpec as P

HALF = 9
SHIFT = 4
EDGE_ROWS = 16
LANES = 128
SLOT = 64
GROUPS = 4
SIDE = 16
SCIENCE_TOP = 6.0
WEIGHT_TOP = 0.5
LEVELS = 65535.0

MESH = pl.DeviceIdType.MESH


def links_of(size, place):
    if size == 1:
        return []
    if size == 2:
        return [(1 - 2 * place, 0, place, None, None)]
    return [
        (-1, 0, 1, place > 0, place < size - 1),
        (1, 1, 0, place < size - 1, place > 0),
    ]


def both(first, second):
    if first is None:
        return second
    if second is None:
        return first
    return jnp.logical_and(first, second)


def guarded(side, body):
    if side is None:
        body()
    else:
        pl.when(side)(body)


def encode(science, weight):
    high = (science + SCIENCE_TOP) * (LEVELS / (2.0 * SCIENCE_TOP)) + 0.5
    low = weight * (LEVELS / WEIGHT_TOP) + 0.5
    high = jnp.clip(high, 0.0, LEVELS).astype(jnp.int32)
    low = jnp.clip(low, 0.0, LEVELS).astype(jnp.int32)
    return jnp.bitwise_or(jnp.left_shift(high, 16), low)


def decode(code):
    high = lax.shift_right_logical(code, jnp.full(code.shape, 16, jnp.int32))
    low = jnp.bitwise_and(code, 65535)
    science = high.astype(jnp.float32) * (2.0 * SCIENCE_TOP / LEVELS) - SCIENCE_TOP
    return science, low.astype(jnp.float32) * (WEIGHT_TOP / LEVELS)


def kernel(
    sizes,
    intersection_hbm,
    offsets_hbm,
    basis_index_hbm,
    coefficients_hbm,
    template_hbm,
    science_hbm,
    variance_hbm,
    bad_mask_hbm,
    basis_hbm,
    residual,
    coadd,
    intersection,
    offsets,
    offsets_in,
    basis_index,
    basis_index_in,
    coefficients,
    coefs_in,
    template,
    science,
    variance,
    bad_mask,
    basis,
    chosen,
    chosen_edge,
    chosen_side,
    chosen_corner,
    own_edge,
    own_side,
    own_diagonal,
    centre,
    vertical,
    lateral,
    corner,
    own_vertical,
    own_lateral,
    own_corner,
    coefs,
    coef_row,
    table,
    kernels,
    slab,
    toeplitz,
    weight,
    code,
    code_in,
    model_out,
    model_in,
    numer,
    denom,
    local_sem,
    send_sem,
    recv_sem,
    own_send,
    own_recv,
    token,
):
    n_epoch, n_strip, n_band = sizes
    tile_dev, height, width = template.shape
    exp_dev = science.shape[0]
    n_poly, _, n_sel = coefficients.shape
    ks, _, n_basis = basis.shape
    n_lane = width // LANES
    half = LANES // 2
    f32, bf16 = jnp.float32, jnp.bfloat16
    group = lax.axis_index("groups")
    me = lax.axis_index("epoch")
    strip = lax.axis_index("strip")
    band = lax.axis_index("band")

    ups = links_of(n_strip, strip)
    sides = links_of(n_band, band)
    none = (0, None, None, None, None)
    near = [(u, s) for u in [none] + ups for s in [none] + sides]

    def device(epoch, u, s):
        return (group, epoch, strip + u[0], band + s[0])

    loads = [
        pltpu.make_async_copy(held, here, local_sem.at[i])
        for i, (held, here) in enumerate(
            (
                (intersection_hbm, intersection),
                (template_hbm, template),
                (variance_hbm, variance),
                (bad_mask_hbm, bad_mask),
                (science_hbm, science),
                (coefficients_hbm, coefficients),
                (basis_index_hbm, basis_index),
                (basis_hbm, basis),
                (offsets_hbm, offsets),
            )
        )
    ]
    for load in loads:
        load.start()

    def count(size, place):
        if size < 3:
            return size
        return 1 + jnp.minimum(place, 1) + jnp.minimum(size - 1 - place, 1)

    def before(size, place):
        return place if size < 3 else jnp.minimum(place, 1)

    across = count(n_band, band)
    partners = count(n_strip, strip) * across
    ahead_of_me = before(n_strip, strip) * across + before(n_band, band)

    def lower(u, s):
        if u is not none:
            return strip + u[0] < strip
        return band + s[0] < band

    barrier = pltpu.get_barrier_semaphore()

    def signal(sem, epoch, u, s):
        pl.semaphore_signal(sem, inc=1, device_id=device(epoch, u, s), device_id_type=MESH)

    def to_epoch(sem, epoch):
        for u, s in near:
            guarded(both(u[3], s[3]), lambda u=u, s=s: signal(sem, epoch, u, s))

    for u, s in near[1:]:
        guarded(
            both(both(u[3], s[3]), jnp.logical_not(lower(u, s))),
            lambda u=u, s=s: signal(barrier, me, u, s),
        )
    for step in range(1, n_epoch):
        pl.when(me + step < n_epoch)(lambda step=step: to_epoch(barrier, me + step))
    met = partners * me + ahead_of_me

    @pl.when(met > 0)
    def _():
        pl.semaphore_wait(barrier, met)

    for u, s in near[1:]:
        guarded(
            both(both(u[3], s[3]), lower(u, s)),
            lambda u=u, s=s: signal(token.at[me], me, u, s),
        )
    for epoch in range(n_epoch - 1):
        pl.when(epoch < me)(lambda epoch=epoch: signal(token.at[me], epoch, none, none))

    def slot_of(sender, receiver):
        return sender - (sender > receiver).astype(jnp.int32)

    lane = lax.broadcasted_iota(jnp.int32, (8, LANES), 1)
    sub = lax.broadcasted_iota(jnp.int32, (8, LANES), 0)

    def within(base):
        return jnp.bitwise_and(lane - base, LANES - 1) < SIDE

    def side_tile(wide, which):
        first, last = wide[:, :LANES], wide[:, width - LANES :]
        if n_band == 2:
            return jnp.where(band == 0, last, first), (1 - band) * (LANES - SIDE)
        return (first, 0) if which == 0 else (last, LANES - SIDE)

    def packed(wide, which):
        tile, base = side_tile(wide, which)
        out = jnp.zeros((8, LANES), f32)
        for i in range(wide.shape[0] // 8):
            part = tile[8 * i : 8 * i + 8]
            if i > 0:
                part = pltpu.roll(part, SIDE * i, 1)
            out = jnp.where(within(base + SIDE * i), part, out)
        return out.astype(bf16)

    def copy(source, dest, sent, received, to):
        return pltpu.make_async_remote_copy(
            src_ref=source,
            dst_ref=dest,
            send_sem=sent,
            recv_sem=received,
            device_id=to,
            device_id_type=MESH,
        )

    n_up, n_side = len(ups), len(sides)
    images = []
    for u, s in near:
        i = 0 if u is none else 1 + ups.index(u)
        j = 0 if s is none else 1 + sides.index(s)
        images.append((u, s, i * (1 + n_side) + j))
    n_image = (1 + n_up) * (1 + n_side)
    CODE, COEF, OFFS, INDX, MODEL = (n_image + i for i in range(5))

    def image(epoch, u, s, kind, sender, at=None):
        source_at = epoch if at is None else at
        if u is none and s is none:
            source, dest = chosen.at[source_at], centre.at[sender]
        elif s is none:
            source, dest = chosen_edge.at[u[1], source_at], vertical.at[u[2], sender]
        elif u is none:
            source, dest = chosen_side.at[s[1], source_at], lateral.at[s[2], sender]
        else:
            source = chosen_corner.at[u[1], s[1], source_at]
            dest = corner.at[u[2], s[2], sender]
        return copy(
            source, dest, send_sem.at[kind], recv_sem.at[slot_of(sender, epoch), kind], device(epoch, u, s)
        )

    def arriving(epoch, u, s, kind):
        if u is none and s is none:
            dest = centre.at[epoch]
        elif s is none:
            dest = vertical.at[u[2], epoch]
        elif u is none:
            dest = lateral.at[s[2], epoch]
        else:
            dest = corner.at[u[2], s[2], epoch]
        return copy(dest, dest, send_sem.at[kind], recv_sem.at[slot_of(epoch, me), kind], device(epoch, u, s))

    def landing(links, place, size):
        if size == 2:
            return [(k[0], k[1], 1 - place, None, None) for k in links]
        return [(k[0], k[1], k[2], k[4], k[3]) for k in links]

    ups_in = landing(ups, strip, n_strip)
    sides_in = landing(sides, band, n_band)
    images_in = []
    for u, s, kind in images:
        a = none if u is none else ups_in[ups.index(u)]
        b = none if s is none else sides_in[sides.index(s)]
        images_in.append((a, b, kind))

    def send_image(epoch):
        for u, s, kind in images:
            guarded(
                both(u[3], s[3]), lambda u=u, s=s, kind=kind: image(epoch, u, s, kind, me).start()
            )

    def wait_image(epoch):
        for u, s, kind in images_in:
            guarded(
                both(u[3], s[3]), lambda u=u, s=s, kind=kind: arriving(epoch, u, s, kind).wait_recv()
            )

    def small(epoch, sender):
        return [
            copy(held, into.at[sender], send_sem.at[kind], recv_sem.at[slot_of(sender, epoch), kind], device(epoch, none, none))
            for held, into, kind in (
                (offsets_hbm, offsets_in, OFFS),
                (basis_index_hbm, basis_index_in, INDX),
            )
        ]

    def coefficient_tile(epoch, sender):
        return copy(
            coef_row.at[epoch], coefs_in.at[sender], send_sem.at[COEF], recv_sem.at[slot_of(sender, epoch), COEF],
            device(epoch, none, none),
        )

    def coded(epoch, sender):
        return copy(
            code.at[epoch], code_in.at[sender], send_sem.at[CODE], recv_sem.at[slot_of(sender, epoch), CODE],
            device(epoch, none, none),
        )

    def returned(epoch, sender):
        return copy(
            model_out.at[epoch], model_in.at[sender], send_sem.at[MODEL], recv_sem.at[slot_of(sender, epoch), MODEL],
            device(epoch, none, none),
        )

    def own_piece(u, s, kind, incoming):
        if s is none:
            source, dest = own_edge.at[0 if incoming else u[1]], own_vertical.at[u[2]]
        elif u is none:
            source, dest = own_side.at[0 if incoming else s[1]], own_lateral.at[s[2]]
        else:
            source = own_diagonal.at[0 if incoming else u[1], 0 if incoming else s[1]]
            dest = own_corner.at[u[2], s[2]]
        if incoming:
            source = dest
        return copy(source, dest, own_send.at[kind], own_recv.at[kind], device(me, u, s))

    def send_small(epoch):
        for one in small(epoch, me):
            one.start()

    for epoch in range(n_epoch - 1):
        pl.when(epoch < me)(lambda epoch=epoch: send_small(epoch))

    loads[0].wait()
    loads[1].wait()

    def rim(wide, which):
        low, high = wide[:EDGE_ROWS], wide[height - EDGE_ROWS :]
        if n_strip == 2:
            return jnp.where(strip == 0, high, low)
        return low if which == 0 else high

    for epoch in range(n_epoch):
        tile = intersection[epoch * exp_dev + me] - me * tile_dev
        picked = template[jnp.clip(tile, 0, tile_dev - 1)]
        chosen[epoch] = picked
        wide = picked.astype(f32)
        for side in range(n_side):
            chosen_side[side, epoch] = packed(wide, side)
        for which in range(n_up):
            edge = rim(wide, which)
            chosen_edge[which, epoch] = edge.astype(bf16)
            for side in range(n_side):
                chosen_corner[which, side, epoch] = packed(edge, side)
    loads[5].wait()
    for exposure in range(exp_dev):
        coefs[exposure] = jnp.zeros((8, LANES), f32)
        for p in range(n_poly):
            coefs[exposure, p : p + 1, 0:n_sel] = coefficients[p, exposure : exposure + 1, :]
        coef_row[exposure] = jnp.sum(
            pltpu.roll(coefs[exposure], 0, 1, stride=n_sel, stride_axis=0), axis=0, keepdims=True
        )

    for epoch in range(n_epoch - 1):
        pl.when(epoch < me)(lambda epoch=epoch: coefficient_tile(epoch, me).start())
    pl.when(me > 0)(lambda: send_image(0))
    loads[2].wait()
    loads[3].wait()
    loads[4].wait()
    for epoch in range(n_epoch):
        share = bad_mask[epoch].astype(f32) / variance[epoch]
        weight[epoch] = share
        code[epoch] = encode(science[epoch], share)
    for epoch in range(n_epoch - 1):

        @pl.when(epoch < me)
        def _(epoch=epoch):
            if epoch > 0:
                send_image(epoch)
            coded(epoch, me).start()

    for t in range(tile_dev):
        wide = template[t].astype(f32)
        for side in range(n_side):
            own_side[side, t] = packed(wide, side)
        for which in range(n_up):
            edge = rim(wide, which)
            own_edge[which, t] = edge.astype(bf16)
            for side in range(n_side):
                own_diagonal[which, side, t] = packed(edge, side)
    for u, s, kind in images[1:]:
        guarded(
            both(both(u[3], s[3]), lower(u, s)),
            lambda u=u, s=s, kind=kind: own_piece(u, s, kind, False).start(),
        )

    def clear(ref):
        ref[...] = jnp.zeros(ref.shape, ref.dtype)

    def clear_up(slot):
        clear(vertical.at[slot])
        clear(own_vertical.at[slot])

    def clear_side(slot):
        clear(lateral.at[slot])
        clear(own_lateral.at[slot])

    def clear_corner(slot, at):
        clear(corner.at[slot, at])
        clear(own_corner.at[slot, at])

    if n_strip == 1:
        clear(vertical)
        clear(own_vertical)
        clear(corner)
        clear(own_corner)
    elif n_strip == 2:
        clear_up(strip)
        for at in range(2):
            clear_corner(strip, at)
    else:
        for slot, edge in ((0, strip == 0), (1, strip == n_strip - 1)):

            @pl.when(edge)
            def _(slot=slot):
                clear_up(slot)
                for at in range(2):
                    clear_corner(slot, at)

    if n_band == 1:
        clear(lateral)
        clear(own_lateral)
        if n_strip > 1:
            clear(corner)
            clear(own_corner)
    elif n_band == 2:
        clear_side(band)
        if n_strip == 2:
            clear_corner(1 - strip, band)
        elif n_strip > 2:
            for slot, held in ((0, strip > 0), (1, strip < n_strip - 1)):
                pl.when(held)(lambda slot=slot: clear_corner(slot, band))
    else:
        for slot, edge in ((0, band == 0), (1, band == n_band - 1)):

            @pl.when(edge)
            def _(slot=slot):
                clear_side(slot)
                for at in range(2):
                    clear_corner(at, slot)

    slab[:, :, height + 2 * EDGE_ROWS :, :] = jnp.zeros(
        (slab.shape[0], slab.shape[1], 8, LANES), f32
    )

    n_pairs = (ks + 1) // 2
    n_tiles = n_pairs * SLOT // LANES
    later = jnp.bitwise_and(lane, 7) >= sub

    def mix_of(some, indices):
        parts = []
        for j in range(n_sel):
            column = jnp.broadcast_to(some[:, j : j + 1], (8, LANES))
            parts.append(jnp.where(lane == indices(j), column, 0.0))
        while len(parts) > 1:
            parts = [
                parts[i] + parts[i + 1] if i + 1 < len(parts) else parts[i]
                for i in range(0, len(parts), 2)
            ]
        mix = jnp.where(sub < n_poly, parts[0], 0.0)
        mix = mix + pltpu.roll(mix, half, 1)
        high = mix.astype(bf16).astype(f32)
        return high, mix - high

    def unpacked(line):
        wide = jnp.broadcast_to(line, (8, LANES))
        out = wide
        for p in range(1, n_poly):
            out = jnp.where(sub == p, pltpu.roll(wide, LANES - n_sel * p, 1), out)
        return out

    def mixed(pairs):
        rows = jnp.concatenate([p[0] for p in pairs] + [p[1] for p in pairs], axis=0)
        out = lax.dot_general(
            rows.astype(bf16), table[...], (((1,), (1,)), ((), ())), preferred_element_type=f32
        )
        size = 8 * len(pairs)
        return (out[:size] + out[size:]).astype(bf16).astype(f32)

    def spread(row, into):
        for p in range(0, n_poly, 2):
            for t in range(n_tiles):
                halves = []
                for h in range(2):
                    at = row * 8 + p + h
                    wide = jnp.broadcast_to(
                        kernels[at : at + 1, t * LANES : (t + 1) * LANES], (8, LANES)
                    )
                    close = pltpu.roll(wide, 0, 1, stride=1, stride_axis=0)
                    far = pltpu.roll(wide, 8, 1, stride=1, stride_axis=0)
                    halves.append(jnp.where(later, close, far))
                toeplitz[into, p * 8 : (p + 2) * 8, t * LANES : (t + 1) * LANES] = (
                    jnp.concatenate(halves, axis=0).astype(bf16)
                )

    loads[6].wait()
    pairs = [
        mix_of(
            coefs[exposure],
            lambda j, exposure=exposure: basis_index[exposure, j],
        )
        for exposure in range(exp_dev)
    ]

    loads[7].wait()
    blank = jnp.zeros((8, LANES), f32)

    def taps(b, g):
        if b >= ks or g * 8 >= ks:
            return blank
        here = min(8, ks - g * 8)
        tile = basis[g * 8 : g * 8 + here, b, :]
        if here < 8:
            tile = jnp.concatenate([tile, jnp.zeros((8 - here, n_basis), f32)], axis=0)
        tile = jnp.concatenate([tile, jnp.zeros((8, LANES - n_basis), f32)], axis=1)
        high = tile.astype(bf16).astype(f32)
        return jnp.where(lane < half, high, pltpu.roll(tile - high, half, 1))

    table[...] = jnp.concatenate(
        [
            taps(2 * q + h, g)
            for q in range(n_pairs)
            for g in range(GROUPS)
            for h in range(2)
        ],
        axis=0,
    ).astype(bf16)
    kernels[0 : 8 * exp_dev] = mixed(pairs)
    loads[8].wait()
    for exposure in range(exp_dev):
        spread(exposure, exposure)

    row = lax.broadcasted_iota(jnp.int32, (height, 1), 0) + strip * height
    col = lax.broadcasted_iota(jnp.int32, (1, width), 1) + band * width
    r = (2.0 * row.astype(f32) + 1.0) / (height * n_strip) - 1.0
    c = (2.0 * col.astype(f32) + 1.0) / (width * n_band) - 1.0
    r = jnp.broadcast_to(r, (height, width))
    c = jnp.broadcast_to(c, (height, width))

    span = height + 8 * GROUPS - 8
    at_lane = lax.broadcasted_iota(jnp.int32, (span, LANES), 1)

    beside = [(0, LANES - SIDE), (1, 0)]
    if n_band == 2:
        beside = [(1 - band, band * (LANES - SIDE))]

    def lay(board, middle, up, side, edge, at):
        for rows, body, rims in (
            (0, up(0), [(edge(0, k).astype(f32), base) for k, base in beside]),
            (EDGE_ROWS, middle, [(side(k).astype(f32), base) for k, base in beside]),
            (EDGE_ROWS + height, up(1), [(edge(1, k).astype(f32), base) for k, base in beside]),
        ):
            wide = body.astype(f32)
            size = wide.shape[0]
            for t in range(n_lane):
                slab[board, t, rows : rows + size, :] = wide[:, t * LANES : (t + 1) * LANES]
            for i in range(size // 8):
                part = jnp.zeros((8, LANES), f32)
                for held, base in rims:
                    turned = held if i == 0 else pltpu.roll(held, LANES - SIDE * i, 1)
                    part = jnp.where(within(base), turned, part)
                slab[board, n_lane, rows + 8 * i : rows + 8 * i + 8, :] = part

    def lay_own(board, tile):
        lay(
            board,
            template[tile],
            lambda v: own_vertical[v, tile],
            lambda s: own_lateral[s, tile],
            lambda v, s: own_corner[v, s, tile],
            tile,
        )

    def lay_other(board, epoch):
        lay(
            board,
            centre[epoch],
            lambda v: vertical[v, epoch],
            lambda s: lateral[s, epoch],
            lambda v, s: corner[v, s, epoch],
            epoch,
        )

    def models(board, factor, down, along):
        views = []
        for h in range(2):
            turned = [
                pltpu.roll(slab[board, t, pl.ds(down, span), :], along - h, 1)
                for t in range(n_lane + 1)
            ]
            views.append(
                jnp.concatenate(
                    [
                        jnp.where(at_lane < along - h, turned[t - 1], turned[t])
                        for t in range(n_lane + 1)
                    ],
                    axis=1,
                )
            )
        tiles = [
            jnp.concatenate(
                [views[0][g * 8 : g * 8 + 8], views[1][g * 8 : g * 8 + 8]], axis=0
            ).astype(bf16)
            for g in range(span // 8)
        ]
        moved = [[tile[:, 2 * q : 2 * q + width] for tile in tiles] for q in range(n_pairs)]
        for block in range(height // 8):
            stacked = jnp.concatenate(
                [moved[q][block + g] for q in range(n_pairs) for g in range(GROUPS)], axis=0
            )
            conv = jnp.dot(factor, stacked, preferred_element_type=f32)
            q = [conv[p * 8 : (p + 1) * 8] for p in range(n_poly)]
            at = slice(block * 8, block * 8 + 8)
            rr, cc = r[at], c[at]
            yield at, q[0] + rr * (q[1] + rr * q[3] + cc * q[4]) + cc * (q[2] + cc * q[5])

    def tile_of(epoch):
        return intersection[epoch * exp_dev + me] - me * tile_dev

    def down_of(shift):
        return EDGE_ROWS - HALF + shift

    def along_of(shift):
        return HALF - shift

    behind = partners - 1 - ahead_of_me

    @pl.when(behind > 0)
    def _():
        pl.semaphore_wait(token.at[me], behind)

    for u, s, kind in images[1:]:
        guarded(
            both(both(u[3], s[3]), jnp.logical_not(lower(u, s))),
            lambda u=u, s=s, kind=kind: own_piece(u, s, kind, False).start(),
        )
    def offer(step):
        @pl.when(me + step < n_epoch)
        def _(epoch=me + step):
            pl.semaphore_wait(token.at[epoch], 1)
            send_small(epoch)
            coefficient_tile(epoch, me).start()
            coded(epoch, me).start()

    early = n_epoch - 2 if n_epoch == 4 else n_epoch - 1
    for step in range(1, early + 1):
        offer(step)

    for u, s, kind in images_in[1:]:
        guarded(both(u[3], s[3]), lambda u=u, s=s, kind=kind: own_piece(u, s, kind, True).wait_recv())

    def own_board(tile):
        return jnp.clip(tile, 0, tile_dev - 1)

    def first():
        tile = tile_of(me)
        for at, model in models(own_board(tile), toeplitz[me], down_of(offsets[0, me]), along_of(offsets[1, me])):
            left = science[me, at] - model
            residual[me, at] = left
            share = weight[me, at]
            for t in range(tile_dev):
                here = (tile == t).astype(f32)
                numer[t, at] = share * left * here
                denom[t, at] = share * here

    def lay_tiles():
        for t in range(tile_dev):
            lay_own(t, t)

    def partner(step):
        return jnp.where(me + step < n_epoch, me + step, n_epoch - 1 - step)

    def theirs(step):
        epoch = partner(step)
        last = exp_dev
        kernels[8 * last : 8 * last + 8] = mixed(
            [mix_of(unpacked(coefs_in[epoch]), lambda j: basis_index_in[epoch, me, j])]
        )
        spread(last, last)
        for at, model in models(
            own_board(tile_of(epoch)),
            toeplitz[last],
            down_of(offsets_in[epoch, 0, me]),
            along_of(offsets_in[epoch, 1, me]),
        ):
            model_out[epoch, at] = model

    def wait_small(step):
        epoch = partner(step)
        for one in small(me, epoch) + [coefficient_tile(me, epoch)]:
            one.wait_recv()

    def answer(step):
        pl.when(partner(step) > me)(lambda: returned(partner(step), me).start())

    def host(step):
        wait_small(step)
        theirs(step)
        answer(step)

    def ours(step):
        epoch = partner(step)
        board = tile_dev + step - 1 if isinstance(step, int) else tile_dev
        lay_other(board, epoch)
        for at, model in models(
            board, toeplitz[epoch], down_of(offsets[0, epoch]), along_of(offsets[1, epoch])
        ):
            residual[epoch, at] = science[epoch, at] - model

    def settle(step):
        epoch = partner(step)
        returned(me, epoch).wait_recv()
        residual[epoch] = science[epoch] - model_in[epoch]

    def mine(step):
        @pl.when(partner(step) > me)
        def _():
            wait_image(partner(step))
            ours(step)

    def finish(step):
        gather(step)
        pl.when(partner(step) < me)(lambda: settle(step))

    def gather(step):
        epoch = partner(step)
        tile = tile_of(epoch)
        coded(me, epoch).wait_recv()
        seen, share = decode(code_in[epoch])
        value = share * (seen - model_out[epoch])
        for t in range(tile_dev):
            here = (tile == t).astype(f32)
            numer[t] = numer[t] + value * here
            denom[t] = denom[t] + share * here

    if n_epoch == 4:

        @pl.when(me == 0)
        def _():
            wait_small(1)
            lay_tiles()
            theirs(1)
            first()
            answer(1)
            offer(3)
            wait_small(2)
            wait_image(1)
            theirs(2)
            ours(1)
            answer(2)
            host(3)
            wait_image(3)
            ours(3)
            wait_image(2)
            ours(2)

        @pl.when(me > 0)
        def _():
            lay_tiles()
            first()
            for step in range(1, n_epoch):
                host(step)
            for step in range(2, 0, -1):
                mine(step)

        for step in range(1, n_epoch):
            finish(step)
    else:
        lay_tiles()
        first()

        def walk(stage):
            lax.fori_loop(1, n_epoch, lambda step, carry: (stage(step), carry)[1], 0)

        walk(host)
        walk(mine)
        walk(finish)

    for t in range(tile_dev):
        coadd[t] = numer[t] / (denom[t] + 1.0)

    for u, s, kind in images[1:]:
        guarded(both(u[3], s[3]), lambda u=u, s=s, kind=kind: own_piece(u, s, kind, False).wait_send())
    if n_epoch > 1:
        rest = pl.ds(0, n_epoch - 1)

        def drain(source, kind, u, s):
            copy(source, source, send_sem.at[kind], recv_sem.at[0, kind], device(me, u, s)).wait_send()

        for number in range(1, n_epoch):

            @pl.when(me == number)
            def _(number=number):
                lead = pl.ds(0, number)
                for u, s, kind in images:
                    if u is none and s is none:
                        source = chosen.at[lead]
                    elif s is none:
                        source = chosen_edge.at[u[1], lead]
                    elif u is none:
                        source = chosen_side.at[s[1], lead]
                    else:
                        source = chosen_corner.at[u[1], s[1], lead]
                    guarded(
                        both(u[3], s[3]),
                        lambda u=u, s=s, kind=kind, source=source: drain(source, kind, u, s),
                    )

            @pl.when(me == n_epoch - 1 - number)
            def _(number=number):
                drain(model_out.at[pl.ds(0, number)], MODEL, none, none)

        for held, kind in (
            (offsets_in, OFFS),
            (basis_index_in, INDX),
            (coef_row, COEF),
            (code, CODE),
        ):
            drain(held.at[rest], kind, none, none)


def leave(residual, coadd, residual_out, coadd_out, sem):
    parts = [
        (held.at[i], out.at[i])
        for held, out in ((residual, residual_out), (coadd, coadd_out))
        for i in range(held.shape[0])
    ]
    copies = [pltpu.make_async_copy(held, out, sem.at[i]) for i, (held, out) in enumerate(parts)]
    for one in copies:
        one.start()
    for one in copies:
        one.wait()


def local(sizes, template, science, variance, bad_mask, intersection, offsets, basis_index, coefficients, basis):
    n_epoch, n_strip, n_band = sizes
    tile_dev, height, width = template.shape
    exp_dev = science.shape[0]
    assert exp_dev == n_epoch
    n_poly = coefficients.shape[2]
    n_sel = basis_index.shape[1]
    ks = basis.shape[1]
    n_pairs = (ks + 1) // 2
    far = pl.BlockSpec(memory_space=pltpu.HBM)
    near = pl.BlockSpec(memory_space=pltpu.VMEM)
    free = pl.BlockSpec(memory_space=pl.ANY)
    bf16, f32 = jnp.bfloat16, jnp.float32
    dma = pltpu.SemaphoreType.DMA
    offsets = offsets.T
    coefficients = coefficients.transpose(2, 0, 1)
    basis = basis.transpose(1, 2, 0)
    n_up, n_side = min(n_strip - 1, 2), min(n_band - 1, 2)
    n_image = (1 + n_up) * (1 + n_side)
    edges, sides = max(n_up, 1), max(n_side, 1)
    rim = EDGE_ROWS
    residual, coadd = pl.pallas_call(
        functools.partial(kernel, sizes),
        out_shape=(
            pltpu.VMEM(science.shape, f32),
            pltpu.VMEM(template.shape, f32),
        ),
        in_specs=[far] * 9,
        out_specs=(near, near),
        scratch_shapes=[
            pltpu.SMEM(intersection.shape, jnp.int32),
            pltpu.SMEM(offsets.shape, jnp.int32),
            pltpu.SMEM((n_epoch,) + offsets.shape, jnp.int32),
            pltpu.SMEM(basis_index.shape, jnp.int32),
            pltpu.SMEM((n_epoch,) + basis_index.shape, jnp.int32),
            pltpu.VMEM(coefficients.shape, f32),
            pltpu.VMEM((n_epoch, 1, LANES), f32),
            pltpu.VMEM(template.shape, bf16),
            pltpu.VMEM(science.shape, f32),
            pltpu.VMEM(science.shape, f32),
            pltpu.VMEM(science.shape, jnp.int32),
            pltpu.VMEM(basis.shape, f32),
            pltpu.VMEM((n_epoch, height, width), bf16),
            pltpu.VMEM((edges, n_epoch, rim, width), bf16),
            pltpu.VMEM((sides, n_epoch, 8, LANES), bf16),
            pltpu.VMEM((edges, sides, n_epoch, 8, LANES), bf16),
            pltpu.VMEM((edges, tile_dev, rim, width), bf16),
            pltpu.VMEM((sides, tile_dev, 8, LANES), bf16),
            pltpu.VMEM((edges, sides, tile_dev, 8, LANES), bf16),
            pltpu.VMEM((n_epoch, height, width), bf16),
            pltpu.VMEM((2, n_epoch, rim, width), bf16),
            pltpu.VMEM((2, n_epoch, 8, LANES), bf16),
            pltpu.VMEM((2, 2, n_epoch, 8, LANES), bf16),
            pltpu.VMEM((2, tile_dev, rim, width), bf16),
            pltpu.VMEM((2, tile_dev, 8, LANES), bf16),
            pltpu.VMEM((2, 2, tile_dev, 8, LANES), bf16),
            pltpu.VMEM((exp_dev, 8, LANES), f32),
            pltpu.VMEM((exp_dev, 1, LANES), f32),
            pltpu.VMEM((n_pairs * SLOT, LANES), bf16),
            pltpu.VMEM((8 * exp_dev + 8, n_pairs * SLOT), f32),
            pltpu.VMEM((tile_dev + max(n_epoch - 1, 1), width // LANES + 1, 2 * rim + height + 8, LANES), f32),
            pltpu.VMEM((exp_dev + 1, n_poly * 8, n_pairs * SLOT), bf16),
            pltpu.VMEM((exp_dev, height, width), f32),
            pltpu.VMEM((n_epoch, height, width), jnp.int32),
            pltpu.VMEM((n_epoch, height, width), jnp.int32),
            pltpu.VMEM((n_epoch, height, width), f32),
            pltpu.VMEM((n_epoch, height, width), f32),
            pltpu.VMEM(template.shape, f32),
            pltpu.VMEM(template.shape, f32),
            dma((9,)),
            dma((n_image + 5,)),
            dma((max(n_epoch - 1, 1), n_image + 5)),
            dma((n_image,)),
            dma((n_image,)),
            pltpu.SemaphoreType.REGULAR((n_epoch,)),
        ],
        compiler_params=pltpu.CompilerParams(
            collective_id=0, has_side_effects=True
        ),
    )(
        intersection, offsets, basis_index, coefficients,
        template, science, variance, bad_mask, basis,
    )
    return pl.pallas_call(
        leave,
        out_shape=(
            jax.ShapeDtypeStruct(science.shape, f32),
            jax.ShapeDtypeStruct(template.shape, f32),
        ),
        in_specs=[near] * 2,
        out_specs=(free, free),
        scratch_shapes=[dma((exp_dev + tile_dev,))],
    )(*(pltpu.with_memory_space_constraint(x, pltpu.VMEM) for x in (residual, coadd)))


def solution(mesh):
    sizes = (mesh.shape["epoch"], mesh.shape["strip"], mesh.shape["band"])
    image = P(("groups", "epoch"), "strip", "band")
    split = ("groups", "epoch")
    in_specs = (
        image, image, image, image, P("groups"),
        P(split, None), P(split, None), P(split, None, None), P(),
    )
    return jax.shard_map(
        functools.partial(local, sizes),
        mesh=mesh,
        in_specs=in_specs,
        out_specs=(image, image),
        check_vma=False,
    )
```

```python
import functools

import jax
import jax.numpy as jnp
from jax import lax
from jax.experimental import pallas as pl
from jax.experimental.pallas import tpu as pltpu
from jax.sharding import PartitionSpec as P

HALF = 9
SHIFT = 4
EDGE_ROWS = 16
LANES = 128
SLOT = 64
GROUPS = 4
SIDE = 16
SCIENCE_TOP = 6.0
WEIGHT_TOP = 0.5
LEVELS = 65535.0

MESH = pl.DeviceIdType.MESH


def links_of(size, place):
    if size == 1:
        return []
    if size == 2:
        return [(1 - 2 * place, 0, place, None, None)]
    return [
        (-1, 0, 1, place > 0, place < size - 1),
        (1, 1, 0, place < size - 1, place > 0),
    ]


def both(first, second):
    if first is None:
        return second
    if second is None:
        return first
    return jnp.logical_and(first, second)


def guarded(side, body):
    if side is None:
        body()
    else:
        pl.when(side)(body)


def encode(science, weight):
    high = (science + SCIENCE_TOP) * (LEVELS / (2.0 * SCIENCE_TOP)) + 0.5
    low = weight * (LEVELS / WEIGHT_TOP) + 0.5
    high = jnp.clip(high, 0.0, LEVELS).astype(jnp.int32)
    low = jnp.clip(low, 0.0, LEVELS).astype(jnp.int32)
    return jnp.bitwise_or(jnp.left_shift(high, 16), low)


def decode(code):
    high = lax.shift_right_logical(code, jnp.full(code.shape, 16, jnp.int32))
    low = jnp.bitwise_and(code, 65535)
    science = high.astype(jnp.float32) * (2.0 * SCIENCE_TOP / LEVELS) - SCIENCE_TOP
    return science, low.astype(jnp.float32) * (WEIGHT_TOP / LEVELS)


def kernel(
    sizes,
    intersection_hbm,
    offsets_hbm,
    basis_index_hbm,
    coefficients_hbm,
    template_hbm,
    science_hbm,
    variance_hbm,
    bad_mask_hbm,
    basis_hbm,
    residual,
    coadd,
    intersection,
    offsets,
    offsets_in,
    basis_index,
    basis_index_in,
    coefficients,
    coefs_in,
    template,
    science,
    variance,
    bad_mask,
    basis,
    chosen,
    chosen_edge,
    chosen_side,
    chosen_corner,
    own_edge,
    own_side,
    own_diagonal,
    centre,
    vertical,
    lateral,
    corner,
    own_vertical,
    own_lateral,
    own_corner,
    coefs,
    coef_row,
    table,
    kernels,
    slab,
    toeplitz,
    weight,
    code,
    code_in,
    model_out,
    model_in,
    numer,
    denom,
    local_sem,
    send_sem,
    recv_sem,
    own_send,
    own_recv,
    token,
):
    n_epoch, n_strip, n_band = sizes
    tile_dev, height, width = template.shape
    exp_dev = science.shape[0]
    n_poly, _, n_sel = coefficients.shape
    ks, _, n_basis = basis.shape
    n_lane = width // LANES
    half = LANES // 2
    f32, bf16 = jnp.float32, jnp.bfloat16
    group = lax.axis_index("groups")
    me = lax.axis_index("epoch")
    strip = lax.axis_index("strip")
    band = lax.axis_index("band")

    ups = links_of(n_strip, strip)
    sides = links_of(n_band, band)
    none = (0, None, None, None, None)
    near = [(u, s) for u in [none] + ups for s in [none] + sides]

    def device(epoch, u, s):
        return (group, epoch, strip + u[0], band + s[0])

    loads = [
        pltpu.make_async_copy(held, here, local_sem.at[i])
        for i, (held, here) in enumerate(
            (
                (intersection_hbm, intersection),
                (template_hbm, template),
                (variance_hbm, variance),
                (bad_mask_hbm, bad_mask),
                (science_hbm, science),
                (coefficients_hbm, coefficients),
                (basis_index_hbm, basis_index),
                (basis_hbm, basis),
                (offsets_hbm, offsets),
            )
        )
    ]
    for i in (5, 6, 8, 0, 1, 2, 3, 4, 7):
        loads[i].start()

    def count(size, place):
        if size < 3:
            return size
        return 1 + jnp.minimum(place, 1) + jnp.minimum(size - 1 - place, 1)

    def before(size, place):
        return place if size < 3 else jnp.minimum(place, 1)

    across = count(n_band, band)
    partners = count(n_strip, strip) * across
    ahead_of_me = before(n_strip, strip) * across + before(n_band, band)

    def lower(u, s):
        if u is not none:
            return strip + u[0] < strip
        return band + s[0] < band

    barrier = pltpu.get_barrier_semaphore()

    def signal(sem, epoch, u, s):
        pl.semaphore_signal(sem, inc=1, device_id=device(epoch, u, s), device_id_type=MESH)

    def to_epoch(sem, epoch):
        for u, s in near:
            guarded(both(u[3], s[3]), lambda u=u, s=s: signal(sem, epoch, u, s))

    for u, s in near[1:]:
        guarded(
            both(both(u[3], s[3]), jnp.logical_not(lower(u, s))),
            lambda u=u, s=s: signal(barrier, me, u, s),
        )
    for step in range(1, n_epoch):
        pl.when(me + step < n_epoch)(lambda step=step: to_epoch(barrier, me + step))
    met = partners * me + ahead_of_me

    @pl.when(met > 0)
    def _():
        pl.semaphore_wait(barrier, met)

    for u, s in near[1:]:
        guarded(
            both(both(u[3], s[3]), lower(u, s)),
            lambda u=u, s=s: signal(token.at[me], me, u, s),
        )
    for epoch in range(n_epoch - 1):
        pl.when(epoch < me)(lambda epoch=epoch: signal(token.at[me], epoch, none, none))

    def slot_of(sender, receiver):
        return sender - (sender > receiver).astype(jnp.int32)

    lane = lax.broadcasted_iota(jnp.int32, (8, LANES), 1)
    sub = lax.broadcasted_iota(jnp.int32, (8, LANES), 0)

    def within(base):
        return jnp.bitwise_and(lane - base, LANES - 1) < SIDE

    def side_tile(wide, which):
        first, last = wide[:, :LANES], wide[:, width - LANES :]
        if n_band == 2:
            return jnp.where(band == 0, last, first), (1 - band) * (LANES - SIDE)
        return (first, 0) if which == 0 else (last, LANES - SIDE)

    def packed(wide, which):
        tile, base = side_tile(wide, which)
        out = jnp.zeros((8, LANES), f32)
        for i in range(wide.shape[0] // 8):
            part = tile[8 * i : 8 * i + 8]
            if i > 0:
                part = pltpu.roll(part, SIDE * i, 1)
            out = jnp.where(within(base + SIDE * i), part, out)
        return out.astype(bf16)

    def copy(source, dest, sent, received, to):
        return pltpu.make_async_remote_copy(
            src_ref=source,
            dst_ref=dest,
            send_sem=sent,
            recv_sem=received,
            device_id=to,
            device_id_type=MESH,
        )

    n_up, n_side = len(ups), len(sides)
    images = []
    for u, s in near:
        i = 0 if u is none else 1 + ups.index(u)
        j = 0 if s is none else 1 + sides.index(s)
        images.append((u, s, i * (1 + n_side) + j))
    n_image = (1 + n_up) * (1 + n_side)
    CODE, COEF, OFFS, INDX, MODEL = (n_image + i for i in range(5))

    def image(epoch, u, s, kind, sender, at=None):
        source_at = epoch if at is None else at
        if u is none and s is none:
            source, dest = chosen.at[source_at], centre.at[sender]
        elif s is none:
            source, dest = chosen_edge.at[u[1], source_at], vertical.at[u[2], sender]
        elif u is none:
            source, dest = chosen_side.at[s[1], source_at], lateral.at[s[2], sender]
        else:
            source = chosen_corner.at[u[1], s[1], source_at]
            dest = corner.at[u[2], s[2], sender]
        return copy(
            source, dest, send_sem.at[kind], recv_sem.at[slot_of(sender, epoch), kind], device(epoch, u, s)
        )

    def arriving(epoch, u, s, kind):
        if u is none and s is none:
            dest = centre.at[epoch]
        elif s is none:
            dest = vertical.at[u[2], epoch]
        elif u is none:
            dest = lateral.at[s[2], epoch]
        else:
            dest = corner.at[u[2], s[2], epoch]
        return copy(dest, dest, send_sem.at[kind], recv_sem.at[slot_of(epoch, me), kind], device(epoch, u, s))

    def landing(links, place, size):
        if size == 2:
            return [(k[0], k[1], 1 - place, None, None) for k in links]
        return [(k[0], k[1], k[2], k[4], k[3]) for k in links]

    ups_in = landing(ups, strip, n_strip)
    sides_in = landing(sides, band, n_band)
    images_in = []
    for u, s, kind in images:
        a = none if u is none else ups_in[ups.index(u)]
        b = none if s is none else sides_in[sides.index(s)]
        images_in.append((a, b, kind))

    def send_image(epoch):
        for u, s, kind in images:
            guarded(
                both(u[3], s[3]), lambda u=u, s=s, kind=kind: image(epoch, u, s, kind, me).start()
            )

    def wait_image(epoch):
        for u, s, kind in images_in:
            guarded(
                both(u[3], s[3]), lambda u=u, s=s, kind=kind: arriving(epoch, u, s, kind).wait_recv()
            )

    def small(epoch, sender):
        return [
            copy(held, into.at[sender], send_sem.at[kind], recv_sem.at[slot_of(sender, epoch), kind], device(epoch, none, none))
            for held, into, kind in (
                (offsets, offsets_in, OFFS),
                (basis_index, basis_index_in, INDX),
            )
        ]

    def coefficient_tile(epoch, sender):
        return copy(
            coef_row.at[epoch], coefs_in.at[sender], send_sem.at[COEF], recv_sem.at[slot_of(sender, epoch), COEF],
            device(epoch, none, none),
        )

    def coded(epoch, sender):
        return copy(
            code.at[epoch], code_in.at[sender], send_sem.at[CODE], recv_sem.at[slot_of(sender, epoch), CODE],
            device(epoch, none, none),
        )

    def returned(epoch, sender):
        return copy(
            model_out.at[epoch], model_in.at[sender], send_sem.at[MODEL], recv_sem.at[slot_of(sender, epoch), 0],
            device(epoch, none, none),
        )

    def own_piece(u, s, kind, incoming):
        if s is none:
            source, dest = own_edge.at[0 if incoming else u[1]], own_vertical.at[u[2]]
        elif u is none:
            source, dest = own_side.at[0 if incoming else s[1]], own_lateral.at[s[2]]
        else:
            source = own_diagonal.at[0 if incoming else u[1], 0 if incoming else s[1]]
            dest = own_corner.at[u[2], s[2]]
        if incoming:
            source = dest
        return copy(source, dest, own_send.at[kind], own_recv.at[kind], device(me, u, s))

    def send_small(epoch):
        for one in small(epoch, me):
            one.start()

    loads[6].wait()
    loads[8].wait()
    for epoch in range(n_epoch - 1):
        pl.when(epoch < me)(lambda epoch=epoch: send_small(epoch))

    loads[5].wait()
    for exposure in range(exp_dev):
        coefs[exposure] = jnp.zeros((8, LANES), f32)
        for p in range(n_poly):
            coefs[exposure, p : p + 1, 0:n_sel] = coefficients[p, exposure : exposure + 1, :]
        coef_row[exposure] = jnp.sum(
            pltpu.roll(coefs[exposure], 0, 1, stride=n_sel, stride_axis=0), axis=0, keepdims=True
        )

    for epoch in range(n_epoch - 1):
        pl.when(epoch < me)(lambda epoch=epoch: coefficient_tile(epoch, me).start())
    loads[0].wait()
    loads[1].wait()

    def rim(wide, which):
        low, high = wide[:EDGE_ROWS], wide[height - EDGE_ROWS :]
        if n_strip == 2:
            return jnp.where(strip == 0, high, low)
        return low if which == 0 else high

    for epoch in range(n_epoch):
        tile = intersection[epoch * exp_dev + me] - me * tile_dev
        picked = template[jnp.clip(tile, 0, tile_dev - 1)]
        chosen[epoch] = picked
        wide = picked.astype(f32)
        for side in range(n_side):
            chosen_side[side, epoch] = packed(wide, side)
        for which in range(n_up):
            edge = rim(wide, which)
            chosen_edge[which, epoch] = edge.astype(bf16)
            for side in range(n_side):
                chosen_corner[which, side, epoch] = packed(edge, side)
    pl.when(me > 0)(lambda: send_image(0))
    loads[2].wait()
    loads[3].wait()
    loads[4].wait()
    for epoch in range(n_epoch):
        share = bad_mask[epoch].astype(f32) / variance[epoch]
        weight[epoch] = share
        code[epoch] = encode(science[epoch], share)
    pl.when(me > 0)(lambda: coded(0, me).start())

    for t in range(tile_dev):
        wide = template[t].astype(f32)
        for side in range(n_side):
            own_side[side, t] = packed(wide, side)
        for which in range(n_up):
            edge = rim(wide, which)
            own_edge[which, t] = edge.astype(bf16)
            for side in range(n_side):
                own_diagonal[which, side, t] = packed(edge, side)
    for u, s, kind in images[1:]:
        guarded(
            both(both(u[3], s[3]), lower(u, s)),
            lambda u=u, s=s, kind=kind: own_piece(u, s, kind, False).start(),
        )

    def clear(ref):
        ref[...] = jnp.zeros(ref.shape, ref.dtype)

    def clear_up(slot):
        clear(vertical.at[slot])
        clear(own_vertical.at[slot])

    def clear_side(slot):
        clear(lateral.at[slot])
        clear(own_lateral.at[slot])

    def clear_corner(slot, at):
        clear(corner.at[slot, at])
        clear(own_corner.at[slot, at])

    if n_strip == 1:
        clear(vertical)
        clear(own_vertical)
        clear(corner)
        clear(own_corner)
    elif n_strip == 2:
        clear_up(strip)
        for at in range(2):
            clear_corner(strip, at)
    else:
        for slot, edge in ((0, strip == 0), (1, strip == n_strip - 1)):

            @pl.when(edge)
            def _(slot=slot):
                clear_up(slot)
                for at in range(2):
                    clear_corner(slot, at)

    if n_band == 1:
        clear(lateral)
        clear(own_lateral)
        if n_strip > 1:
            clear(corner)
            clear(own_corner)
    elif n_band == 2:
        clear_side(band)
        if n_strip == 2:
            clear_corner(1 - strip, band)
        elif n_strip > 2:
            for slot, held in ((0, strip > 0), (1, strip < n_strip - 1)):
                pl.when(held)(lambda slot=slot: clear_corner(slot, band))
    else:
        for slot, edge in ((0, band == 0), (1, band == n_band - 1)):

            @pl.when(edge)
            def _(slot=slot):
                clear_side(slot)
                for at in range(2):
                    clear_corner(at, slot)

    slab[:, :, height + 2 * EDGE_ROWS :, :] = jnp.zeros(
        (slab.shape[0], slab.shape[1], 8, LANES), f32
    )

    n_pairs = (ks + 1) // 2
    n_tiles = n_pairs * SLOT // LANES
    later = jnp.bitwise_and(lane, 7) >= sub

    def mix_of(some, indices):
        parts = []
        for j in range(n_sel):
            column = jnp.broadcast_to(some[:, j : j + 1], (8, LANES))
            parts.append(jnp.where(lane == indices(j), column, 0.0))
        while len(parts) > 1:
            parts = [
                parts[i] + parts[i + 1] if i + 1 < len(parts) else parts[i]
                for i in range(0, len(parts), 2)
            ]
        mix = jnp.where(sub < n_poly, parts[0], 0.0)
        mix = mix + pltpu.roll(mix, half, 1)
        high = mix.astype(bf16).astype(f32)
        return high, mix - high

    def unpacked(line):
        wide = jnp.broadcast_to(line, (8, LANES))
        out = wide
        for p in range(1, n_poly):
            out = jnp.where(sub == p, pltpu.roll(wide, LANES - n_sel * p, 1), out)
        return out

    def mixed(pairs):
        rows = jnp.concatenate([p[0] for p in pairs] + [p[1] for p in pairs], axis=0)
        out = lax.dot_general(
            rows.astype(bf16), table[...], (((1,), (1,)), ((), ())), preferred_element_type=f32
        )
        size = 8 * len(pairs)
        return (out[:size] + out[size:]).astype(bf16).astype(f32)

    def spread(row, into):
        for p in range(0, n_poly, 2):
            for t in range(n_tiles):
                halves = []
                for h in range(2):
                    at = row * 8 + p + h
                    wide = jnp.broadcast_to(
                        kernels[at : at + 1, t * LANES : (t + 1) * LANES], (8, LANES)
                    )
                    close = pltpu.roll(wide, 0, 1, stride=1, stride_axis=0)
                    far = pltpu.roll(wide, 8, 1, stride=1, stride_axis=0)
                    halves.append(jnp.where(later, close, far))
                toeplitz[into, p * 8 : (p + 2) * 8, t * LANES : (t + 1) * LANES] = (
                    jnp.concatenate(halves, axis=0).astype(bf16)
                )

    pairs = [
        mix_of(
            coefs[exposure],
            lambda j, exposure=exposure: basis_index[exposure, j],
        )
        for exposure in range(exp_dev)
    ]

    loads[7].wait()
    blank = jnp.zeros((8, LANES), f32)

    def taps(b, g):
        if b >= ks or g * 8 >= ks:
            return blank
        here = min(8, ks - g * 8)
        tile = basis[g * 8 : g * 8 + here, b, :]
        if here < 8:
            tile = jnp.concatenate([tile, jnp.zeros((8 - here, n_basis), f32)], axis=0)
        tile = jnp.concatenate([tile, jnp.zeros((8, LANES - n_basis), f32)], axis=1)
        high = tile.astype(bf16).astype(f32)
        return jnp.where(lane < half, high, pltpu.roll(tile - high, half, 1))

    table[...] = jnp.concatenate(
        [
            taps(2 * q + h, g)
            for q in range(n_pairs)
            for g in range(GROUPS)
            for h in range(2)
        ],
        axis=0,
    ).astype(bf16)
    kernels[0 : 8 * exp_dev] = mixed(pairs)
    for exposure in range(exp_dev):
        spread(exposure, exposure)

    row = lax.broadcasted_iota(jnp.int32, (height, 1), 0) + strip * height
    col = lax.broadcasted_iota(jnp.int32, (1, width), 1) + band * width
    r = (2.0 * row.astype(f32) + 1.0) / (height * n_strip) - 1.0
    c = (2.0 * col.astype(f32) + 1.0) / (width * n_band) - 1.0
    r = jnp.broadcast_to(r, (height, width))
    c = jnp.broadcast_to(c, (height, width))

    span = height + 8 * GROUPS - 8
    at_lane = lax.broadcasted_iota(jnp.int32, (span, LANES), 1)

    beside = [(0, LANES - SIDE), (1, 0)]
    if n_band == 2:
        beside = [(1 - band, band * (LANES - SIDE))]

    def lay(board, middle, up, side, edge, at):
        for rows, body, rims in (
            (0, up(0), [(edge(0, k).astype(f32), base) for k, base in beside]),
            (EDGE_ROWS, middle, [(side(k).astype(f32), base) for k, base in beside]),
            (EDGE_ROWS + height, up(1), [(edge(1, k).astype(f32), base) for k, base in beside]),
        ):
            wide = body.astype(f32)
            size = wide.shape[0]
            for t in range(n_lane):
                slab[board, t, rows : rows + size, :] = wide[:, t * LANES : (t + 1) * LANES]
            for i in range(size // 8):
                part = jnp.zeros((8, LANES), f32)
                for held, base in rims:
                    turned = held if i == 0 else pltpu.roll(held, LANES - SIDE * i, 1)
                    part = jnp.where(within(base), turned, part)
                slab[board, n_lane, rows + 8 * i : rows + 8 * i + 8, :] = part

    def lay_own(board, tile):
        lay(
            board,
            template[tile],
            lambda v: own_vertical[v, tile],
            lambda s: own_lateral[s, tile],
            lambda v, s: own_corner[v, s, tile],
            tile,
        )

    def lay_other(board, epoch):
        lay(
            board,
            centre[epoch],
            lambda v: vertical[v, epoch],
            lambda s: lateral[s, epoch],
            lambda v, s: corner[v, s, epoch],
            epoch,
        )

    def models(board, factor, down, along):
        views = []
        for h in range(2):
            turned = [
                pltpu.roll(slab[board, t, pl.ds(down, span), :], along - h, 1)
                for t in range(n_lane + 1)
            ]
            views.append(
                jnp.concatenate(
                    [
                        jnp.where(at_lane < along - h, turned[t - 1], turned[t])
                        for t in range(n_lane + 1)
                    ],
                    axis=1,
                )
            )
        tiles = [
            jnp.concatenate(
                [views[0][g * 8 : g * 8 + 8], views[1][g * 8 : g * 8 + 8]], axis=0
            ).astype(bf16)
            for g in range(span // 8)
        ]
        moved = [[tile[:, 2 * q : 2 * q + width] for tile in tiles] for q in range(n_pairs)]
        for block in range(height // 8):
            stacked = jnp.concatenate(
                [moved[q][block + g] for q in range(n_pairs) for g in range(GROUPS)], axis=0
            )
            conv = jnp.dot(factor, stacked, preferred_element_type=f32)
            q = [conv[p * 8 : (p + 1) * 8] for p in range(n_poly)]
            at = slice(block * 8, block * 8 + 8)
            rr, cc = r[at], c[at]
            yield at, q[0] + rr * (q[1] + rr * q[3] + cc * q[4]) + cc * (q[2] + cc * q[5])

    def tile_of(epoch):
        return intersection[epoch * exp_dev + me] - me * tile_dev

    def down_of(shift):
        return EDGE_ROWS - HALF + shift

    def along_of(shift):
        return HALF - shift

    behind = partners - 1 - ahead_of_me

    @pl.when(behind > 0)
    def _():
        pl.semaphore_wait(token.at[me], behind)

    for u, s, kind in images[1:]:
        guarded(
            both(both(u[3], s[3]), jnp.logical_not(lower(u, s))),
            lambda u=u, s=s, kind=kind: own_piece(u, s, kind, False).start(),
        )
    for epoch in range(1, n_epoch - 1):

        @pl.when(epoch < me)
        def _(epoch=epoch):
            send_image(epoch)
            coded(epoch, me).start()

    def offer(step):
        @pl.when(me + step < n_epoch)
        def _(epoch=me + step):
            pl.semaphore_wait(token.at[epoch], 1)
            send_small(epoch)
            coefficient_tile(epoch, me).start()
            coded(epoch, me).start()

    early = n_epoch - 2 if n_epoch == 4 else n_epoch - 1
    for step in range(1, early + 1):
        offer(step)

    for u, s, kind in images_in[1:]:
        guarded(both(u[3], s[3]), lambda u=u, s=s, kind=kind: own_piece(u, s, kind, True).wait_recv())

    def own_board(tile):
        return jnp.clip(tile, 0, tile_dev - 1)

    def first():
        tile = tile_of(me)
        for at, model in models(own_board(tile), toeplitz[me], down_of(offsets[0, me]), along_of(offsets[1, me])):
            left = science[me, at] - model
            residual[me, at] = left
            share = weight[me, at]
            for t in range(tile_dev):
                here = (tile == t).astype(f32)
                numer[t, at] = share * left * here
                denom[t, at] = share * here

    def lay_tiles():
        for t in range(tile_dev):
            lay_own(t, t)

    def partner(step):
        return jnp.where(me + step < n_epoch, me + step, n_epoch - 1 - step)

    def theirs(step):
        epoch = partner(step)
        last = exp_dev
        kernels[8 * last : 8 * last + 8] = mixed(
            [mix_of(unpacked(coefs_in[epoch]), lambda j: basis_index_in[epoch, me, j])]
        )
        spread(last, last)
        for at, model in models(
            own_board(tile_of(epoch)),
            toeplitz[last],
            down_of(offsets_in[epoch, 0, me]),
            along_of(offsets_in[epoch, 1, me]),
        ):
            model_out[epoch, at] = model

    def wait_small(step):
        epoch = partner(step)
        for one in small(me, epoch) + [coefficient_tile(me, epoch)]:
            one.wait_recv()

    def answer(step):
        pl.when(partner(step) > me)(lambda: returned(partner(step), me).start())

    def host(step):
        wait_small(step)
        theirs(step)
        answer(step)

    def ours(step):
        epoch = partner(step)
        board = tile_dev + step - 1 if isinstance(step, int) else tile_dev
        lay_other(board, epoch)
        for at, model in models(
            board, toeplitz[epoch], down_of(offsets[0, epoch]), along_of(offsets[1, epoch])
        ):
            residual[epoch, at] = science[epoch, at] - model

    def settle(step):
        epoch = partner(step)
        returned(me, epoch).wait_recv()
        residual[epoch] = science[epoch] - model_in[epoch]

    def mine(step):
        @pl.when(partner(step) > me)
        def _():
            wait_image(partner(step))
            ours(step)

    def finish(step):
        gather(step)
        pl.when(partner(step) < me)(lambda: settle(step))

    def gather(step):
        epoch = partner(step)
        tile = tile_of(epoch)
        coded(me, epoch).wait_recv()
        seen, share = decode(code_in[epoch])
        value = share * (seen - model_out[epoch])
        for t in range(tile_dev):
            here = (tile == t).astype(f32)
            numer[t] = numer[t] + value * here
            denom[t] = denom[t] + share * here

    if n_epoch == 4:

        @pl.when(me == 0)
        def _():
            lay_tiles()
            first()
            host(1)
            offer(3)
            wait_small(2)
            wait_image(1)
            theirs(2)
            ours(1)
            answer(2)
            host(3)
            wait_image(3)
            wait_image(2)
            ours(3)
            ours(2)

        @pl.when(me > 0)
        def _():
            lay_tiles()
            first()
            for step in range(1, n_epoch):
                host(step)
            for step in range(2, 0, -1):
                mine(step)

        for step in (1, 3, 2):
            finish(step)
    else:
        lay_tiles()
        first()

        def walk(stage):
            lax.fori_loop(1, n_epoch, lambda step, carry: (stage(step), carry)[1], 0)

        walk(host)
        walk(mine)
        walk(finish)

    for t in range(tile_dev):
        coadd[t] = numer[t] / (denom[t] + 1.0)

    for u, s, kind in images[1:]:
        guarded(both(u[3], s[3]), lambda u=u, s=s, kind=kind: own_piece(u, s, kind, False).wait_send())
    if n_epoch > 1:
        rest = pl.ds(0, n_epoch - 1)

        def drain(source, kind, u, s):
            copy(source, source, send_sem.at[kind], recv_sem.at[0, 0], device(me, u, s)).wait_send()

        for number in range(1, n_epoch):

            @pl.when(me == number)
            def _(number=number):
                lead = pl.ds(0, number)
                for u, s, kind in images:
                    if u is none and s is none:
                        source = chosen.at[lead]
                    elif s is none:
                        source = chosen_edge.at[u[1], lead]
                    elif u is none:
                        source = chosen_side.at[s[1], lead]
                    else:
                        source = chosen_corner.at[u[1], s[1], lead]
                    guarded(
                        both(u[3], s[3]),
                        lambda u=u, s=s, kind=kind, source=source: drain(source, kind, u, s),
                    )

            @pl.when(me == n_epoch - 1 - number)
            def _(number=number):
                drain(model_out.at[pl.ds(0, number)], MODEL, none, none)

        for held, kind in (
            (offsets_in, OFFS),
            (basis_index_in, INDX),
            (coef_row, COEF),
            (code, CODE),
        ):
            drain(held.at[rest], kind, none, none)


def leave(residual, coadd, residual_out, coadd_out, sem):
    parts = [
        (held.at[i], out.at[i])
        for held, out in ((residual, residual_out), (coadd, coadd_out))
        for i in range(held.shape[0])
    ]
    copies = [pltpu.make_async_copy(held, out, sem.at[i]) for i, (held, out) in enumerate(parts)]
    for one in copies:
        one.start()
    for one in copies:
        one.wait()


def local(sizes, template, science, variance, bad_mask, intersection, offsets, basis_index, coefficients, basis):
    n_epoch, n_strip, n_band = sizes
    tile_dev, height, width = template.shape
    exp_dev = science.shape[0]
    assert exp_dev == n_epoch
    n_poly = coefficients.shape[2]
    n_sel = basis_index.shape[1]
    ks = basis.shape[1]
    n_pairs = (ks + 1) // 2
    far = pl.BlockSpec(memory_space=pltpu.HBM)
    near = pl.BlockSpec(memory_space=pltpu.VMEM)
    free = pl.BlockSpec(memory_space=pl.ANY)
    bf16, f32 = jnp.bfloat16, jnp.float32
    dma = pltpu.SemaphoreType.DMA
    offsets = offsets.T
    coefficients = coefficients.transpose(2, 0, 1)
    basis = basis.transpose(1, 2, 0)
    n_up, n_side = min(n_strip - 1, 2), min(n_band - 1, 2)
    n_image = (1 + n_up) * (1 + n_side)
    edges, sides = max(n_up, 1), max(n_side, 1)
    rim = EDGE_ROWS
    residual, coadd = pl.pallas_call(
        functools.partial(kernel, sizes),
        out_shape=(
            pltpu.VMEM(science.shape, f32),
            pltpu.VMEM(template.shape, f32),
        ),
        in_specs=[far] * 9,
        out_specs=(near, near),
        scratch_shapes=[
            pltpu.SMEM(intersection.shape, jnp.int32),
            pltpu.SMEM(offsets.shape, jnp.int32),
            pltpu.SMEM((n_epoch,) + offsets.shape, jnp.int32),
            pltpu.SMEM(basis_index.shape, jnp.int32),
            pltpu.SMEM((n_epoch,) + basis_index.shape, jnp.int32),
            pltpu.VMEM(coefficients.shape, f32),
            pltpu.VMEM((n_epoch, 1, LANES), f32),
            pltpu.VMEM(template.shape, bf16),
            pltpu.VMEM(science.shape, f32),
            pltpu.VMEM(science.shape, f32),
            pltpu.VMEM(science.shape, jnp.int32),
            pltpu.VMEM(basis.shape, f32),
            pltpu.VMEM((n_epoch, height, width), bf16),
            pltpu.VMEM((edges, n_epoch, rim, width), bf16),
            pltpu.VMEM((sides, n_epoch, 8, LANES), bf16),
            pltpu.VMEM((edges, sides, n_epoch, 8, LANES), bf16),
            pltpu.VMEM((edges, tile_dev, rim, width), bf16),
            pltpu.VMEM((sides, tile_dev, 8, LANES), bf16),
            pltpu.VMEM((edges, sides, tile_dev, 8, LANES), bf16),
            pltpu.VMEM((n_epoch, height, width), bf16),
            pltpu.VMEM((2, n_epoch, rim, width), bf16),
            pltpu.VMEM((2, n_epoch, 8, LANES), bf16),
            pltpu.VMEM((2, 2, n_epoch, 8, LANES), bf16),
            pltpu.VMEM((2, tile_dev, rim, width), bf16),
            pltpu.VMEM((2, tile_dev, 8, LANES), bf16),
            pltpu.VMEM((2, 2, tile_dev, 8, LANES), bf16),
            pltpu.VMEM((exp_dev, 8, LANES), f32),
            pltpu.VMEM((exp_dev, 1, LANES), f32),
            pltpu.VMEM((n_pairs * SLOT, LANES), bf16),
            pltpu.VMEM((8 * exp_dev + 8, n_pairs * SLOT), f32),
            pltpu.VMEM((tile_dev + max(n_epoch - 1, 1), width // LANES + 1, 2 * rim + height + 8, LANES), f32),
            pltpu.VMEM((exp_dev + 1, n_poly * 8, n_pairs * SLOT), bf16),
            pltpu.VMEM((exp_dev, height, width), f32),
            pltpu.VMEM((n_epoch, height, width), jnp.int32),
            pltpu.VMEM((n_epoch, height, width), jnp.int32),
            pltpu.VMEM((n_epoch, height, width), f32),
            pltpu.VMEM((n_epoch, height, width), f32),
            pltpu.VMEM(template.shape, f32),
            pltpu.VMEM(template.shape, f32),
            dma((9,)),
            dma((n_image + 5,)),
            dma((max(n_epoch - 1, 1), n_image + 4)),
            dma((n_image,)),
            dma((n_image,)),
            pltpu.SemaphoreType.REGULAR((n_epoch,)),
        ],
        compiler_params=pltpu.CompilerParams(
            collective_id=0, has_side_effects=True
        ),
    )(
        intersection, offsets, basis_index, coefficients,
        template, science, variance, bad_mask, basis,
    )
    return pl.pallas_call(
        leave,
        out_shape=(
            jax.ShapeDtypeStruct(science.shape, f32),
            jax.ShapeDtypeStruct(template.shape, f32),
        ),
        in_specs=[near] * 2,
        out_specs=(free, free),
        scratch_shapes=[dma((exp_dev + tile_dev,))],
    )(*(pltpu.with_memory_space_constraint(x, pltpu.VMEM) for x in (residual, coadd)))


def solution(mesh):
    sizes = (mesh.shape["epoch"], mesh.shape["strip"], mesh.shape["band"])
    image = P(("groups", "epoch"), "strip", "band")
    split = ("groups", "epoch")
    in_specs = (
        image, image, image, image, P("groups"),
        P(split, None), P(split, None), P(split, None, None), P(),
    )
    return jax.shard_map(
        functools.partial(local, sizes),
        mesh=mesh,
        in_specs=in_specs,
        out_specs=(image, image),
        check_vma=False,
    )
```

```python
import functools

import jax
import jax.numpy as jnp
from jax import lax
from jax.experimental import pallas as pl
from jax.experimental.pallas import tpu as pltpu
from jax.sharding import PartitionSpec as P

HALF = 9
SHIFT = 4
EDGE_ROWS = 16
LANES = 128
SLOT = 64
GROUPS = 4
SIDE = 16
SCIENCE_TOP = 6.0
WEIGHT_TOP = 0.5
LEVELS = 65535.0

MESH = pl.DeviceIdType.MESH


def links_of(size, place):
    if size == 1:
        return []
    if size == 2:
        return [(1 - 2 * place, 0, place, None, None)]
    return [
        (-1, 0, 1, place > 0, place < size - 1),
        (1, 1, 0, place < size - 1, place > 0),
    ]


def both(first, second):
    if first is None:
        return second
    if second is None:
        return first
    return jnp.logical_and(first, second)


def guarded(side, body):
    if side is None:
        body()
    else:
        pl.when(side)(body)


def encode(science, weight):
    high = (science + SCIENCE_TOP) * (LEVELS / (2.0 * SCIENCE_TOP)) + 0.5
    low = weight * (LEVELS / WEIGHT_TOP) + 0.5
    high = jnp.clip(high, 0.0, LEVELS).astype(jnp.int32)
    low = jnp.clip(low, 0.0, LEVELS).astype(jnp.int32)
    return jnp.bitwise_or(jnp.left_shift(high, 16), low)


def decode(code):
    high = lax.shift_right_logical(code, jnp.full(code.shape, 16, jnp.int32))
    low = jnp.bitwise_and(code, 65535)
    science = high.astype(jnp.float32) * (2.0 * SCIENCE_TOP / LEVELS) - SCIENCE_TOP
    return science, low.astype(jnp.float32) * (WEIGHT_TOP / LEVELS)


def kernel(
    sizes,
    intersection_hbm,
    offsets_hbm,
    basis_index_hbm,
    coefficients_hbm,
    template_hbm,
    science_hbm,
    variance_hbm,
    bad_mask_hbm,
    basis_hbm,
    residual,
    coadd,
    intersection,
    offsets,
    offsets_in,
    basis_index,
    basis_index_in,
    coefficients,
    coefs_in,
    template,
    science,
    variance,
    bad_mask,
    basis,
    chosen,
    chosen_edge,
    chosen_side,
    chosen_corner,
    own_edge,
    own_side,
    own_diagonal,
    centre,
    vertical,
    lateral,
    corner,
    own_vertical,
    own_lateral,
    own_corner,
    coefs,
    coef_row,
    table,
    kernels,
    slab,
    toeplitz,
    weight,
    code,
    code_in,
    model_out,
    model_in,
    numer,
    denom,
    local_sem,
    send_sem,
    recv_sem,
    own_send,
    own_recv,
    token,
):
    n_epoch, n_strip, n_band = sizes
    tile_dev, height, width = template.shape
    exp_dev = science.shape[0]
    n_poly, _, n_sel = coefficients.shape
    ks, _, n_basis = basis.shape
    n_lane = width // LANES
    half = LANES // 2
    f32, bf16 = jnp.float32, jnp.bfloat16
    group = lax.axis_index("groups")
    me = lax.axis_index("epoch")
    strip = lax.axis_index("strip")
    band = lax.axis_index("band")

    ups = links_of(n_strip, strip)
    sides = links_of(n_band, band)
    none = (0, None, None, None, None)
    near = [(u, s) for u in [none] + ups for s in [none] + sides]

    def device(epoch, u, s):
        return (group, epoch, strip + u[0], band + s[0])

    loads = [
        pltpu.make_async_copy(held, here, local_sem.at[i])
        for i, (held, here) in enumerate(
            (
                (intersection_hbm, intersection),
                (template_hbm, template),
                (variance_hbm, variance),
                (bad_mask_hbm, bad_mask),
                (science_hbm, science),
                (coefficients_hbm, coefficients),
                (basis_index_hbm, basis_index),
                (basis_hbm, basis),
                (offsets_hbm, offsets),
            )
        )
    ]
    for i in (5, 6, 8, 0, 1, 2, 3, 4, 7):
        loads[i].start()

    def count(size, place):
        if size < 3:
            return size
        return 1 + jnp.minimum(place, 1) + jnp.minimum(size - 1 - place, 1)

    def before(size, place):
        return place if size < 3 else jnp.minimum(place, 1)

    across = count(n_band, band)
    partners = count(n_strip, strip) * across
    ahead_of_me = before(n_strip, strip) * across + before(n_band, band)

    def lower(u, s):
        if u is not none:
            return strip + u[0] < strip
        return band + s[0] < band

    swap = n_epoch == 4

    barrier = pltpu.get_barrier_semaphore()

    def signal(sem, epoch, u, s):
        pl.semaphore_signal(sem, inc=1, device_id=device(epoch, u, s), device_id_type=MESH)

    def to_epoch(sem, epoch):
        for u, s in near:
            guarded(both(u[3], s[3]), lambda u=u, s=s: signal(sem, epoch, u, s))

    for u, s in near[1:]:
        guarded(
            both(both(u[3], s[3]), jnp.logical_not(lower(u, s))),
            lambda u=u, s=s: signal(barrier, me, u, s),
        )
    for step in range(1, n_epoch):
        pl.when(me + step < n_epoch)(lambda step=step: to_epoch(barrier, me + step))
    met = partners * me + ahead_of_me

    @pl.when(met > 0)
    def _():
        pl.semaphore_wait(barrier, met)

    for u, s in near[1:]:
        guarded(
            both(both(u[3], s[3]), lower(u, s)),
            lambda u=u, s=s: signal(token.at[me], me, u, s),
        )
    for epoch in range(n_epoch - 1):
        if swap and epoch == 0:
            pl.when(me == n_epoch - 1)(lambda: to_epoch(token.at[me], 0))
            pl.when(jnp.logical_and(me > 0, me < n_epoch - 1))(
                lambda: signal(token.at[me], 0, none, none)
            )
        else:
            pl.when(epoch < me)(lambda epoch=epoch: signal(token.at[me], epoch, none, none))

    def slot_of(sender, receiver):
        return sender - (sender > receiver).astype(jnp.int32)

    lane = lax.broadcasted_iota(jnp.int32, (8, LANES), 1)
    sub = lax.broadcasted_iota(jnp.int32, (8, LANES), 0)

    def within(base):
        return jnp.bitwise_and(lane - base, LANES - 1) < SIDE

    def side_tile(wide, which):
        first, last = wide[:, :LANES], wide[:, width - LANES :]
        if n_band == 2:
            return jnp.where(band == 0, last, first), (1 - band) * (LANES - SIDE)
        return (first, 0) if which == 0 else (last, LANES - SIDE)

    def packed(wide, which):
        tile, base = side_tile(wide, which)
        out = jnp.zeros((8, LANES), f32)
        for i in range(wide.shape[0] // 8):
            part = tile[8 * i : 8 * i + 8]
            if i > 0:
                part = pltpu.roll(part, SIDE * i, 1)
            out = jnp.where(within(base + SIDE * i), part, out)
        return out.astype(bf16)

    def copy(source, dest, sent, received, to):
        return pltpu.make_async_remote_copy(
            src_ref=source,
            dst_ref=dest,
            send_sem=sent,
            recv_sem=received,
            device_id=to,
            device_id_type=MESH,
        )

    n_up, n_side = len(ups), len(sides)
    images = []
    for u, s in near:
        i = 0 if u is none else 1 + ups.index(u)
        j = 0 if s is none else 1 + sides.index(s)
        images.append((u, s, i * (1 + n_side) + j))
    n_image = (1 + n_up) * (1 + n_side)
    CODE, COEF, OFFS, INDX, MODEL = (n_image + i for i in range(5))

    def image(epoch, u, s, kind, sender, at=None):
        source_at = epoch if at is None else at
        if u is none and s is none:
            source, dest = chosen.at[source_at], centre.at[sender]
        elif s is none:
            source, dest = chosen_edge.at[u[1], source_at], vertical.at[u[2], sender]
        elif u is none:
            source, dest = chosen_side.at[s[1], source_at], lateral.at[s[2], sender]
        else:
            source = chosen_corner.at[u[1], s[1], source_at]
            dest = corner.at[u[2], s[2], sender]
        return copy(
            source, dest, send_sem.at[kind], recv_sem.at[slot_of(sender, epoch), kind], device(epoch, u, s)
        )

    def arriving(epoch, u, s, kind):
        if u is none and s is none:
            dest = centre.at[epoch]
        elif s is none:
            dest = vertical.at[u[2], epoch]
        elif u is none:
            dest = lateral.at[s[2], epoch]
        else:
            dest = corner.at[u[2], s[2], epoch]
        return copy(dest, dest, send_sem.at[kind], recv_sem.at[slot_of(epoch, me), kind], device(epoch, u, s))

    def landing(links, place, size):
        if size == 2:
            return [(k[0], k[1], 1 - place, None, None) for k in links]
        return [(k[0], k[1], k[2], k[4], k[3]) for k in links]

    ups_in = landing(ups, strip, n_strip)
    sides_in = landing(sides, band, n_band)
    images_in = []
    for u, s, kind in images:
        a = none if u is none else ups_in[ups.index(u)]
        b = none if s is none else sides_in[sides.index(s)]
        images_in.append((a, b, kind))

    def send_image(epoch):
        for u, s, kind in images:
            guarded(
                both(u[3], s[3]), lambda u=u, s=s, kind=kind: image(epoch, u, s, kind, me).start()
            )

    def wait_image(epoch):
        for u, s, kind in images_in:
            guarded(
                both(u[3], s[3]), lambda u=u, s=s, kind=kind: arriving(epoch, u, s, kind).wait_recv()
            )

    def small(epoch, sender):
        return [
            copy(held, into.at[sender], send_sem.at[kind], recv_sem.at[slot_of(sender, epoch), kind], device(epoch, none, none))
            for held, into, kind in (
                (offsets, offsets_in, OFFS),
                (basis_index, basis_index_in, INDX),
            )
        ]

    def coefficient_tile(epoch, sender):
        return copy(
            coef_row.at[epoch], coefs_in.at[sender], send_sem.at[COEF], recv_sem.at[slot_of(sender, epoch), COEF],
            device(epoch, none, none),
        )

    def coded(epoch, sender):
        return copy(
            code.at[epoch], code_in.at[sender], send_sem.at[CODE], recv_sem.at[slot_of(sender, epoch), CODE],
            device(epoch, none, none),
        )

    def returned(epoch, sender):
        return copy(
            model_out.at[epoch], model_in.at[sender], send_sem.at[MODEL], recv_sem.at[slot_of(sender, epoch), 0],
            device(epoch, none, none),
        )

    def own_piece(u, s, kind, incoming):
        if s is none:
            source, dest = own_edge.at[0 if incoming else u[1]], own_vertical.at[u[2]]
        elif u is none:
            source, dest = own_side.at[0 if incoming else s[1]], own_lateral.at[s[2]]
        else:
            source = own_diagonal.at[0 if incoming else u[1], 0 if incoming else s[1]]
            dest = own_corner.at[u[2], s[2]]
        if incoming:
            source = dest
        return copy(source, dest, own_send.at[kind], own_recv.at[kind], device(me, u, s))

    def send_small(epoch):
        for one in small(epoch, me):
            one.start()

    loads[6].wait()
    loads[8].wait()
    for epoch in range(n_epoch - 1):
        pl.when(epoch < me)(lambda epoch=epoch: send_small(epoch))

    loads[5].wait()
    for exposure in range(exp_dev):
        coefs[exposure] = jnp.zeros((8, LANES), f32)
        for p in range(n_poly):
            coefs[exposure, p : p + 1, 0:n_sel] = coefficients[p, exposure : exposure + 1, :]
        coef_row[exposure] = jnp.sum(
            pltpu.roll(coefs[exposure], 0, 1, stride=n_sel, stride_axis=0), axis=0, keepdims=True
        )

    for epoch in range(n_epoch - 1):
        pl.when(epoch < me)(lambda epoch=epoch: coefficient_tile(epoch, me).start())
    loads[0].wait()
    loads[1].wait()

    def rim(wide, which):
        low, high = wide[:EDGE_ROWS], wide[height - EDGE_ROWS :]
        if n_strip == 2:
            return jnp.where(strip == 0, high, low)
        return low if which == 0 else high

    for epoch in range(n_epoch):
        tile = intersection[epoch * exp_dev + me] - me * tile_dev
        picked = template[jnp.clip(tile, 0, tile_dev - 1)]
        chosen[epoch] = picked
        wide = picked.astype(f32)
        for side in range(n_side):
            chosen_side[side, epoch] = packed(wide, side)
        for which in range(n_up):
            edge = rim(wide, which)
            chosen_edge[which, epoch] = edge.astype(bf16)
            for side in range(n_side):
                chosen_corner[which, side, epoch] = packed(edge, side)
    pl.when(me > 0)(lambda: send_image(0))
    loads[2].wait()
    loads[3].wait()
    loads[4].wait()
    for epoch in range(n_epoch):
        share = bad_mask[epoch].astype(f32) / variance[epoch]
        weight[epoch] = share
        code[epoch] = encode(science[epoch], share)
    pl.when(me > 0)(lambda: coded(0, me).start())

    for t in range(tile_dev):
        wide = template[t].astype(f32)
        for side in range(n_side):
            own_side[side, t] = packed(wide, side)
        for which in range(n_up):
            edge = rim(wide, which)
            own_edge[which, t] = edge.astype(bf16)
            for side in range(n_side):
                own_diagonal[which, side, t] = packed(edge, side)
    for u, s, kind in images[1:]:
        guarded(
            both(both(u[3], s[3]), lower(u, s)),
            lambda u=u, s=s, kind=kind: own_piece(u, s, kind, False).start(),
        )

    def clear(ref):
        ref[...] = jnp.zeros(ref.shape, ref.dtype)

    def clear_up(slot):
        clear(vertical.at[slot])
        clear(own_vertical.at[slot])

    def clear_side(slot):
        clear(lateral.at[slot])
        clear(own_lateral.at[slot])

    def clear_corner(slot, at):
        clear(corner.at[slot, at])
        clear(own_corner.at[slot, at])

    if n_strip == 1:
        clear(vertical)
        clear(own_vertical)
        clear(corner)
        clear(own_corner)
    elif n_strip == 2:
        clear_up(strip)
        for at in range(2):
            clear_corner(strip, at)
    else:
        for slot, edge in ((0, strip == 0), (1, strip == n_strip - 1)):

            @pl.when(edge)
            def _(slot=slot):
                clear_up(slot)
                for at in range(2):
                    clear_corner(slot, at)

    if n_band == 1:
        clear(lateral)
        clear(own_lateral)
        if n_strip > 1:
            clear(corner)
            clear(own_corner)
    elif n_band == 2:
        clear_side(band)
        if n_strip == 2:
            clear_corner(1 - strip, band)
        elif n_strip > 2:
            for slot, held in ((0, strip > 0), (1, strip < n_strip - 1)):
                pl.when(held)(lambda slot=slot: clear_corner(slot, band))
    else:
        for slot, edge in ((0, band == 0), (1, band == n_band - 1)):

            @pl.when(edge)
            def _(slot=slot):
                clear_side(slot)
                for at in range(2):
                    clear_corner(at, slot)

    slab[:, :, height + 2 * EDGE_ROWS :, :] = jnp.zeros(
        (slab.shape[0], slab.shape[1], 8, LANES), f32
    )

    n_pairs = (ks + 1) // 2
    n_tiles = n_pairs * SLOT // LANES
    later = jnp.bitwise_and(lane, 7) >= sub

    def mix_of(some, indices):
        parts = []
        for j in range(n_sel):
            column = jnp.broadcast_to(some[:, j : j + 1], (8, LANES))
            parts.append(jnp.where(lane == indices(j), column, 0.0))
        while len(parts) > 1:
            parts = [
                parts[i] + parts[i + 1] if i + 1 < len(parts) else parts[i]
                for i in range(0, len(parts), 2)
            ]
        mix = jnp.where(sub < n_poly, parts[0], 0.0)
        mix = mix + pltpu.roll(mix, half, 1)
        high = mix.astype(bf16).astype(f32)
        return high, mix - high

    def unpacked(line):
        wide = jnp.broadcast_to(line, (8, LANES))
        out = wide
        for p in range(1, n_poly):
            out = jnp.where(sub == p, pltpu.roll(wide, LANES - n_sel * p, 1), out)
        return out

    def mixed(pairs):
        rows = jnp.concatenate([p[0] for p in pairs] + [p[1] for p in pairs], axis=0)
        out = lax.dot_general(
            rows.astype(bf16), table[...], (((1,), (1,)), ((), ())), preferred_element_type=f32
        )
        size = 8 * len(pairs)
        return (out[:size] + out[size:]).astype(bf16).astype(f32)

    def spread(row, into):
        for p in range(0, n_poly, 2):
            for t in range(n_tiles):
                halves = []
                for h in range(2):
                    at = row * 8 + p + h
                    wide = jnp.broadcast_to(
                        kernels[at : at + 1, t * LANES : (t + 1) * LANES], (8, LANES)
                    )
                    close = pltpu.roll(wide, 0, 1, stride=1, stride_axis=0)
                    far = pltpu.roll(wide, 8, 1, stride=1, stride_axis=0)
                    halves.append(jnp.where(later, close, far))
                toeplitz[into, p * 8 : (p + 2) * 8, t * LANES : (t + 1) * LANES] = (
                    jnp.concatenate(halves, axis=0).astype(bf16)
                )

    pairs = [
        mix_of(
            coefs[exposure],
            lambda j, exposure=exposure: basis_index[exposure, j],
        )
        for exposure in range(exp_dev)
    ]

    loads[7].wait()
    blank = jnp.zeros((8, LANES), f32)

    def taps(b, g):
        if b >= ks or g * 8 >= ks:
            return blank
        here = min(8, ks - g * 8)
        tile = basis[g * 8 : g * 8 + here, b, :]
        if here < 8:
            tile = jnp.concatenate([tile, jnp.zeros((8 - here, n_basis), f32)], axis=0)
        tile = jnp.concatenate([tile, jnp.zeros((8, LANES - n_basis), f32)], axis=1)
        high = tile.astype(bf16).astype(f32)
        return jnp.where(lane < half, high, pltpu.roll(tile - high, half, 1))

    table[...] = jnp.concatenate(
        [
            taps(2 * q + h, g)
            for q in range(n_pairs)
            for g in range(GROUPS)
            for h in range(2)
        ],
        axis=0,
    ).astype(bf16)
    kernels[0 : 8 * exp_dev] = mixed(pairs)
    for exposure in range(exp_dev):
        spread(exposure, exposure)

    row = lax.broadcasted_iota(jnp.int32, (height, 1), 0) + strip * height
    col = lax.broadcasted_iota(jnp.int32, (1, width), 1) + band * width
    r = (2.0 * row.astype(f32) + 1.0) / (height * n_strip) - 1.0
    c = (2.0 * col.astype(f32) + 1.0) / (width * n_band) - 1.0
    r = jnp.broadcast_to(r, (height, width))
    c = jnp.broadcast_to(c, (height, width))

    span = height + 8 * GROUPS - 8
    at_lane = lax.broadcasted_iota(jnp.int32, (span, LANES), 1)

    beside = [(0, LANES - SIDE), (1, 0)]
    if n_band == 2:
        beside = [(1 - band, band * (LANES - SIDE))]

    def lay(board, middle, up, side, edge, at):
        for rows, body, rims in (
            (0, up(0), [(edge(0, k).astype(f32), base) for k, base in beside]),
            (EDGE_ROWS, middle, [(side(k).astype(f32), base) for k, base in beside]),
            (EDGE_ROWS + height, up(1), [(edge(1, k).astype(f32), base) for k, base in beside]),
        ):
            wide = body.astype(f32)
            size = wide.shape[0]
            for t in range(n_lane):
                slab[board, t, rows : rows + size, :] = wide[:, t * LANES : (t + 1) * LANES]
            for i in range(size // 8):
                part = jnp.zeros((8, LANES), f32)
                for held, base in rims:
                    turned = held if i == 0 else pltpu.roll(held, LANES - SIDE * i, 1)
                    part = jnp.where(within(base), turned, part)
                slab[board, n_lane, rows + 8 * i : rows + 8 * i + 8, :] = part

    def lay_own(board, tile):
        lay(
            board,
            template[tile],
            lambda v: own_vertical[v, tile],
            lambda s: own_lateral[s, tile],
            lambda v, s: own_corner[v, s, tile],
            tile,
        )

    def lay_other(board, epoch):
        lay(
            board,
            centre[epoch],
            lambda v: vertical[v, epoch],
            lambda s: lateral[s, epoch],
            lambda v, s: corner[v, s, epoch],
            epoch,
        )

    def models(board, factor, down, along):
        views = []
        for h in range(2):
            turned = [
                pltpu.roll(slab[board, t, pl.ds(down, span), :], along - h, 1)
                for t in range(n_lane + 1)
            ]
            views.append(
                jnp.concatenate(
                    [
                        jnp.where(at_lane < along - h, turned[t - 1], turned[t])
                        for t in range(n_lane + 1)
                    ],
                    axis=1,
                )
            )
        tiles = [
            jnp.concatenate(
                [views[0][g * 8 : g * 8 + 8], views[1][g * 8 : g * 8 + 8]], axis=0
            ).astype(bf16)
            for g in range(span // 8)
        ]
        moved = [[tile[:, 2 * q : 2 * q + width] for tile in tiles] for q in range(n_pairs)]
        for block in range(height // 8):
            stacked = jnp.concatenate(
                [moved[q][block + g] for q in range(n_pairs) for g in range(GROUPS)], axis=0
            )
            conv = jnp.dot(factor, stacked, preferred_element_type=f32)
            q = [conv[p * 8 : (p + 1) * 8] for p in range(n_poly)]
            at = slice(block * 8, block * 8 + 8)
            rr, cc = r[at], c[at]
            yield at, q[0] + rr * (q[1] + rr * q[3] + cc * q[4]) + cc * (q[2] + cc * q[5])

    def tile_of(epoch):
        return intersection[epoch * exp_dev + me] - me * tile_dev

    def down_of(shift):
        return EDGE_ROWS - HALF + shift

    def along_of(shift):
        return HALF - shift

    behind = partners - 1 - ahead_of_me

    @pl.when(behind > 0)
    def _():
        pl.semaphore_wait(token.at[me], behind)

    for u, s, kind in images[1:]:
        guarded(
            both(both(u[3], s[3]), jnp.logical_not(lower(u, s))),
            lambda u=u, s=s, kind=kind: own_piece(u, s, kind, False).start(),
        )
    for epoch in range(1, n_epoch - 1):

        @pl.when(epoch < me)
        def _(epoch=epoch):
            send_image(epoch)
            coded(epoch, me).start()

    def offer(step):
        @pl.when(me + step < n_epoch)
        def _(epoch=me + step):
            far = swap and step == n_epoch - 1
            pl.semaphore_wait(token.at[epoch], partners if far else 1)
            send_small(epoch)
            coefficient_tile(epoch, me).start()
            if far:
                send_image(epoch)
            coded(epoch, me).start()

    early = n_epoch - 2 if n_epoch == 4 else n_epoch - 1
    for step in range(1, early + 1):
        offer(step)

    for u, s, kind in images_in[1:]:
        guarded(both(u[3], s[3]), lambda u=u, s=s, kind=kind: own_piece(u, s, kind, True).wait_recv())

    def own_board(tile):
        return jnp.clip(tile, 0, tile_dev - 1)

    def first():
        tile = tile_of(me)
        for at, model in models(own_board(tile), toeplitz[me], down_of(offsets[0, me]), along_of(offsets[1, me])):
            left = science[me, at] - model
            residual[me, at] = left
            share = weight[me, at]
            for t in range(tile_dev):
                here = (tile == t).astype(f32)
                numer[t, at] = share * left * here
                denom[t, at] = share * here

    def lay_tiles():
        for t in range(tile_dev):
            lay_own(t, t)

    def partner(step):
        return jnp.where(me + step < n_epoch, me + step, n_epoch - 1 - step)

    def theirs(step):
        epoch = partner(step)
        last = exp_dev
        kernels[8 * last : 8 * last + 8] = mixed(
            [mix_of(unpacked(coefs_in[epoch]), lambda j: basis_index_in[epoch, me, j])]
        )
        spread(last, last)
        for at, model in models(
            own_board(tile_of(epoch)),
            toeplitz[last],
            down_of(offsets_in[epoch, 0, me]),
            along_of(offsets_in[epoch, 1, me]),
        ):
            model_out[epoch, at] = model

    def wait_small(step):
        epoch = partner(step)
        for one in small(me, epoch) + [coefficient_tile(me, epoch)]:
            one.wait_recv()

    def answer(step):
        pl.when(partner(step) > me)(lambda: returned(partner(step), me).start())

    def host(step):
        wait_small(step)
        theirs(step)
        answer(step)

    def ours(step):
        epoch = partner(step)
        board = tile_dev + step - 1 if isinstance(step, int) else tile_dev
        lay_other(board, epoch)
        for at, model in models(
            board, toeplitz[epoch], down_of(offsets[0, epoch]), along_of(offsets[1, epoch])
        ):
            residual[epoch, at] = science[epoch, at] - model

    def settle(step):
        epoch = partner(step)
        returned(me, epoch).wait_recv()
        residual[epoch] = science[epoch] - model_in[epoch]

    def mine(step):
        @pl.when(partner(step) > me)
        def _():
            wait_image(partner(step))
            ours(step)

    def finish(step):
        gather(step)
        back = partner(step) < me
        if swap:
            back = jnp.logical_and(back, me - partner(step) < n_epoch - 1)
        pl.when(back)(lambda: settle(step))

    def gather(step):
        epoch = partner(step)
        tile = tile_of(epoch)
        coded(me, epoch).wait_recv()
        seen, share = decode(code_in[epoch])
        value = share * (seen - model_out[epoch])
        for t in range(tile_dev):
            here = (tile == t).astype(f32)
            numer[t] = numer[t] + value * here
            denom[t] = denom[t] + share * here

    if n_epoch == 4:

        @pl.when(me == 0)
        def _():
            lay_tiles()
            first()
            host(1)
            offer(3)
            wait_small(2)
            wait_image(1)
            theirs(2)
            ours(1)
            answer(2)
            wait_small(3)
            theirs(3)
            wait_image(3)
            ours(3)
            wait_image(2)
            ours(2)

        @pl.when(me > 0)
        def _():
            lay_tiles()
            first()
            for step in range(1, n_epoch):
                host(step)
            for step in range(2, 0, -1):
                mine(step)

            @pl.when(me == n_epoch - 1)
            def _():
                wait_image(0)
                ours(3)


        for step in (1, 3, 2):
            finish(step)
    else:
        lay_tiles()
        first()

        def walk(stage):
            lax.fori_loop(1, n_epoch, lambda step, carry: (stage(step), carry)[1], 0)

        walk(host)
        walk(mine)
        walk(finish)

    for t in range(tile_dev):
        coadd[t] = numer[t] / (denom[t] + 1.0)

    for u, s, kind in images[1:]:
        guarded(both(u[3], s[3]), lambda u=u, s=s, kind=kind: own_piece(u, s, kind, False).wait_send())
    if n_epoch > 1:
        rest = pl.ds(0, n_epoch - 1)

        def drain(source, kind, u, s):
            copy(source, source, send_sem.at[kind], recv_sem.at[0, 0], device(me, u, s)).wait_send()

        for number in range(n_epoch):

            @pl.when(jnp.logical_and(me == number, number > 0 or swap))
            def _(number=number):
                lead = pl.ds(0, max(number, 1))
                for u, s, kind in images:
                    if u is none and s is none:
                        source = chosen.at[lead]
                    elif s is none:
                        source = chosen_edge.at[u[1], lead]
                    elif u is none:
                        source = chosen_side.at[s[1], lead]
                    else:
                        source = chosen_corner.at[u[1], s[1], lead]
                    guarded(
                        both(u[3], s[3]),
                        lambda u=u, s=s, kind=kind, source=source: drain(source, kind, u, s),
                    )

            models_sent = n_epoch - 1 - number
            if swap and number == 0:
                models_sent -= 1
            if models_sent > 0:

                @pl.when(me == number)
                def _(models_sent=models_sent):
                    drain(model_out.at[pl.ds(0, models_sent)], MODEL, none, none)

        for held, kind in (
            (offsets_in, OFFS),
            (basis_index_in, INDX),
            (coef_row, COEF),
            (code, CODE),
        ):
            drain(held.at[rest], kind, none, none)


def leave(residual, coadd, residual_out, coadd_out, sem):
    parts = [
        (held.at[i], out.at[i])
        for held, out in ((residual, residual_out), (coadd, coadd_out))
        for i in range(held.shape[0])
    ]
    copies = [pltpu.make_async_copy(held, out, sem.at[i]) for i, (held, out) in enumerate(parts)]
    for one in copies:
        one.start()
    for one in copies:
        one.wait()


def local(sizes, template, science, variance, bad_mask, intersection, offsets, basis_index, coefficients, basis):
    n_epoch, n_strip, n_band = sizes
    tile_dev, height, width = template.shape
    exp_dev = science.shape[0]
    assert exp_dev == n_epoch
    n_poly = coefficients.shape[2]
    n_sel = basis_index.shape[1]
    ks = basis.shape[1]
    n_pairs = (ks + 1) // 2
    far = pl.BlockSpec(memory_space=pltpu.HBM)
    near = pl.BlockSpec(memory_space=pltpu.VMEM)
    free = pl.BlockSpec(memory_space=pl.ANY)
    bf16, f32 = jnp.bfloat16, jnp.float32
    dma = pltpu.SemaphoreType.DMA
    offsets = offsets.T
    coefficients = coefficients.transpose(2, 0, 1)
    basis = basis.transpose(1, 2, 0)
    n_up, n_side = min(n_strip - 1, 2), min(n_band - 1, 2)
    n_image = (1 + n_up) * (1 + n_side)
    edges, sides = max(n_up, 1), max(n_side, 1)
    rim = EDGE_ROWS
    residual, coadd = pl.pallas_call(
        functools.partial(kernel, sizes),
        out_shape=(
            pltpu.VMEM(science.shape, f32),
            pltpu.VMEM(template.shape, f32),
        ),
        in_specs=[far] * 9,
        out_specs=(near, near),
        scratch_shapes=[
            pltpu.SMEM(intersection.shape, jnp.int32),
            pltpu.SMEM(offsets.shape, jnp.int32),
            pltpu.SMEM((n_epoch,) + offsets.shape, jnp.int32),
            pltpu.SMEM(basis_index.shape, jnp.int32),
            pltpu.SMEM((n_epoch,) + basis_index.shape, jnp.int32),
            pltpu.VMEM(coefficients.shape, f32),
            pltpu.VMEM((n_epoch, 1, LANES), f32),
            pltpu.VMEM(template.shape, bf16),
            pltpu.VMEM(science.shape, f32),
            pltpu.VMEM(science.shape, f32),
            pltpu.VMEM(science.shape, jnp.int32),
            pltpu.VMEM(basis.shape, f32),
            pltpu.VMEM((n_epoch, height, width), bf16),
            pltpu.VMEM((edges, n_epoch, rim, width), bf16),
            pltpu.VMEM((sides, n_epoch, 8, LANES), bf16),
            pltpu.VMEM((edges, sides, n_epoch, 8, LANES), bf16),
            pltpu.VMEM((edges, tile_dev, rim, width), bf16),
            pltpu.VMEM((sides, tile_dev, 8, LANES), bf16),
            pltpu.VMEM((edges, sides, tile_dev, 8, LANES), bf16),
            pltpu.VMEM((n_epoch, height, width), bf16),
            pltpu.VMEM((2, n_epoch, rim, width), bf16),
            pltpu.VMEM((2, n_epoch, 8, LANES), bf16),
            pltpu.VMEM((2, 2, n_epoch, 8, LANES), bf16),
            pltpu.VMEM((2, tile_dev, rim, width), bf16),
            pltpu.VMEM((2, tile_dev, 8, LANES), bf16),
            pltpu.VMEM((2, 2, tile_dev, 8, LANES), bf16),
            pltpu.VMEM((exp_dev, 8, LANES), f32),
            pltpu.VMEM((exp_dev, 1, LANES), f32),
            pltpu.VMEM((n_pairs * SLOT, LANES), bf16),
            pltpu.VMEM((8 * exp_dev + 8, n_pairs * SLOT), f32),
            pltpu.VMEM((tile_dev + max(n_epoch - 1, 1), width // LANES + 1, 2 * rim + height + 8, LANES), f32),
            pltpu.VMEM((exp_dev + 1, n_poly * 8, n_pairs * SLOT), bf16),
            pltpu.VMEM((exp_dev, height, width), f32),
            pltpu.VMEM((n_epoch, height, width), jnp.int32),
            pltpu.VMEM((n_epoch, height, width), jnp.int32),
            pltpu.VMEM((n_epoch, height, width), f32),
            pltpu.VMEM((n_epoch, height, width), f32),
            pltpu.VMEM(template.shape, f32),
            pltpu.VMEM(template.shape, f32),
            dma((9,)),
            dma((n_image + 5,)),
            dma((max(n_epoch - 1, 1), n_image + 4)),
            dma((n_image,)),
            dma((n_image,)),
            pltpu.SemaphoreType.REGULAR((n_epoch,)),
        ],
        compiler_params=pltpu.CompilerParams(
            collective_id=0, has_side_effects=True
        ),
    )(
        intersection, offsets, basis_index, coefficients,
        template, science, variance, bad_mask, basis,
    )
    return pl.pallas_call(
        leave,
        out_shape=(
            jax.ShapeDtypeStruct(science.shape, f32),
            jax.ShapeDtypeStruct(template.shape, f32),
        ),
        in_specs=[near] * 2,
        out_specs=(free, free),
        scratch_shapes=[dma((exp_dev + tile_dev,))],
    )(*(pltpu.with_memory_space_constraint(x, pltpu.VMEM) for x in (residual, coadd)))


def solution(mesh):
    sizes = (mesh.shape["epoch"], mesh.shape["strip"], mesh.shape["band"])
    image = P(("groups", "epoch"), "strip", "band")
    split = ("groups", "epoch")
    in_specs = (
        image, image, image, image, P("groups"),
        P(split, None), P(split, None), P(split, None, None), P(),
    )
    return jax.shard_map(
        functools.partial(local, sizes),
        mesh=mesh,
        in_specs=in_specs,
        out_specs=(image, image),
        check_vma=False,
    )
```

```python
import functools

import jax
import jax.numpy as jnp
from jax import lax
from jax.experimental import pallas as pl
from jax.experimental.pallas import tpu as pltpu
from jax.sharding import PartitionSpec as P

HALF = 9
SHIFT = 4
EDGE_ROWS = 16
LANES = 128
SLOT = 64
GROUPS = 4
SIDE = 16
SCIENCE_TOP = 6.0
WEIGHT_TOP = 0.5
LEVELS = 65535.0

MESH = pl.DeviceIdType.MESH


def links_of(size, place):
    if size == 1:
        return []
    if size == 2:
        return [(1 - 2 * place, 0, place, None, None)]
    return [
        (-1, 0, 1, place > 0, place < size - 1),
        (1, 1, 0, place < size - 1, place > 0),
    ]


def both(first, second):
    if first is None:
        return second
    if second is None:
        return first
    return jnp.logical_and(first, second)


def guarded(side, body):
    if side is None:
        body()
    else:
        pl.when(side)(body)


def encode(science, weight):
    high = (science + SCIENCE_TOP) * (LEVELS / (2.0 * SCIENCE_TOP)) + 0.5
    low = weight * (LEVELS / WEIGHT_TOP) + 0.5
    high = jnp.clip(high, 0.0, LEVELS).astype(jnp.int32)
    low = jnp.clip(low, 0.0, LEVELS).astype(jnp.int32)
    return jnp.bitwise_or(jnp.left_shift(high, 16), low)


def decode(code):
    high = lax.shift_right_logical(code, jnp.full(code.shape, 16, jnp.int32))
    low = jnp.bitwise_and(code, 65535)
    science = high.astype(jnp.float32) * (2.0 * SCIENCE_TOP / LEVELS) - SCIENCE_TOP
    return science, low.astype(jnp.float32) * (WEIGHT_TOP / LEVELS)


def kernel(
    sizes,
    intersection_hbm,
    offsets_hbm,
    basis_index_hbm,
    coefficients_hbm,
    template_hbm,
    science_hbm,
    variance_hbm,
    bad_mask_hbm,
    basis_hbm,
    residual,
    coadd,
    intersection,
    offsets,
    offsets_in,
    basis_index,
    basis_index_in,
    coefficients,
    coefs_in,
    template,
    science,
    variance,
    bad_mask,
    basis,
    chosen,
    chosen_edge,
    chosen_side,
    chosen_corner,
    own_edge,
    own_side,
    own_diagonal,
    centre,
    vertical,
    lateral,
    corner,
    own_vertical,
    own_lateral,
    own_corner,
    coefs,
    coef_row,
    table,
    kernels,
    slab,
    toeplitz,
    weight,
    code,
    code_in,
    model_out,
    model_in,
    numer,
    denom,
    local_sem,
    send_sem,
    recv_sem,
    own_send,
    own_recv,
    token,
):
    n_epoch, n_strip, n_band = sizes
    tile_dev, height, width = template.shape
    exp_dev = science.shape[0]
    n_poly, _, n_sel = coefficients.shape
    ks, _, n_basis = basis.shape
    n_lane = width // LANES
    half = LANES // 2
    f32, bf16 = jnp.float32, jnp.bfloat16
    group = lax.axis_index("groups")
    me = lax.axis_index("epoch")
    strip = lax.axis_index("strip")
    band = lax.axis_index("band")

    ups = links_of(n_strip, strip)
    sides = links_of(n_band, band)
    none = (0, None, None, None, None)
    near = [(u, s) for u in [none] + ups for s in [none] + sides]

    def device(epoch, u, s):
        return (group, epoch, strip + u[0], band + s[0])

    loads = [
        pltpu.make_async_copy(held, here, local_sem.at[i])
        for i, (held, here) in enumerate(
            (
                (intersection_hbm, intersection),
                (template_hbm, template),
                (variance_hbm, variance),
                (bad_mask_hbm, bad_mask),
                (science_hbm, science),
                (coefficients_hbm, coefficients),
                (basis_index_hbm, basis_index),
                (basis_hbm, basis),
                (offsets_hbm, offsets),
            )
        )
    ]
    for i in (5, 6, 8, 0, 1, 2, 3, 4, 7):
        loads[i].start()

    def count(size, place):
        if size < 3:
            return size
        return 1 + jnp.minimum(place, 1) + jnp.minimum(size - 1 - place, 1)

    def before(size, place):
        return place if size < 3 else jnp.minimum(place, 1)

    across = count(n_band, band)
    partners = count(n_strip, strip) * across
    ahead_of_me = before(n_strip, strip) * across + before(n_band, band)

    def lower(u, s):
        if u is not none:
            return strip + u[0] < strip
        return band + s[0] < band

    swap = n_epoch == 4

    barrier = pltpu.get_barrier_semaphore()

    def signal(sem, epoch, u, s):
        pl.semaphore_signal(sem, inc=1, device_id=device(epoch, u, s), device_id_type=MESH)

    def to_epoch(sem, epoch):
        for u, s in near:
            guarded(both(u[3], s[3]), lambda u=u, s=s: signal(sem, epoch, u, s))

    for u, s in near[1:]:
        guarded(
            both(both(u[3], s[3]), jnp.logical_not(lower(u, s))),
            lambda u=u, s=s: signal(barrier, me, u, s),
        )
    for step in range(1, n_epoch):
        pl.when(me + step < n_epoch)(lambda step=step: to_epoch(barrier, me + step))
    met = partners * me + ahead_of_me

    @pl.when(met > 0)
    def _():
        pl.semaphore_wait(barrier, met)

    for u, s in near[1:]:
        guarded(
            both(both(u[3], s[3]), lower(u, s)),
            lambda u=u, s=s: signal(token.at[me], me, u, s),
        )
    for epoch in range(n_epoch - 1):
        if swap and epoch == 0:
            pl.when(me == n_epoch - 1)(lambda: to_epoch(token.at[me], 0))
            pl.when(jnp.logical_and(me > 0, me < n_epoch - 1))(
                lambda: signal(token.at[me], 0, none, none)
            )
        else:
            pl.when(epoch < me)(lambda epoch=epoch: signal(token.at[me], epoch, none, none))

    def slot_of(sender, receiver):
        return sender - (sender > receiver).astype(jnp.int32)

    lane = lax.broadcasted_iota(jnp.int32, (8, LANES), 1)
    sub = lax.broadcasted_iota(jnp.int32, (8, LANES), 0)

    def within(base):
        return jnp.bitwise_and(lane - base, LANES - 1) < SIDE

    def side_tile(wide, which):
        first, last = wide[:, :LANES], wide[:, width - LANES :]
        if n_band == 2:
            return jnp.where(band == 0, last, first), (1 - band) * (LANES - SIDE)
        return (first, 0) if which == 0 else (last, LANES - SIDE)

    def packed(wide, which):
        tile, base = side_tile(wide, which)
        out = jnp.zeros((8, LANES), f32)
        for i in range(wide.shape[0] // 8):
            part = tile[8 * i : 8 * i + 8]
            if i > 0:
                part = pltpu.roll(part, SIDE * i, 1)
            out = jnp.where(within(base + SIDE * i), part, out)
        return out.astype(bf16)

    def copy(source, dest, sent, received, to):
        return pltpu.make_async_remote_copy(
            src_ref=source,
            dst_ref=dest,
            send_sem=sent,
            recv_sem=received,
            device_id=to,
            device_id_type=MESH,
        )

    n_up, n_side = len(ups), len(sides)
    images = []
    for u, s in near:
        i = 0 if u is none else 1 + ups.index(u)
        j = 0 if s is none else 1 + sides.index(s)
        images.append((u, s, i * (1 + n_side) + j))
    n_image = (1 + n_up) * (1 + n_side)
    CODE, COEF, OFFS, INDX, MODEL = (n_image + i for i in range(5))

    def image(epoch, u, s, kind, sender, at=None):
        source_at = epoch if at is None else at
        if u is none and s is none:
            source, dest = chosen.at[source_at], centre.at[sender]
        elif s is none:
            source, dest = chosen_edge.at[u[1], source_at], vertical.at[u[2], sender]
        elif u is none:
            source, dest = chosen_side.at[s[1], source_at], lateral.at[s[2], sender]
        else:
            source = chosen_corner.at[u[1], s[1], source_at]
            dest = corner.at[u[2], s[2], sender]
        return copy(
            source, dest, send_sem.at[kind], recv_sem.at[slot_of(sender, epoch), kind], device(epoch, u, s)
        )

    def arriving(epoch, u, s, kind):
        if u is none and s is none:
            dest = centre.at[epoch]
        elif s is none:
            dest = vertical.at[u[2], epoch]
        elif u is none:
            dest = lateral.at[s[2], epoch]
        else:
            dest = corner.at[u[2], s[2], epoch]
        return copy(dest, dest, send_sem.at[kind], recv_sem.at[slot_of(epoch, me), kind], device(epoch, u, s))

    def landing(links, place, size):
        if size == 2:
            return [(k[0], k[1], 1 - place, None, None) for k in links]
        return [(k[0], k[1], k[2], k[4], k[3]) for k in links]

    ups_in = landing(ups, strip, n_strip)
    sides_in = landing(sides, band, n_band)
    images_in = []
    for u, s, kind in images:
        a = none if u is none else ups_in[ups.index(u)]
        b = none if s is none else sides_in[sides.index(s)]
        images_in.append((a, b, kind))

    def send_image(epoch):
        for u, s, kind in reversed(images):
            guarded(
                both(u[3], s[3]), lambda u=u, s=s, kind=kind: image(epoch, u, s, kind, me).start()
            )

    def wait_image(epoch):
        for u, s, kind in images_in:
            guarded(
                both(u[3], s[3]), lambda u=u, s=s, kind=kind: arriving(epoch, u, s, kind).wait_recv()
            )

    def small(epoch, sender):
        return [
            copy(held, into.at[sender], send_sem.at[kind], recv_sem.at[slot_of(sender, epoch), kind], device(epoch, none, none))
            for held, into, kind in (
                (offsets, offsets_in, OFFS),
                (basis_index, basis_index_in, INDX),
            )
        ]

    def coefficient_tile(epoch, sender):
        return copy(
            coef_row.at[epoch], coefs_in.at[sender], send_sem.at[COEF], recv_sem.at[slot_of(sender, epoch), COEF],
            device(epoch, none, none),
        )

    def coded(epoch, sender):
        return copy(
            code.at[epoch], code_in.at[sender], send_sem.at[CODE], recv_sem.at[slot_of(sender, epoch), CODE],
            device(epoch, none, none),
        )

    def returned(epoch, sender):
        return copy(
            model_out.at[epoch], model_in.at[sender], send_sem.at[MODEL], recv_sem.at[slot_of(sender, epoch), 0],
            device(epoch, none, none),
        )

    def own_piece(u, s, kind, incoming):
        if s is none:
            source, dest = own_edge.at[0 if incoming else u[1]], own_vertical.at[u[2]]
        elif u is none:
            source, dest = own_side.at[0 if incoming else s[1]], own_lateral.at[s[2]]
        else:
            source = own_diagonal.at[0 if incoming else u[1], 0 if incoming else s[1]]
            dest = own_corner.at[u[2], s[2]]
        if incoming:
            source = dest
        return copy(source, dest, own_send.at[kind], own_recv.at[kind], device(me, u, s))

    def send_small(epoch):
        for one in small(epoch, me):
            one.start()

    loads[6].wait()
    loads[8].wait()
    for epoch in range(n_epoch - 1):
        pl.when(epoch < me)(lambda epoch=epoch: send_small(epoch))

    loads[5].wait()
    for exposure in range(exp_dev):
        coefs[exposure] = jnp.zeros((8, LANES), f32)
        for p in range(n_poly):
            coefs[exposure, p : p + 1, 0:n_sel] = coefficients[p, exposure : exposure + 1, :]
        coef_row[exposure] = jnp.sum(
            pltpu.roll(coefs[exposure], 0, 1, stride=n_sel, stride_axis=0), axis=0, keepdims=True
        )

    for epoch in range(n_epoch - 1):
        pl.when(epoch < me)(lambda epoch=epoch: coefficient_tile(epoch, me).start())
    loads[0].wait()
    loads[1].wait()

    def rim(wide, which):
        low, high = wide[:EDGE_ROWS], wide[height - EDGE_ROWS :]
        if n_strip == 2:
            return jnp.where(strip == 0, high, low)
        return low if which == 0 else high

    for epoch in range(n_epoch):
        tile = intersection[epoch * exp_dev + me] - me * tile_dev
        picked = template[jnp.clip(tile, 0, tile_dev - 1)]
        chosen[epoch] = picked
        wide = picked.astype(f32)
        for side in range(n_side):
            chosen_side[side, epoch] = packed(wide, side)
        for which in range(n_up):
            edge = rim(wide, which)
            chosen_edge[which, epoch] = edge.astype(bf16)
            for side in range(n_side):
                chosen_corner[which, side, epoch] = packed(edge, side)
    pl.when(me > 0)(lambda: send_image(0))
    loads[2].wait()
    loads[3].wait()
    loads[4].wait()
    for epoch in range(n_epoch):
        share = bad_mask[epoch].astype(f32) / variance[epoch]
        weight[epoch] = share
        code[epoch] = encode(science[epoch], share)
    pl.when(me > 0)(lambda: coded(0, me).start())

    for t in range(tile_dev):
        wide = template[t].astype(f32)
        for side in range(n_side):
            own_side[side, t] = packed(wide, side)
        for which in range(n_up):
            edge = rim(wide, which)
            own_edge[which, t] = edge.astype(bf16)
            for side in range(n_side):
                own_diagonal[which, side, t] = packed(edge, side)
    for u, s, kind in images[1:]:
        guarded(
            both(both(u[3], s[3]), lower(u, s)),
            lambda u=u, s=s, kind=kind: own_piece(u, s, kind, False).start(),
        )

    def clear(ref):
        ref[...] = jnp.zeros(ref.shape, ref.dtype)

    def clear_up(slot):
        clear(vertical.at[slot])
        clear(own_vertical.at[slot])

    def clear_side(slot):
        clear(lateral.at[slot])
        clear(own_lateral.at[slot])

    def clear_corner(slot, at):
        clear(corner.at[slot, at])
        clear(own_corner.at[slot, at])

    if n_strip == 1:
        clear(vertical)
        clear(own_vertical)
        clear(corner)
        clear(own_corner)
    elif n_strip == 2:
        clear_up(strip)
        for at in range(2):
            clear_corner(strip, at)
    else:
        for slot, edge in ((0, strip == 0), (1, strip == n_strip - 1)):

            @pl.when(edge)
            def _(slot=slot):
                clear_up(slot)
                for at in range(2):
                    clear_corner(slot, at)

    if n_band == 1:
        clear(lateral)
        clear(own_lateral)
        if n_strip > 1:
            clear(corner)
            clear(own_corner)
    elif n_band == 2:
        clear_side(band)
        if n_strip == 2:
            clear_corner(1 - strip, band)
        elif n_strip > 2:
            for slot, held in ((0, strip > 0), (1, strip < n_strip - 1)):
                pl.when(held)(lambda slot=slot: clear_corner(slot, band))
    else:
        for slot, edge in ((0, band == 0), (1, band == n_band - 1)):

            @pl.when(edge)
            def _(slot=slot):
                clear_side(slot)
                for at in range(2):
                    clear_corner(at, slot)

    slab[:, :, height + 2 * EDGE_ROWS :, :] = jnp.zeros(
        (slab.shape[0], slab.shape[1], 8, LANES), f32
    )

    n_pairs = (ks + 1) // 2
    n_tiles = n_pairs * SLOT // LANES
    later = jnp.bitwise_and(lane, 7) >= sub

    def mix_of(some, indices):
        parts = []
        for j in range(n_sel):
            column = jnp.broadcast_to(some[:, j : j + 1], (8, LANES))
            parts.append(jnp.where(lane == indices(j), column, 0.0))
        while len(parts) > 1:
            parts = [
                parts[i] + parts[i + 1] if i + 1 < len(parts) else parts[i]
                for i in range(0, len(parts), 2)
            ]
        mix = jnp.where(sub < n_poly, parts[0], 0.0)
        mix = mix + pltpu.roll(mix, half, 1)
        high = mix.astype(bf16).astype(f32)
        return high, mix - high

    def unpacked(line):
        wide = jnp.broadcast_to(line, (8, LANES))
        out = wide
        for p in range(1, n_poly):
            out = jnp.where(sub == p, pltpu.roll(wide, LANES - n_sel * p, 1), out)
        return out

    def mixed(pairs):
        rows = jnp.concatenate([p[0] for p in pairs] + [p[1] for p in pairs], axis=0)
        out = lax.dot_general(
            rows.astype(bf16), table[...], (((1,), (1,)), ((), ())), preferred_element_type=f32
        )
        size = 8 * len(pairs)
        return (out[:size] + out[size:]).astype(bf16).astype(f32)

    def spread(row, into):
        for p in range(0, n_poly, 2):
            for t in range(n_tiles):
                halves = []
                for h in range(2):
                    at = row * 8 + p + h
                    wide = jnp.broadcast_to(
                        kernels[at : at + 1, t * LANES : (t + 1) * LANES], (8, LANES)
                    )
                    close = pltpu.roll(wide, 0, 1, stride=1, stride_axis=0)
                    far = pltpu.roll(wide, 8, 1, stride=1, stride_axis=0)
                    halves.append(jnp.where(later, close, far))
                toeplitz[into, p * 8 : (p + 2) * 8, t * LANES : (t + 1) * LANES] = (
                    jnp.concatenate(halves, axis=0).astype(bf16)
                )

    pairs = [
        mix_of(
            coefs[exposure],
            lambda j, exposure=exposure: basis_index[exposure, j],
        )
        for exposure in range(exp_dev)
    ]

    loads[7].wait()
    blank = jnp.zeros((8, LANES), f32)

    def taps(b, g):
        if b >= ks or g * 8 >= ks:
            return blank
        here = min(8, ks - g * 8)
        tile = basis[g * 8 : g * 8 + here, b, :]
        if here < 8:
            tile = jnp.concatenate([tile, jnp.zeros((8 - here, n_basis), f32)], axis=0)
        tile = jnp.concatenate([tile, jnp.zeros((8, LANES - n_basis), f32)], axis=1)
        high = tile.astype(bf16).astype(f32)
        return jnp.where(lane < half, high, pltpu.roll(tile - high, half, 1))

    table[...] = jnp.concatenate(
        [
            taps(2 * q + h, g)
            for q in range(n_pairs)
            for g in range(GROUPS)
            for h in range(2)
        ],
        axis=0,
    ).astype(bf16)
    kernels[0 : 8 * exp_dev] = mixed(pairs)
    for exposure in range(exp_dev):
        spread(exposure, exposure)

    row = lax.broadcasted_iota(jnp.int32, (height, 1), 0) + strip * height
    col = lax.broadcasted_iota(jnp.int32, (1, width), 1) + band * width
    r = (2.0 * row.astype(f32) + 1.0) / (height * n_strip) - 1.0
    c = (2.0 * col.astype(f32) + 1.0) / (width * n_band) - 1.0
    r = jnp.broadcast_to(r, (height, width))
    c = jnp.broadcast_to(c, (height, width))

    span = height + 8 * GROUPS - 8
    at_lane = lax.broadcasted_iota(jnp.int32, (span, LANES), 1)

    beside = [(0, LANES - SIDE), (1, 0)]
    if n_band == 2:
        beside = [(1 - band, band * (LANES - SIDE))]

    def lay(board, middle, up, side, edge, at):
        for rows, body, rims in (
            (0, up(0), [(edge(0, k).astype(f32), base) for k, base in beside]),
            (EDGE_ROWS, middle, [(side(k).astype(f32), base) for k, base in beside]),
            (EDGE_ROWS + height, up(1), [(edge(1, k).astype(f32), base) for k, base in beside]),
        ):
            wide = body.astype(f32)
            size = wide.shape[0]
            for t in range(n_lane):
                slab[board, t, rows : rows + size, :] = wide[:, t * LANES : (t + 1) * LANES]
            for i in range(size // 8):
                part = jnp.zeros((8, LANES), f32)
                for held, base in rims:
                    turned = held if i == 0 else pltpu.roll(held, LANES - SIDE * i, 1)
                    part = jnp.where(within(base), turned, part)
                slab[board, n_lane, rows + 8 * i : rows + 8 * i + 8, :] = part

    def lay_own(board, tile):
        lay(
            board,
            template[tile],
            lambda v: own_vertical[v, tile],
            lambda s: own_lateral[s, tile],
            lambda v, s: own_corner[v, s, tile],
            tile,
        )

    def lay_other(board, epoch):
        lay(
            board,
            centre[epoch],
            lambda v: vertical[v, epoch],
            lambda s: lateral[s, epoch],
            lambda v, s: corner[v, s, epoch],
            epoch,
        )

    def models(board, factor, down, along):
        views = []
        for h in range(2):
            turned = [
                pltpu.roll(slab[board, t, pl.ds(down, span), :], along - h, 1)
                for t in range(n_lane + 1)
            ]
            views.append(
                jnp.concatenate(
                    [
                        jnp.where(at_lane < along - h, turned[t - 1], turned[t])
                        for t in range(n_lane + 1)
                    ],
                    axis=1,
                )
            )
        tiles = [
            jnp.concatenate(
                [views[0][g * 8 : g * 8 + 8], views[1][g * 8 : g * 8 + 8]], axis=0
            ).astype(bf16)
            for g in range(span // 8)
        ]
        moved = [[tile[:, 2 * q : 2 * q + width] for tile in tiles] for q in range(n_pairs)]
        for block in range(height // 8):
            stacked = jnp.concatenate(
                [moved[q][block + g] for q in range(n_pairs) for g in range(GROUPS)], axis=0
            )
            conv = jnp.dot(factor, stacked, preferred_element_type=f32)
            q = [conv[p * 8 : (p + 1) * 8] for p in range(n_poly)]
            at = slice(block * 8, block * 8 + 8)
            rr, cc = r[at], c[at]
            yield at, q[0] + rr * (q[1] + rr * q[3] + cc * q[4]) + cc * (q[2] + cc * q[5])

    def tile_of(epoch):
        return intersection[epoch * exp_dev + me] - me * tile_dev

    def down_of(shift):
        return EDGE_ROWS - HALF + shift

    def along_of(shift):
        return HALF - shift

    behind = partners - 1 - ahead_of_me

    @pl.when(behind > 0)
    def _():
        pl.semaphore_wait(token.at[me], behind)

    for u, s, kind in images[1:]:
        guarded(
            both(both(u[3], s[3]), jnp.logical_not(lower(u, s))),
            lambda u=u, s=s, kind=kind: own_piece(u, s, kind, False).start(),
        )
    for epoch in range(1, n_epoch - 1):

        @pl.when(epoch < me)
        def _(epoch=epoch):
            send_image(epoch)
            coded(epoch, me).start()

    def offer(step):
        @pl.when(me + step < n_epoch)
        def _(epoch=me + step):
            far = swap and step == n_epoch - 1
            pl.semaphore_wait(token.at[epoch], partners if far else 1)
            send_small(epoch)
            coefficient_tile(epoch, me).start()
            if far:
                send_image(epoch)
            coded(epoch, me).start()

    early = n_epoch - 2 if n_epoch == 4 else n_epoch - 1
    for step in range(1, early + 1):
        offer(step)

    for u, s, kind in images_in[1:]:
        guarded(both(u[3], s[3]), lambda u=u, s=s, kind=kind: own_piece(u, s, kind, True).wait_recv())

    def own_board(tile):
        return jnp.clip(tile, 0, tile_dev - 1)

    def first():
        tile = tile_of(me)
        for at, model in models(own_board(tile), toeplitz[me], down_of(offsets[0, me]), along_of(offsets[1, me])):
            left = science[me, at] - model
            residual[me, at] = left
            share = weight[me, at]
            for t in range(tile_dev):
                here = (tile == t).astype(f32)
                numer[t, at] = share * left * here
                denom[t, at] = share * here

    def lay_tiles():
        for t in range(tile_dev):
            lay_own(t, t)

    def partner(step):
        return jnp.where(me + step < n_epoch, me + step, n_epoch - 1 - step)

    def theirs(step):
        epoch = partner(step)
        last = exp_dev
        kernels[8 * last : 8 * last + 8] = mixed(
            [mix_of(unpacked(coefs_in[epoch]), lambda j: basis_index_in[epoch, me, j])]
        )
        spread(last, last)
        for at, model in models(
            own_board(tile_of(epoch)),
            toeplitz[last],
            down_of(offsets_in[epoch, 0, me]),
            along_of(offsets_in[epoch, 1, me]),
        ):
            model_out[epoch, at] = model

    def wait_small(step):
        epoch = partner(step)
        for one in small(me, epoch) + [coefficient_tile(me, epoch)]:
            one.wait_recv()

    def answer(step):
        pl.when(partner(step) > me)(lambda: returned(partner(step), me).start())

    def host(step):
        wait_small(step)
        theirs(step)
        answer(step)

    def ours(step):
        epoch = partner(step)
        board = tile_dev + step - 1 if isinstance(step, int) else tile_dev
        lay_other(board, epoch)
        for at, model in models(
            board, toeplitz[epoch], down_of(offsets[0, epoch]), along_of(offsets[1, epoch])
        ):
            residual[epoch, at] = science[epoch, at] - model

    def settle(step):
        epoch = partner(step)
        returned(me, epoch).wait_recv()
        residual[epoch] = science[epoch] - model_in[epoch]

    def mine(step):
        @pl.when(partner(step) > me)
        def _():
            wait_image(partner(step))
            ours(step)

    def finish(step):
        gather(step)
        back = partner(step) < me
        if swap:
            back = jnp.logical_and(back, me - partner(step) < n_epoch - 1)
        pl.when(back)(lambda: settle(step))

    def gather(step):
        epoch = partner(step)
        tile = tile_of(epoch)
        coded(me, epoch).wait_recv()
        seen, share = decode(code_in[epoch])
        value = share * (seen - model_out[epoch])
        for t in range(tile_dev):
            here = (tile == t).astype(f32)
            numer[t] = numer[t] + value * here
            denom[t] = denom[t] + share * here

    if n_epoch == 4:

        @pl.when(me == 0)
        def _():
            lay_tiles()
            first()
            host(1)
            offer(3)
            wait_small(2)
            wait_image(1)
            theirs(2)
            ours(1)
            answer(2)
            wait_small(3)
            theirs(3)
            wait_image(3)
            wait_image(2)
            ours(3)
            ours(2)

        @pl.when(me > 0)
        def _():
            lay_tiles()
            first()
            for step in range(1, n_epoch):
                host(step)
            for step in range(2, 0, -1):
                mine(step)

            @pl.when(me == n_epoch - 1)
            def _():
                wait_image(0)
                ours(3)


        for step in (1, 3, 2):
            finish(step)
    else:
        lay_tiles()
        first()

        def walk(stage):
            lax.fori_loop(1, n_epoch, lambda step, carry: (stage(step), carry)[1], 0)

        walk(host)
        walk(mine)
        walk(finish)

    for t in range(tile_dev):
        coadd[t] = numer[t] / (denom[t] + 1.0)

    for u, s, kind in images[1:]:
        guarded(both(u[3], s[3]), lambda u=u, s=s, kind=kind: own_piece(u, s, kind, False).wait_send())
    if n_epoch > 1:
        rest = pl.ds(0, n_epoch - 1)

        def drain(source, kind, u, s):
            copy(source, source, send_sem.at[kind], recv_sem.at[0, 0], device(me, u, s)).wait_send()

        for number in range(n_epoch):

            @pl.when(jnp.logical_and(me == number, number > 0 or swap))
            def _(number=number):
                lead = pl.ds(0, max(number, 1))
                for u, s, kind in images:
                    if u is none and s is none:
                        source = chosen.at[lead]
                    elif s is none:
                        source = chosen_edge.at[u[1], lead]
                    elif u is none:
                        source = chosen_side.at[s[1], lead]
                    else:
                        source = chosen_corner.at[u[1], s[1], lead]
                    guarded(
                        both(u[3], s[3]),
                        lambda u=u, s=s, kind=kind, source=source: drain(source, kind, u, s),
                    )

            models_sent = n_epoch - 1 - number
            if swap and number == 0:
                models_sent -= 1
            if models_sent > 0:

                @pl.when(me == number)
                def _(models_sent=models_sent):
                    drain(model_out.at[pl.ds(0, models_sent)], MODEL, none, none)

        for held, kind in (
            (offsets_in, OFFS),
            (basis_index_in, INDX),
            (coef_row, COEF),
            (code, CODE),
        ):
            drain(held.at[rest], kind, none, none)


def leave(residual, coadd, residual_out, coadd_out, sem):
    parts = [
        (held.at[i], out.at[i])
        for held, out in ((residual, residual_out), (coadd, coadd_out))
        for i in range(held.shape[0])
    ]
    copies = [pltpu.make_async_copy(held, out, sem.at[i]) for i, (held, out) in enumerate(parts)]
    for one in copies:
        one.start()
    for one in copies:
        one.wait()


def local(sizes, template, science, variance, bad_mask, intersection, offsets, basis_index, coefficients, basis):
    n_epoch, n_strip, n_band = sizes
    tile_dev, height, width = template.shape
    exp_dev = science.shape[0]
    assert exp_dev == n_epoch
    n_poly = coefficients.shape[2]
    n_sel = basis_index.shape[1]
    ks = basis.shape[1]
    n_pairs = (ks + 1) // 2
    far = pl.BlockSpec(memory_space=pltpu.HBM)
    near = pl.BlockSpec(memory_space=pltpu.VMEM)
    free = pl.BlockSpec(memory_space=pl.ANY)
    bf16, f32 = jnp.bfloat16, jnp.float32
    dma = pltpu.SemaphoreType.DMA
    offsets = offsets.T
    coefficients = coefficients.transpose(2, 0, 1)
    basis = basis.transpose(1, 2, 0)
    n_up, n_side = min(n_strip - 1, 2), min(n_band - 1, 2)
    n_image = (1 + n_up) * (1 + n_side)
    edges, sides = max(n_up, 1), max(n_side, 1)
    rim = EDGE_ROWS
    residual, coadd = pl.pallas_call(
        functools.partial(kernel, sizes),
        out_shape=(
            pltpu.VMEM(science.shape, f32),
            pltpu.VMEM(template.shape, f32),
        ),
        in_specs=[far] * 9,
        out_specs=(near, near),
        scratch_shapes=[
            pltpu.SMEM(intersection.shape, jnp.int32),
            pltpu.SMEM(offsets.shape, jnp.int32),
            pltpu.SMEM((n_epoch,) + offsets.shape, jnp.int32),
            pltpu.SMEM(basis_index.shape, jnp.int32),
            pltpu.SMEM((n_epoch,) + basis_index.shape, jnp.int32),
            pltpu.VMEM(coefficients.shape, f32),
            pltpu.VMEM((n_epoch, 1, LANES), f32),
            pltpu.VMEM(template.shape, bf16),
            pltpu.VMEM(science.shape, f32),
            pltpu.VMEM(science.shape, f32),
            pltpu.VMEM(science.shape, jnp.int32),
            pltpu.VMEM(basis.shape, f32),
            pltpu.VMEM((n_epoch, height, width), bf16),
            pltpu.VMEM((edges, n_epoch, rim, width), bf16),
            pltpu.VMEM((sides, n_epoch, 8, LANES), bf16),
            pltpu.VMEM((edges, sides, n_epoch, 8, LANES), bf16),
            pltpu.VMEM((edges, tile_dev, rim, width), bf16),
            pltpu.VMEM((sides, tile_dev, 8, LANES), bf16),
            pltpu.VMEM((edges, sides, tile_dev, 8, LANES), bf16),
            pltpu.VMEM((n_epoch, height, width), bf16),
            pltpu.VMEM((2, n_epoch, rim, width), bf16),
            pltpu.VMEM((2, n_epoch, 8, LANES), bf16),
            pltpu.VMEM((2, 2, n_epoch, 8, LANES), bf16),
            pltpu.VMEM((2, tile_dev, rim, width), bf16),
            pltpu.VMEM((2, tile_dev, 8, LANES), bf16),
            pltpu.VMEM((2, 2, tile_dev, 8, LANES), bf16),
            pltpu.VMEM((exp_dev, 8, LANES), f32),
            pltpu.VMEM((exp_dev, 1, LANES), f32),
            pltpu.VMEM((n_pairs * SLOT, LANES), bf16),
            pltpu.VMEM((8 * exp_dev + 8, n_pairs * SLOT), f32),
            pltpu.VMEM((tile_dev + max(n_epoch - 1, 1), width // LANES + 1, 2 * rim + height + 8, LANES), f32),
            pltpu.VMEM((exp_dev + 1, n_poly * 8, n_pairs * SLOT), bf16),
            pltpu.VMEM((exp_dev, height, width), f32),
            pltpu.VMEM((n_epoch, height, width), jnp.int32),
            pltpu.VMEM((n_epoch, height, width), jnp.int32),
            pltpu.VMEM((n_epoch, height, width), f32),
            pltpu.VMEM((n_epoch, height, width), f32),
            pltpu.VMEM(template.shape, f32),
            pltpu.VMEM(template.shape, f32),
            dma((9,)),
            dma((n_image + 5,)),
            dma((max(n_epoch - 1, 1), n_image + 4)),
            dma((n_image,)),
            dma((n_image,)),
            pltpu.SemaphoreType.REGULAR((n_epoch,)),
        ],
        compiler_params=pltpu.CompilerParams(
            collective_id=0, has_side_effects=True
        ),
    )(
        intersection, offsets, basis_index, coefficients,
        template, science, variance, bad_mask, basis,
    )
    return pl.pallas_call(
        leave,
        out_shape=(
            jax.ShapeDtypeStruct(science.shape, f32),
            jax.ShapeDtypeStruct(template.shape, f32),
        ),
        in_specs=[near] * 2,
        out_specs=(free, free),
        scratch_shapes=[dma((exp_dev + tile_dev,))],
    )(*(pltpu.with_memory_space_constraint(x, pltpu.VMEM) for x in (residual, coadd)))


def solution(mesh):
    sizes = (mesh.shape["epoch"], mesh.shape["strip"], mesh.shape["band"])
    image = P(("groups", "epoch"), "strip", "band")
    split = ("groups", "epoch")
    in_specs = (
        image, image, image, image, P("groups"),
        P(split, None), P(split, None), P(split, None, None), P(),
    )
    return jax.shard_map(
        functools.partial(local, sizes),
        mesh=mesh,
        in_specs=in_specs,
        out_specs=(image, image),
        check_vma=False,
    )
```
